128 devices in a mesh: dp: 4 (over y), row: 4 (over z_hi, core), col: 8 (over x, z_lo).
Axes of the slice: x: 4, y: 4, z: 4 (z_hi: 2, z_lo: 2; z = z_hi * 2 + z_lo), core: 2. Of those that a mesh axis runs over, the one named last changes fastest.
Arguments:
- latent: bfloat16 [4, 64, 64, 2240], P('dp', 'row', 'col'), may hold values from -40 to 40
- query_weight: bfloat16 [2240, 1120], replicated, may hold values from -0.125 to 0.125
- key_weight: bfloat16 [2240, 1120], replicated, may hold values from -0.125 to 0.125
- value_weight: bfloat16 [2240, 1120], replicated, may hold values from -0.125 to 0.125
- upstream_grad: bfloat16 [4, 64, 64, 1120], P('dp', 'row', 'col'), may hold values from -6 to 6
Outputs:
- latent_grad: bfloat16 [4, 64, 64, 2240], P('dp', 'row', 'col')
- query_weight_grad: float32 [2240, 1120], P(('row', 'col'), 'dp')
- key_weight_grad: float32 [2240, 1120], P(('row', 'col'), 'dp')
- value_weight_grad: float32 [2240, 1120], P(('row', 'col'), 'dp')
The draws below stay inside these ranges and needn't reach their ends.
All inputs are finite; a program needn't handle non-finite values.
Results may differ from the reference program's by a relative error of at most 0.039.
Values sent between devices are 32-bit elements; how exact they have to be, the bound alone decides.
No kernel may reach another device: no remote copies, remote signals or barrier semaphores. Data moves between devices by JAX's collectives and lax.ppermute only.
A program may use at most 192 MiB of HBM per device.

```python
import math
import jax
import jax.numpy as jnp
from jax import lax

D = 2240
HD = 112
HEADS = 10
IMAGES = 4
GH = 64
GW = 64
TOKENS = 4096


def draw_latent(key, part):
    base_key, token_key, channel_key = jax.random.split(key, 3)
    shape = (IMAGES, GH, GW, D)
    base = jnp.clip(jax.random.normal(base_key, shape, jnp.float32), -5.0, 5.0)
    token_scale = jnp.exp(jax.random.uniform(token_key, (IMAGES, GH, GW, 1), jnp.float32, -1.15, 1.15))
    position = (jnp.arange(GH, dtype=jnp.float32)[:, None] * GW + jnp.arange(GW, dtype=jnp.float32)[None, :]) / (GH * GW)
    rising = jnp.exp(math.log(3.0) * (position - 0.5))[None, :, :, None]
    channel_scale = jnp.exp(jax.random.uniform(channel_key, (D,), jnp.float32, -1.15, 1.15))
    return (base * token_scale * rising * channel_scale / 2.2).astype(jnp.bfloat16)


def shard_levels(own_key, dims, shards, least, top_value):
    loudness = 1.0
    for axis_at, shards_of in shards:
        steps = jax.random.uniform(jax.random.fold_in(jax.random.fold_in(own_key, 6), axis_at), (shards_of,), jnp.float32, least / len(shards), top_value / len(shards))
        loudness = loudness * jnp.repeat(jnp.exp(steps), dims[axis_at] // shards_of).reshape((-1,) + (1,) * (len(dims) - 1 - axis_at))
    return loudness


def gaussian(key, shape, spread, limit, shards=(), kind=jnp.bfloat16):
    values = jax.random.normal(key, shape, jnp.float32) * spread
    if len(shards) > 0:
        values = shard_levels(key, shape, shards, -0.22, 0.18) * values
    return jnp.clip(values, min=-limit, max=limit).astype(kind)


def setup_inputs(seed: int = 0) -> dict:
    streams_of = jax.random.split(jax.random.key(seed), 6)
    return {
        "latent": draw_latent(jax.random.fold_in(streams_of[5], 71), 0),
        "query_weight": gaussian(streams_of[1], (D, HEADS * HD), D ** -0.5, 0.125),
        "key_weight": gaussian(streams_of[2], (D, HEADS * HD), D ** -0.5, 0.125),
        "value_weight": gaussian(streams_of[3], (D, HEADS * HD), D ** -0.5, 0.125),
        "upstream_grad": gaussian(streams_of[4], (IMAGES, GH, GW, HEADS * HD), 1.0, 6.0, ((0, 4), (1, 4), (2, 8))),
    }


EPSILON = 1e-15
HIGHEST_PRECISION = lax.Precision.HIGHEST

def head_split(matrix):
    return matrix.astype(jnp.float32).reshape(matrix.shape[0], HEADS, HD)

def to_low(values):
    return lax.optimization_barrier(values.astype(jnp.bfloat16)).astype(jnp.float32)

def image_grads(pixels, query_weight, key_weight, value_weight, upstream, loss_scale):
    token_rows = pixels.reshape(-1, D)
    query_rows = jnp.dot(token_rows, query_weight, preferred_element_type=jnp.float32).astype(jnp.bfloat16)
    key_rows = jnp.dot(token_rows, key_weight, preferred_element_type=jnp.float32).astype(jnp.bfloat16)
    value_rows = jnp.dot(token_rows, value_weight, preferred_element_type=jnp.float32).astype(jnp.bfloat16)
    relu_query = head_split(jax.nn.relu(query_rows))
    relu_key = head_split(jax.nn.relu(key_rows))
    value_heads = head_split(value_rows)
    key_state = jnp.einsum('thj,thm->hjm', relu_key, value_heads, precision=HIGHEST_PRECISION)
    key_total = lax.optimization_barrier(jnp.sum(relu_key, axis=0))
    denominator = jnp.einsum('thj,hj->th', relu_query, key_total, precision=HIGHEST_PRECISION) + EPSILON
    attended = jnp.einsum('thj,hjm->thm', relu_query, key_state, precision=HIGHEST_PRECISION) / denominator[:, :, None]
    cotangent = head_split(upstream.reshape(-1, HEADS * HD)) * loss_scale
    grad_numer = cotangent / denominator[:, :, None]
    grad_denom = -lax.optimization_barrier(jnp.sum(cotangent * attended, axis=2)) / denominator
    grad_numer_low = to_low(grad_numer)
    grad_relu_query = jnp.einsum('thm,hjm->thj', grad_numer_low, key_state, precision=HIGHEST_PRECISION) + grad_denom[:, :, None] * key_total[None]
    query_heads = query_rows.reshape(-1, HEADS, HD)
    grad_query = jnp.where(query_heads > 0, grad_relu_query, 0.0).reshape(-1, HEADS * HD).astype(jnp.bfloat16)
    state_grad = jnp.einsum('thj,thm->hjm', relu_query, grad_numer_low, precision=HIGHEST_PRECISION)
    total_grad = jnp.einsum('thj,th->hj', relu_query, grad_denom, precision=HIGHEST_PRECISION)
    return (token_rows, key_rows, relu_key, value_heads, grad_query, state_grad, total_grad)

def finish_image(token_rows, key_rows, relu_key, value_heads, grad_query, state_grad, total_grad, query_weight, key_weight, value_weight):
    grad_value = jnp.einsum('thj,hjm->thm', relu_key, state_grad, precision=HIGHEST_PRECISION).reshape(-1, HEADS * HD).astype(jnp.bfloat16)
    grad_relu_key = jnp.einsum('thm,hjm->thj', value_heads, state_grad, precision=HIGHEST_PRECISION) + total_grad[None]
    key_heads = key_rows.reshape(-1, HEADS, HD)
    grad_key = jnp.where(key_heads > 0, grad_relu_key, 0.0).reshape(-1, HEADS * HD).astype(jnp.bfloat16)
    summed = jnp.dot(grad_query, query_weight.T, preferred_element_type=jnp.float32)
    summed = summed + jnp.dot(grad_key, key_weight.T, preferred_element_type=jnp.float32)
    summed = summed + jnp.dot(grad_value, value_weight.T, preferred_element_type=jnp.float32)
    query_term = jnp.dot(token_rows.T, grad_query, preferred_element_type=jnp.float32)
    key_term = jnp.dot(token_rows.T, grad_key, preferred_element_type=jnp.float32)
    value_term = jnp.dot(token_rows.T, grad_value, preferred_element_type=jnp.float32)
    return (summed.astype(jnp.bfloat16), query_term, key_term, value_term)

def reference(latent, query_weight, key_weight, value_weight, upstream_grad):
    loss_scale = 4.0 * math.sqrt(TOKENS)
    normalizer = 1.0 / math.sqrt(TOKENS * IMAGES)
    grad_images = []
    query_sum = jnp.zeros((D, HEADS * HD), jnp.float32)
    key_sum = jnp.zeros((D, HEADS * HD), jnp.float32)
    value_sum = jnp.zeros((D, HEADS * HD), jnp.float32)
    for image_index in range(IMAGES):
        first = image_grads(latent[image_index], query_weight, key_weight, value_weight, upstream_grad[image_index], loss_scale)
        result = finish_image(*first, query_weight, key_weight, value_weight)
        grad_images.append(result[0].reshape(latent.shape[1:]))
        query_sum = query_sum + result[1]
        key_sum = key_sum + result[2]
        value_sum = value_sum + result[3]
    latent_grad = jnp.stack(grad_images, axis=0)
    return (latent_grad, query_sum * normalizer, key_sum * normalizer, value_sum * normalizer)
```

```python
import math

import jax
import jax.numpy as jnp
from jax import lax
from jax.sharding import Mesh, PartitionSpec as P

D = 2240
HD = 112
HEADS = 10
HW = HEADS * HD

EPSILON = 1e-15
HIGHEST = lax.Precision.HIGHEST
IMAGE = ("zh", "core", "x", "zl")
PLANE = ("zh", "x", "zl")


def project(token_rows, weight):
    return jnp.dot(token_rows, weight, preferred_element_type=jnp.float32).astype(jnp.bfloat16)


def back_project(gradient, weight):
    return lax.dot_general(
        gradient, weight, (((1,), (1,)), ((), ())), preferred_element_type=jnp.float32
    )


def exchange(blocks, axes):
    return lax.all_to_all(blocks, axes, 0, 0, tiled=True)


def einsum_high(spec, left, right):
    return jnp.einsum(
        spec, left, right, precision=HIGHEST, preferred_element_type=jnp.float32
    )


def gather_columns(gradient, replicas, scale):
    count = gradient.shape[0]
    blocks = gradient.astype(jnp.float32).reshape(count, replicas, HW // replicas)
    blocks = exchange(jnp.transpose(blocks, (1, 0, 2)), "dp")
    return (blocks.reshape(replicas * count, HW // replicas) * scale).astype(jnp.bfloat16)


def scatter_rows(partial, zh, plane):
    cols = partial.shape[1]
    cores = 2
    blocks = partial.reshape(zh, cores, plane // zh, D // (plane * cores), cols)
    core = lax.axis_index("core")
    own = lax.dynamic_index_in_dim(blocks, core, 1, keepdims=False)
    other = lax.dynamic_index_in_dim(blocks, 1 - core, 1, keepdims=False)
    own = own + lax.ppermute(other, "core", [(0, 1), (1, 0)])
    own = exchange(own.reshape(plane, D // (plane * cores), cols), PLANE)
    return jnp.sum(own, axis=0)


def body(latent, query_weight, key_weight, value_weight, upstream_grad):
    zh = lax.axis_size("zh")
    plane = zh * lax.axis_size("x") * lax.axis_size("zl")
    tiles = plane * lax.axis_size("core")
    replicas = lax.axis_size("dp")
    tokens = latent.reshape(-1, D)
    count = tokens.shape[0]
    image_tokens = count * tiles
    loss_scale = 4.0 * math.sqrt(image_tokens)
    normalizer = 1.0 / math.sqrt(image_tokens * replicas)
    part = HW // tiles

    all_tokens = exchange(
        jnp.broadcast_to(tokens.astype(jnp.float32)[None], (replicas, count, D)), "dp"
    )
    all_tokens = (all_tokens.reshape(replicas * count, D) * 0.5).astype(jnp.bfloat16)

    key_rows = project(tokens, key_weight)
    value_rows = project(tokens, value_weight)
    relu_key = jax.nn.relu(key_rows).reshape(-1, HEADS, HD)
    value_heads = value_rows.reshape(-1, HEADS, HD)
    local_state = jnp.einsum(
        "thj,thm->hjm", relu_key, value_heads, preferred_element_type=jnp.float32
    )
    local_total = jnp.sum(relu_key, axis=0, dtype=jnp.float32)
    sent = jnp.concatenate(
        [
            local_state.reshape(tiles, part, HD),
            jnp.broadcast_to(local_total[None], (tiles, HEADS, HD)),
        ],
        axis=1,
    )
    got = exchange(sent, IMAGE)
    sums = jnp.sum(got, axis=0)
    state_part = sums[:part]
    key_total = sums[part:]

    query_heads = project(tokens, query_weight).reshape(-1, HEADS, HD)
    relu_query = jax.nn.relu(query_heads)
    denominator = einsum_high("thj,hj->th", relu_query, key_total) + EPSILON
    cotangent = upstream_grad.reshape(-1, HEADS, HD).astype(jnp.float32) * loss_scale
    grad_numer = cotangent / denominator[:, :, None]
    grad_numer_low = grad_numer.astype(jnp.bfloat16)
    local_state_grad = jnp.einsum(
        "thj,thm->hjm", relu_query, grad_numer_low, preferred_element_type=jnp.float32
    )
    sent = jnp.concatenate(
        [
            jnp.broadcast_to(state_part[None], (tiles, part, HD)),
            local_state_grad.reshape(tiles, part, HD),
        ],
        axis=1,
    )
    got = exchange(sent, IMAGE)
    key_state = got[:, :part].reshape(HEADS, HD, HD)
    state_grad_part = jnp.sum(got[:, part:], axis=0)

    attended = einsum_high("thj,hjm->thm", relu_query, key_state) / denominator[:, :, None]
    grad_denom = -jnp.sum(cotangent * attended, axis=2) / denominator
    local_total_grad = einsum_high("thj,th->hj", relu_query, grad_denom)
    sent = jnp.concatenate(
        [
            jnp.broadcast_to(state_grad_part[None], (tiles, part, HD)),
            jnp.broadcast_to(local_total_grad[None], (tiles, HEADS, HD)),
        ],
        axis=1,
    )
    got = exchange(sent, IMAGE)
    state_grad = got[:, :part].reshape(HEADS, HD, HD)
    total_grad = jnp.sum(got[:, part:], axis=0)

    grad_relu_query = (
        einsum_high("thm,hjm->thj", grad_numer_low, key_state)
        + grad_denom[:, :, None] * key_total[None]
    )
    grad_query = jnp.where(query_heads > 0, grad_relu_query, 0.0)
    grad_query = grad_query.reshape(-1, HW).astype(jnp.bfloat16)
    query_columns = gather_columns(grad_query, replicas, 2.0 * normalizer)

    grad_value = einsum_high("thj,hjm->thm", relu_key, state_grad)
    grad_value = grad_value.reshape(-1, HW).astype(jnp.bfloat16)
    grad_relu_key = einsum_high("thm,hjm->thj", value_heads, state_grad) + total_grad[None]
    grad_key = jnp.where(key_rows.reshape(-1, HEADS, HD) > 0, grad_relu_key, 0.0)
    grad_key = grad_key.reshape(-1, HW).astype(jnp.bfloat16)
    key_columns = gather_columns(grad_key, replicas, 2.0 * normalizer)
    value_columns = gather_columns(grad_value, replicas, 2.0 * normalizer)

    summed = back_project(grad_query, query_weight) + back_project(grad_key, key_weight)
    summed = summed + back_project(grad_value, value_weight)
    latent_grad = summed.astype(jnp.bfloat16).reshape(latent.shape)

    def weight_grad(columns):
        partial = lax.dot_general(
            all_tokens, columns, (((0,), (0,)), ((), ())), preferred_element_type=jnp.float32
        )
        return scatter_rows(partial, zh, plane)

    return (
        latent_grad,
        weight_grad(query_columns),
        weight_grad(key_columns),
        weight_grad(value_columns),
    )


def solution(mesh):
    devices = mesh.devices
    cores = 2
    zl = 2
    dp, row, col = devices.shape
    fine = Mesh(
        devices.reshape(dp, row // cores, cores, col // zl, zl),
        ("dp", "zh", "core", "x", "zl"),
    )
    grid = P("dp", ("zh", "core"), ("x", "zl"), None)
    weight_out = P(("zh", "core", "x", "zl"), "dp")
    return jax.shard_map(
        body,
        mesh=fine,
        in_specs=(grid, P(), P(), P(), grid),
        out_specs=(grid, weight_out, weight_out, weight_out),
        check_vma=False,
    )
```

```python
import math

import jax
import jax.numpy as jnp
from jax import lax
from jax.experimental import pallas as pl
from jax.experimental.pallas import tpu as pltpu
from jax.sharding import Mesh, PartitionSpec as P

D = 2240
HD = 112
HEADS = 10
HW = HEADS * HD
TILES = 32
PART = HW // TILES
PLANE_SIZE = 16
CORES = 2
ROWS = D // TILES
PADDED_ROWS = 72
REPLICAS = 4
COLS = HW // REPLICAS
TOKENS = 128

EPSILON = 1e-15
IMAGE = ("zh", "core", "x", "zl")
PLANE = ("zh", "x", "zl")
CHUNKS = [(start, min(384, D - start)) for start in range(0, D, 384)]

F32 = jnp.float32
BF16 = jnp.bfloat16
IN_VMEM = pl.BlockSpec(memory_space=pltpu.VMEM)
IN_SMEM = pl.BlockSpec(memory_space=pltpu.SMEM)
IN_HBM = pl.BlockSpec(memory_space=pltpu.HBM)


def shaped(shape, dtype=F32):
    return jax.ShapeDtypeStruct(shape, dtype)


def call(kernel, name, outs, in_specs, scratch=(), vmem=12):
    return pl.pallas_call(
        kernel,
        name=name,
        out_shape=outs,
        in_specs=in_specs,
        out_specs=[IN_VMEM] * len(outs),
        scratch_shapes=list(scratch),
        compiler_params=pltpu.CompilerParams(vmem_limit_bytes=vmem * 1024 * 1024),
    )


def dot(left, right, left_dim, right_dim):
    return lax.dot_general(
        left, right, (((left_dim,), (right_dim,)), ((), ())), preferred_element_type=F32
    )


def split_dot(left, right, left_dim, right_dim):
    high = right.astype(BF16)
    low = (right - high.astype(F32)).astype(BF16)
    return dot(left, high, left_dim, right_dim) + dot(left, low, left_dim, right_dim)


def relu(values):
    return jnp.maximum(values, jnp.zeros_like(values))


def weight_copies(weight, buffer, semaphores, first):
    copies = []
    for index, (start, size) in enumerate(CHUNKS):
        copies.append(
            pltpu.make_async_copy(
                weight.at[pl.ds(start, size)],
                buffer.at[pl.ds(start, size)],
                semaphores.at[first + index],
            )
        )
    return copies


def project(tokens, buffer, copies):
    total = None
    for (start, size), copy in zip(CHUNKS, copies):
        copy.wait()
        term = dot(tokens[:, start : start + size], buffer[start : start + size, :], 1, 0)
        total = term if total is None else total + term
    return total.astype(BF16)


def store_parts(sent, at, state):
    for tile in range(TILES):
        sent[tile, at : at + PART, :] = state[tile * PART : (tile + 1) * PART, :]


def load_parts(state, got):
    for tile in range(TILES):
        state[tile * PART : (tile + 1) * PART, :] = got[tile, :PART, :]


def head(ref, index):
    return ref[index * HD : (index + 1) * HD, :]


def key_value_kernel(
    tokens, key_weight, value_weight, key, value, sent, key_buffer, value_buffer, state, total, semaphores
):
    value_copies = weight_copies(value_weight, value_buffer, semaphores, 0)
    key_copies = weight_copies(key_weight, key_buffer, semaphores, len(CHUNKS))
    for copy in value_copies + key_copies:
        copy.start()
    rows = tokens[...]
    value_rows = project(rows, value_buffer, value_copies)
    key_rows = project(rows, key_buffer, key_copies)
    for index in range(HEADS):
        part = slice(index * HD, (index + 1) * HD)
        key_head = key_rows[:, part]
        value_head = value_rows[:, part]
        key[index] = key_head
        value[index] = value_head
        positive = relu(key_head)
        state[index * HD : (index + 1) * HD, :] = dot(positive, value_head, 0, 0)
        total[index : index + 1, :] = jnp.sum(positive.astype(F32), axis=0, keepdims=True)
    store_parts(sent, 0, state)
    totals = total[...]
    for tile in range(TILES):
        sent[tile, PART : PART + HEADS, :] = totals


def query_kernel(tokens, weight, query):
    query_rows = dot(tokens[...], weight[...], 1, 0).astype(BF16)
    for index in range(HEADS):
        query[index] = query_rows[:, index * HD : (index + 1) * HD]


def inverse_denominator(positive, total):
    return 1.0 / (jnp.sum(positive * total, axis=1, keepdims=True) + EPSILON)


def numerator_kernel(loss_scale, got, query, upstream, sent, numer, total, state):
    sums = got[0]
    for tile in range(1, TILES):
        sums = sums + got[tile]
    state_part = sums[:PART]
    totals = sums[PART : PART + HEADS]
    total[...] = totals
    for index in range(HEADS):
        part = slice(index * HD, (index + 1) * HD)
        positive = relu(query[index])
        inverse = inverse_denominator(positive.astype(F32), totals[index : index + 1])
        cotangent = upstream[:, part].astype(F32) * loss_scale
        numer_low = (cotangent * inverse).astype(BF16)
        numer[index] = numer_low
        state[index * HD : (index + 1) * HD, :] = dot(positive, numer_low, 0, 0)
    for tile in range(TILES):
        sent[tile, :PART, :] = state_part
    store_parts(sent, PART, state)


def total_grad_kernel(loss_scale, got, query, upstream, total, sent, grad_denom, state, totals):
    load_parts(state, got)
    for index in range(HEADS):
        part = slice(index * HD, (index + 1) * HD)
        positive = relu(query[index])
        wide = positive.astype(F32)
        inverse = inverse_denominator(wide, total[index : index + 1, :])
        cotangent = upstream[:, part].astype(F32) * loss_scale
        product = split_dot(positive, head(state, index), 1, 0)
        grad = -(jnp.sum(cotangent * product, axis=1, keepdims=True) * inverse) * inverse
        grad_denom[:, index : index + 1] = grad
        totals[index : index + 1, :] = jnp.sum(wide * grad, axis=0, keepdims=True)
    part_sum = got[0, PART:, :]
    for tile in range(1, TILES):
        part_sum = part_sum + got[tile, PART:, :]
    values = totals[...]
    for tile in range(TILES):
        sent[tile, :PART, :] = part_sum
        sent[tile, PART : PART + HEADS, :] = values


def place_columns(place, blocks, outs, at):
    for slot, out in enumerate(outs):
        out[:, at : at + COLS] = blocks[lax.rem(place[0] + slot, REPLICAS)]


def split_columns(flat, blocks):
    for block in range(REPLICAS):
        blocks[block] = flat[:, block * COLS : (block + 1) * COLS]


def query_grad_kernel(
    place, got, query, numer, total, grad_denom, grad, own, first, second, third, state, flat, blocks
):
    load_parts(state, got)
    for index in range(HEADS):
        part = slice(index * HD, (index + 1) * HD)
        values = split_dot(numer[index], head(state, index), 1, 1)
        values = values + grad_denom[:, index : index + 1] * total[index : index + 1, :]
        values = jnp.where(query[index].astype(F32) > 0, values, 0.0).astype(BF16)
        grad[:, part] = values
        flat[:, part] = values.astype(F32)
    split_columns(flat, blocks)
    place_columns(place, blocks, (own, first, second, third), 0)


def key_value_grad_kernel(
    place, got, key, value, grad_key, grad_value, own, first, second, third, state, flat_key, flat_value, blocks
):
    load_parts(state, got)
    totals = got[0, PART : PART + HEADS, :]
    for tile in range(1, TILES):
        totals = totals + got[tile, PART : PART + HEADS, :]
    for index in range(HEADS):
        part = slice(index * HD, (index + 1) * HD)
        key_head = key[index]
        positive = relu(key_head)
        state_head = head(state, index)
        values = split_dot(positive, state_head, 1, 0).astype(BF16)
        grad_value[:, part] = values
        flat_value[:, part] = values.astype(F32)
        values = split_dot(value[index], state_head, 1, 1) + totals[index : index + 1]
        values = jnp.where(key_head.astype(F32) > 0, values, 0.0).astype(BF16)
        grad_key[:, part] = values
        flat_key[:, part] = values.astype(F32)
    outs = (own, first, second, third)
    split_columns(flat_key, blocks)
    place_columns(place, blocks, outs, 0)
    split_columns(flat_value, blocks)
    place_columns(place, blocks, outs, COLS)


def turn_kernel(tokens, out):
    for start in range(0, D, 128):
        size = min(128, D - start)
        out[start : start + size, :] = tokens[:, start : start + size].astype(F32).T


def join_kernel(own, first, second, third, out):
    for slot, turned in enumerate((own, first, second, third)):
        out[:, slot * TOKENS : (slot + 1) * TOKENS] = turned[...].astype(BF16)


def weight_grad_kernel(normalizer, core, tokens, own, first, second, third, kept, sent, columns):
    for slot, block in enumerate((own, first, second, third)):
        columns[slot * TOKENS : (slot + 1) * TOKENS, :] = block[...].astype(BF16)
    right = columns[...]
    span = PLANE_SIZE // CORES
    for out, which in ((sent, 1 - core[0]), (kept, core[0])):
        for half in range(CORES):
            start = pl.multiple_of((half * CORES + which) * (span * ROWS), 16)
            product = dot(tokens[pl.ds(start, span * ROWS), :], right, 1, 0) * normalizer
            for index in range(span):
                out[half * span + index, :ROWS, :] = product[index * ROWS : (index + 1) * ROWS]


def exchange(blocks, axes):
    return lax.all_to_all(blocks, axes, 0, 0, tiled=True)


def shift(values, by):
    return lax.ppermute(values, "dp", [(i, (i + by) % REPLICAS) for i in range(REPLICAS)])


def back_project(gradient, weight):
    return dot(gradient, weight, 1, 1)


def body(latent, query_weight, key_weight, value_weight, upstream_grad):
    image_tokens = TOKENS * TILES
    loss_scale = 4.0 * math.sqrt(image_tokens)
    normalizer = 1.0 / math.sqrt(image_tokens * REPLICAS)
    tokens = latent.reshape(TOKENS, D)
    upstream = upstream_grad.reshape(TOKENS, HW)
    place = lax.axis_index("dp").reshape(1)
    core = lax.axis_index("core").reshape(1)
    heads = shaped((HEADS, TOKENS, HD), BF16)
    flat = shaped((TOKENS, HW), BF16)
    state = pltpu.VMEM((HW, HD), F32)
    totals = pltpu.VMEM((HEADS, HD), F32)
    weight = pltpu.VMEM((D, HW), BF16)
    wide = pltpu.VMEM((TOKENS, HW), F32)
    blocks = pltpu.VMEM((REPLICAS, TOKENS, COLS), F32)

    key, value, sent = call(
        key_value_kernel,
        "key_value",
        [heads, heads, shaped((TILES, PART + HEADS, HD))],
        [IN_VMEM, IN_HBM, IN_HBM],
        [weight, weight, state, totals, pltpu.SemaphoreType.DMA((2 * len(CHUNKS),))],
        vmem=20,
    )(tokens, key_weight, value_weight)
    sent, later_tokens = lax.optimization_barrier((sent, tokens))
    (turned,) = call(turn_kernel, "turn", [shaped((D, TOKENS))], [IN_VMEM])(later_tokens)
    turned = [turned] + [shift(turned, s) for s in (1, 2, 3)]
    got = exchange(sent, IMAGE)
    (query,) = call(
        query_kernel,
        "query",
        [heads],
        [IN_VMEM, IN_VMEM],
    )(tokens, query_weight)
    sent, numer, total = call(
        lambda *refs: numerator_kernel(loss_scale, *refs),
        "numerator",
        [shaped((TILES, 2 * PART, HD)), heads, shaped((HEADS, HD))],
        [IN_VMEM] * 3,
        [state],
    )(got, query, upstream)
    got_state = exchange(sent, IMAGE)
    sent, grad_denom = call(
        lambda *refs: total_grad_kernel(loss_scale, *refs),
        "total_grad",
        [shaped((TILES, PART + HEADS, HD)), shaped((TOKENS, HEADS))],
        [IN_VMEM] * 4,
        [state, totals],
    )(got_state, query, upstream, total)
    sent, turned[1], turned[3] = lax.optimization_barrier((sent, turned[1], turned[3]))
    got = exchange(sent, IMAGE)

    block = shaped((TOKENS, COLS))
    grad_query, *query_columns = call(
        query_grad_kernel,
        "query_grad",
        [flat, block, block, block, block],
        [IN_SMEM] + [IN_VMEM] * 5,
        [state, wide, blocks],
    )(place, got_state, query, numer, total, grad_denom)
    query_columns = [query_columns[0]] + [shift(query_columns[s], s) for s in (1, 2, 3)]
    (all_tokens,) = call(
        join_kernel, "join", [shaped((D, REPLICAS * TOKENS), BF16)], [IN_VMEM] * 4
    )(*turned)
    got, all_tokens, query_columns = lax.optimization_barrier((got, all_tokens, query_columns))

    block = shaped((TOKENS, 2 * COLS))
    grad_key, grad_value, *key_value_columns = call(
        key_value_grad_kernel,
        "key_value_grad",
        [flat, flat, block, block, block, block],
        [IN_SMEM] + [IN_VMEM] * 3,
        [state, wide, wide, blocks],
    )(place, got, key, value)
    key_value_columns = [key_value_columns[0]] + [
        shift(key_value_columns[s], s) for s in (1, 2, 3)
    ]

    def weight_grad(columns):
        width = columns[0].shape[1]
        half = shaped((PLANE_SIZE, PADDED_ROWS, width))
        kept, given = call(
            lambda *refs: weight_grad_kernel(normalizer, *refs),
            "weight_grad",
            [half, half],
            [IN_SMEM] + [IN_VMEM] * 5,
            [pltpu.VMEM((REPLICAS * TOKENS, width), BF16)],
            vmem=24,
        )(core, all_tokens, *columns)
        kept = kept + lax.ppermute(given, "core", [(0, 1), (1, 0)])
        return jnp.sum(exchange(kept, PLANE), axis=0)[:ROWS]

    query_out = weight_grad(query_columns)
    key_value_out = weight_grad(key_value_columns)

    summed = back_project(grad_query, query_weight) + back_project(grad_key, key_weight)
    summed = summed + back_project(grad_value, value_weight)
    latent_grad = summed.astype(BF16).reshape(latent.shape)
    return latent_grad, query_out, key_value_out[:, :COLS], key_value_out[:, COLS:]


def solution(mesh):
    devices = mesh.devices
    fine = Mesh(
        devices.reshape(REPLICAS, 2, CORES, 4, 2), ("dp", "zh", "core", "x", "zl")
    )
    grid = P("dp", ("zh", "core"), ("x", "zl"), None)
    weight_out = P(("zh", "core", "x", "zl"), "dp")
    return jax.shard_map(
        body,
        mesh=fine,
        in_specs=(grid, P(), P(), P(), grid),
        out_specs=(grid, weight_out, weight_out, weight_out),
        check_vma=False,
    )
```

```python
import math

import jax
import jax.numpy as jnp
from jax import lax
from jax.experimental import pallas as pl
from jax.experimental.pallas import tpu as pltpu
from jax.sharding import Mesh, PartitionSpec as P

D = 2240
HD = 112
HEADS = 10
HW = HEADS * HD
TILES = 32
PART = HW // TILES
PLANE_SIZE = 16
CORES = 2
ROWS = D // TILES
PADDED_ROWS = 72
SPLIT = 40
REPLICAS = 4
RING = 4
COLS = HW // REPLICAS
TOKENS = 128

EPSILON = 1e-15
IMAGE = ("zh", "core", "x", "zl")
PLANE = ("zh", "x", "zl")
CHUNKS = [(start, min(384, D - start)) for start in range(0, D, 384)]

F32 = jnp.float32
BF16 = jnp.bfloat16
IN_VMEM = pl.BlockSpec(memory_space=pltpu.VMEM)
IN_SMEM = pl.BlockSpec(memory_space=pltpu.SMEM)
IN_HBM = pl.BlockSpec(memory_space=pltpu.HBM)


def shaped(shape, dtype=F32):
    return jax.ShapeDtypeStruct(shape, dtype)


def call(kernel, name, outs, in_specs, scratch=(), vmem=12):
    return pl.pallas_call(
        kernel,
        name=name,
        out_shape=outs,
        in_specs=in_specs,
        out_specs=[IN_VMEM] * len(outs),
        scratch_shapes=list(scratch),
        compiler_params=pltpu.CompilerParams(vmem_limit_bytes=vmem * 1024 * 1024),
    )


def dot(left, right, left_dim, right_dim):
    return lax.dot_general(
        left, right, (((left_dim,), (right_dim,)), ((), ())), preferred_element_type=F32
    )


def split_dot(left, right, left_dim, right_dim):
    high = right.astype(BF16)
    low = (right - high.astype(F32)).astype(BF16)
    return dot(left, high, left_dim, right_dim) + dot(left, low, left_dim, right_dim)


def relu(values):
    return jnp.maximum(values, jnp.zeros_like(values))


def weight_copies(weight, buffer, semaphores, first):
    copies = []
    for index, (start, size) in enumerate(CHUNKS):
        copies.append(
            pltpu.make_async_copy(
                weight.at[pl.ds(start, size)],
                buffer.at[pl.ds(start, size)],
                semaphores.at[first + index],
            )
        )
    return copies


def project(tokens, buffer, copies):
    total = None
    for (start, size), copy in zip(CHUNKS, copies):
        copy.wait()
        term = dot(tokens[:, start : start + size], buffer[start : start + size, :], 1, 0)
        total = term if total is None else total + term
    return total.astype(BF16)


def store_parts(sent, at, state):
    for tile in range(TILES):
        sent[tile, at : at + PART, :] = state[tile * PART : (tile + 1) * PART, :]


def load_parts(state, got):
    for tile in range(TILES):
        state[tile * PART : (tile + 1) * PART, :] = got[tile, :PART, :]


def head(ref, index):
    return ref[index * HD : (index + 1) * HD, :]


def key_value_kernel(
    tokens, key_weight, value_weight, key, value, sent, key_buffer, value_buffer, state, total, semaphores
):
    value_copies = weight_copies(value_weight, value_buffer, semaphores, 0)
    key_copies = weight_copies(key_weight, key_buffer, semaphores, len(CHUNKS))
    for copy in value_copies + key_copies:
        copy.start()
    rows = tokens[...]
    value_rows = project(rows, value_buffer, value_copies)
    key_rows = project(rows, key_buffer, key_copies)
    for index in range(HEADS):
        part = slice(index * HD, (index + 1) * HD)
        key_head = key_rows[:, part]
        value_head = value_rows[:, part]
        key[index] = key_head
        value[index] = value_head
        positive = relu(key_head)
        state[index * HD : (index + 1) * HD, :] = dot(positive, value_head, 0, 0)
        total[index : index + 1, :] = jnp.sum(positive.astype(F32), axis=0, keepdims=True)
    store_parts(sent, 0, state)
    totals = total[...]
    for tile in range(TILES):
        sent[tile, PART : PART + HEADS, :] = totals


def query_kernel(tokens, weight, query):
    query_rows = dot(tokens[...], weight[...], 1, 0).astype(BF16)
    for index in range(HEADS):
        query[index] = query_rows[:, index * HD : (index + 1) * HD]


def inverse_denominator(positive, total):
    return 1.0 / (jnp.sum(positive * total, axis=1, keepdims=True) + EPSILON)


def numerator_kernel(loss_scale, got, query, upstream, sent, numer, total, state):
    sums = got[0]
    for tile in range(1, TILES):
        sums = sums + got[tile]
    state_part = sums[:PART]
    totals = sums[PART : PART + HEADS]
    total[...] = totals
    for index in range(HEADS):
        part = slice(index * HD, (index + 1) * HD)
        positive = relu(query[index])
        inverse = inverse_denominator(positive.astype(F32), totals[index : index + 1])
        cotangent = upstream[:, part].astype(F32) * loss_scale
        numer_low = (cotangent * inverse).astype(BF16)
        numer[index] = numer_low
        state[index * HD : (index + 1) * HD, :] = dot(positive, numer_low, 0, 0)
    for tile in range(TILES):
        sent[tile, :PART, :] = state_part
    store_parts(sent, PART, state)


def total_grad_kernel(loss_scale, got, query, upstream, total, sent, grad_denom, state, totals):
    load_parts(state, got)
    for index in range(HEADS):
        part = slice(index * HD, (index + 1) * HD)
        positive = relu(query[index])
        wide = positive.astype(F32)
        inverse = inverse_denominator(wide, total[index : index + 1, :])
        cotangent = upstream[:, part].astype(F32) * loss_scale
        product = split_dot(positive, head(state, index), 1, 0)
        grad = -(jnp.sum(cotangent * product, axis=1, keepdims=True) * inverse) * inverse
        grad_denom[:, index : index + 1] = grad
        totals[index : index + 1, :] = jnp.sum(wide * grad, axis=0, keepdims=True)
    part_sum = got[0, PART:, :]
    for tile in range(1, TILES):
        part_sum = part_sum + got[tile, PART:, :]
    values = totals[...]
    for tile in range(TILES):
        sent[tile, :PART, :] = part_sum
        sent[tile, PART : PART + HEADS, :] = values


def place_columns(place, blocks, outs, at):
    for slot, out in enumerate(outs):
        out[:, at : at + COLS] = blocks[lax.rem(place[0] + slot, REPLICAS)]


def split_columns(flat, blocks):
    for block in range(REPLICAS):
        blocks[block] = flat[:, block * COLS : (block + 1) * COLS]


def query_grad_kernel(
    place, got, query, numer, total, grad_denom, grad, own, first, second, third, state, flat, blocks
):
    load_parts(state, got)
    for index in range(HEADS):
        part = slice(index * HD, (index + 1) * HD)
        values = split_dot(numer[index], head(state, index), 1, 1)
        values = values + grad_denom[:, index : index + 1] * total[index : index + 1, :]
        values = jnp.where(query[index].astype(F32) > 0, values, 0.0).astype(BF16)
        grad[:, part] = values
        flat[:, part] = values.astype(F32)
    split_columns(flat, blocks)
    place_columns(place, blocks, (own, first, second, third), 0)


def key_value_grad_kernel(
    place, got, key, value, grad_key, grad_value, own, first, second, third, state, flat_key, flat_value, blocks
):
    load_parts(state, got)
    totals = got[0, PART : PART + HEADS, :]
    for tile in range(1, TILES):
        totals = totals + got[tile, PART : PART + HEADS, :]
    for index in range(HEADS):
        part = slice(index * HD, (index + 1) * HD)
        key_head = key[index]
        positive = relu(key_head)
        state_head = head(state, index)
        values = split_dot(positive, state_head, 1, 0).astype(BF16)
        grad_value[:, part] = values
        flat_value[:, part] = values.astype(F32)
        values = split_dot(value[index], state_head, 1, 1) + totals[index : index + 1]
        values = jnp.where(key_head.astype(F32) > 0, values, 0.0).astype(BF16)
        grad_key[:, part] = values
        flat_key[:, part] = values.astype(F32)
    outs = (own, first, second, third)
    split_columns(flat_key, blocks)
    place_columns(place, blocks, outs, 0)
    split_columns(flat_value, blocks)
    place_columns(place, blocks, outs, COLS)


def turn_kernel(tokens, out):
    for start in range(0, D, 128):
        size = min(128, D - start)
        out[start : start + size, :] = tokens[:, start : start + size].astype(F32).T


def join_kernel(own, first, second, third, out):
    for slot, turned in enumerate((own, first, second, third)):
        out[:, slot * TOKENS : (slot + 1) * TOKENS] = turned[...].astype(BF16)


def weight_grad_kernel(normalizer, core, tokens, own, first, second, third, kept, sent, columns):
    for slot, block in enumerate((own, first, second, third)):
        columns[slot * TOKENS : (slot + 1) * TOKENS, :] = block[...].astype(BF16)
    right = columns[...]
    span = PLANE_SIZE // CORES
    for out, which in ((sent, 1 - core[0]), (kept, core[0])):
        for half in range(CORES):
            start = pl.multiple_of((half * CORES + which) * (span * ROWS), 16)
            product = dot(tokens[pl.ds(start, span * ROWS), :], right, 1, 0) * normalizer
            for index in range(span):
                out[half * span + index, :ROWS, :] = product[index * ROWS : (index + 1) * ROWS]


def first_stage_kernel(spot, kept, got, *outs):
    for slot in range(RING):
        across = lax.rem(spot[0] + slot, RING)
        along = lax.rem(spot[1] + slot, RING)
        for other in range(RING):
            at = (other // 2) * (2 * RING) + across * 2 + other % 2
            outs[slot][other] = kept[at, :SPLIT, :] + got[at, :SPLIT, :]
            at = (along // 2) * (2 * RING) + other * 2 + lax.rem(along, 2)
            outs[RING + slot][other] = kept[at, SPLIT:, :] + got[at, SPLIT:, :]


def second_stage_kernel(spot, *refs):
    uppers, lowers, outs = refs[:RING], refs[RING : 2 * RING], refs[2 * RING :]
    for slot in range(RING):
        along = lax.rem(spot[1] + slot, RING)
        outs[slot][...] = sum_at(uppers, along)
        across = lax.rem(spot[0] + slot, RING)
        outs[RING + slot][...] = sum_at(lowers, across)


def sum_at(refs, at):
    return (refs[0][at] + refs[1][at]) + (refs[2][at] + refs[3][at])


def last_kernel(query, *refs):
    uppers, lowers = refs[:RING], refs[RING : 2 * RING]
    query_out, key_out, value_out = refs[2 * RING :]
    total = query[0]
    for index in range(1, PLANE_SIZE):
        total = total + query[index]
    query_out[...] = total[:ROWS]
    for refs, rows, size in ((uppers, 0, SPLIT), (lowers, SPLIT, ROWS - SPLIT)):
        total = (refs[0][...] + refs[1][...]) + (refs[2][...] + refs[3][...])
        key_out[rows : rows + size, :] = total[:size, :COLS]
        value_out[rows : rows + size, :] = total[:size, COLS:]


def exchange(blocks, axes):
    return lax.all_to_all(blocks, axes, 0, 0, tiled=True)


def shift(values, by, axis):
    return lax.ppermute(values, axis, [(i, (i + by) % RING) for i in range(RING)])


def shifted(slots, axis):
    return [slots[0]] + [shift(slots[s], s, axis) for s in range(1, RING)]


def back_project(gradient, weight):
    return dot(gradient, weight, 1, 1)


def body(latent, query_weight, key_weight, value_weight, upstream_grad):
    image_tokens = TOKENS * TILES
    loss_scale = 4.0 * math.sqrt(image_tokens)
    normalizer = 1.0 / math.sqrt(image_tokens * REPLICAS)
    tokens = latent.reshape(TOKENS, D)
    upstream = upstream_grad.reshape(TOKENS, HW)
    place = lax.axis_index("dp").reshape(1)
    core = lax.axis_index("core").reshape(1)
    spot = jnp.stack([lax.axis_index("x"), lax.axis_index(("zh", "zl"))])
    heads = shaped((HEADS, TOKENS, HD), BF16)
    flat = shaped((TOKENS, HW), BF16)
    state = pltpu.VMEM((HW, HD), F32)
    totals = pltpu.VMEM((HEADS, HD), F32)
    weight = pltpu.VMEM((D, HW), BF16)
    wide = pltpu.VMEM((TOKENS, HW), F32)
    blocks = pltpu.VMEM((REPLICAS, TOKENS, COLS), F32)

    (turned,) = call(turn_kernel, "turn", [shaped((D, TOKENS))], [IN_VMEM])(tokens)
    turned = [turned] + [shift(turned, s, "dp") for s in (1, 3, 2)]

    key, value, sent = call(
        key_value_kernel,
        "key_value",
        [heads, heads, shaped((TILES, PART + HEADS, HD))],
        [IN_VMEM, IN_HBM, IN_HBM],
        [weight, weight, state, totals, pltpu.SemaphoreType.DMA((2 * len(CHUNKS),))],
        vmem=20,
    )(
        tokens,
        pltpu.with_memory_space_constraint(key_weight, pltpu.HBM),
        pltpu.with_memory_space_constraint(value_weight, pltpu.HBM),
    )
    got = exchange(sent, IMAGE)
    (query,) = call(
        query_kernel,
        "query",
        [heads],
        [IN_VMEM, IN_VMEM],
    )(tokens, query_weight)
    sent, numer, total = call(
        lambda *refs: numerator_kernel(loss_scale, *refs),
        "numerator",
        [shaped((TILES, 2 * PART, HD)), heads, shaped((HEADS, HD))],
        [IN_VMEM] * 3,
        [state],
    )(got, query, upstream)
    got_state = exchange(sent, IMAGE)
    sent, grad_denom = call(
        lambda *refs: total_grad_kernel(loss_scale, *refs),
        "total_grad",
        [shaped((TILES, PART + HEADS, HD)), shaped((TOKENS, HEADS))],
        [IN_VMEM] * 4,
        [state, totals],
    )(got_state, query, upstream, total)
    sent, turned[1], turned[2] = lax.optimization_barrier((sent, turned[1], turned[2]))
    got = exchange(sent, IMAGE)

    block = shaped((TOKENS, COLS))
    grad_query, *query_columns = call(
        query_grad_kernel,
        "query_grad",
        [flat, block, block, block, block],
        [IN_SMEM] + [IN_VMEM] * 5,
        [state, wide, blocks],
    )(place, got_state, query, numer, total, grad_denom)
    query_columns = shifted(query_columns, "dp")
    (all_tokens,) = call(
        join_kernel, "join", [shaped((D, REPLICAS * TOKENS), BF16)], [IN_VMEM] * 4
    )(turned[0], turned[1], turned[3], turned[2])
    got, all_tokens, query_columns = lax.optimization_barrier((got, all_tokens, query_columns))

    block = shaped((TOKENS, 2 * COLS))
    grad_key, grad_value, *key_value_columns = call(
        key_value_grad_kernel,
        "key_value_grad",
        [flat, flat, block, block, block, block],
        [IN_SMEM] + [IN_VMEM] * 3,
        [state, wide, wide, blocks],
    )(place, got, key, value)
    key_value_columns = shifted(key_value_columns, "dp")

    def partial_sum(columns):
        width = columns[0].shape[1]
        half = shaped((PLANE_SIZE, PADDED_ROWS, width))
        kept, given = call(
            lambda *refs: weight_grad_kernel(normalizer, *refs),
            "weight_grad",
            [half, half],
            [IN_SMEM] + [IN_VMEM] * 5,
            [pltpu.VMEM((REPLICAS * TOKENS, width), BF16)],
            vmem=24,
        )(core, all_tokens, *columns)
        return kept, lax.ppermute(given, "core", [(0, 1), (1, 0)])

    kept, got = partial_sum(query_columns)
    query_part, key_value_columns = lax.optimization_barrier((kept + got, key_value_columns))
    query_out = exchange(query_part, PLANE)

    kept, got = partial_sum(key_value_columns)
    upper = shaped((RING, SPLIT, 2 * COLS))
    lower = shaped((RING, PADDED_ROWS - SPLIT, 2 * COLS))
    slots = call(
        first_stage_kernel,
        "first_stage",
        [upper] * RING + [lower] * RING,
        [IN_SMEM, IN_VMEM, IN_VMEM],
        vmem=24,
    )(spot, kept, got)
    slots = shifted(slots[:RING], "x") + shifted(slots[RING:], ("zh", "zl"))
    slots, query_out = lax.optimization_barrier((slots, query_out))
    upper = shaped((SPLIT, 2 * COLS))
    lower = shaped((PADDED_ROWS - SPLIT, 2 * COLS))
    slots = call(
        second_stage_kernel,
        "second_stage",
        [upper] * RING + [lower] * RING,
        [IN_SMEM] + [IN_VMEM] * (2 * RING),
    )(spot, *slots)
    slots = shifted(slots[:RING], ("zh", "zl")) + shifted(slots[RING:], "x")
    block = shaped((ROWS, COLS))
    query_out, key_out, value_out = call(
        last_kernel, "last", [block] * 3, [IN_VMEM] * (1 + 2 * RING)
    )(query_out, *slots)

    summed = back_project(grad_query, query_weight) + back_project(grad_key, key_weight)
    summed = summed + back_project(grad_value, value_weight)
    latent_grad = summed.astype(BF16).reshape(latent.shape)
    return latent_grad, query_out, key_out, value_out


def solution(mesh):
    devices = mesh.devices
    fine = Mesh(
        devices.reshape(REPLICAS, 2, CORES, 4, 2), ("dp", "zh", "core", "x", "zl")
    )
    grid = P("dp", ("zh", "core"), ("x", "zl"), None)
    weight_out = P(("zh", "core", "x", "zl"), "dp")
    return jax.shard_map(
        body,
        mesh=fine,
        in_specs=(grid, P(), P(), P(), grid),
        out_specs=(grid, weight_out, weight_out, weight_out),
        check_vma=False,
    )
```

```python
import math

import jax
import jax.numpy as jnp
from jax import lax
from jax.experimental import pallas as pl
from jax.experimental.pallas import tpu as pltpu
from jax.sharding import Mesh, PartitionSpec as P

D = 2240
HD = 112
HEADS = 10
HW = HEADS * HD
TILES = 32
PART = HW // TILES
PLANE_SIZE = 16
CORES = 2
ROWS = D // TILES
PADDED_ROWS = 72
SPLIT = 40
REPLICAS = 4
RING = 4
COLS = HW // REPLICAS
EARLY = 256
LATE = COLS - EARLY
WIDE = 2 * COLS + LATE
TOKENS = 128

EPSILON = 1e-15
IMAGE = ("zh", "core", "x", "zl")
PLANE = ("zh", "x", "zl")
CHUNKS = [(start, min(384, D - start)) for start in range(0, D, 384)]

F32 = jnp.float32
BF16 = jnp.bfloat16
BLOCK = pl.BlockSpec()
IN_SMEM = pl.BlockSpec(memory_space=pltpu.SMEM)
IN_HBM = pl.BlockSpec(memory_space=pltpu.HBM)


def shaped(shape, dtype=F32):
    return pltpu.HBM(shape, dtype)


def call(kernel, name, outs, in_specs, scratch=(), vmem=12, arrived=()):
    run = pl.pallas_call(
        kernel,
        name=name,
        grid=(1,),
        out_shape=outs,
        in_specs=in_specs,
        out_specs=[BLOCK] * len(outs),
        scratch_shapes=list(scratch),
        compiler_params=pltpu.CompilerParams(vmem_limit_bytes=vmem * 1024 * 1024),
    )

    def with_placed(*operands):
        placed = [
            operand
            if spec is IN_SMEM or index in arrived
            else pltpu.with_memory_space_constraint(operand, pltpu.HBM)
            for index, (operand, spec) in enumerate(zip(operands, in_specs))
        ]
        return run(*placed)

    return with_placed


def dot(left, right, left_dim, right_dim):
    return lax.dot_general(
        left, right, (((left_dim,), (right_dim,)), ((), ())), preferred_element_type=F32
    )


def split_dot(left, right, left_dim, right_dim):
    high = right.astype(BF16)
    low = (right - high.astype(F32)).astype(BF16)
    return dot(left, high, left_dim, right_dim) + dot(left, low, left_dim, right_dim)


def relu(values):
    return jnp.maximum(values, jnp.zeros_like(values))


def weight_copies(weight, buffer, semaphores, first):
    copies = []
    for index, (start, size) in enumerate(CHUNKS):
        copies.append(
            pltpu.make_async_copy(
                weight.at[pl.ds(start, size)],
                buffer.at[pl.ds(start, size)],
                semaphores.at[first + index],
            )
        )
    return copies


def project(tokens, buffer, copies):
    total = None
    for (start, size), copy in zip(CHUNKS, copies):
        copy.wait()
        term = dot(tokens[:, start : start + size], buffer[start : start + size, :], 1, 0)
        total = term if total is None else total + term
    return total.astype(BF16)


def store_parts(sent, at, state):
    for tile in range(TILES):
        sent[tile, at : at + PART, :] = state[tile * PART : (tile + 1) * PART, :]


def load_parts(state, got):
    for tile in range(TILES):
        state[tile * PART : (tile + 1) * PART, :] = got[tile, :PART, :]


def head(ref, index):
    return ref[index * HD : (index + 1) * HD, :]


def key_value_kernel(
    tokens, key_weight, value_weight, key, value, sent, key_buffer, value_buffer, state, total, semaphores
):
    value_copies = weight_copies(value_weight, value_buffer, semaphores, 0)
    key_copies = weight_copies(key_weight, key_buffer, semaphores, len(CHUNKS))
    for copy in value_copies + key_copies:
        copy.start()
    rows = tokens[...]
    value_rows = project(rows, value_buffer, value_copies)
    key_rows = project(rows, key_buffer, key_copies)
    for index in range(HEADS):
        part = slice(index * HD, (index + 1) * HD)
        key_head = key_rows[:, part]
        value_head = value_rows[:, part]
        key[index] = key_head
        value[index] = value_head
        positive = relu(key_head)
        state[index * HD : (index + 1) * HD, :] = dot(positive, value_head, 0, 0)
        total[index : index + 1, :] = jnp.sum(positive.astype(F32), axis=0, keepdims=True)
    store_parts(sent, 0, state)
    totals = total[...]
    for tile in range(TILES):
        sent[tile, PART : PART + HEADS, :] = totals


def query_kernel(tokens, weight, query):
    query_rows = dot(tokens[...], weight[...], 1, 0).astype(BF16)
    for index in range(HEADS):
        query[index] = query_rows[:, index * HD : (index + 1) * HD]


def inverse_denominator(positive, total):
    return 1.0 / (jnp.sum(positive * total, axis=1, keepdims=True) + EPSILON)


def numerator_kernel(loss_scale, got, query, upstream, sent, numer, total, state):
    sums = got[0]
    for tile in range(1, TILES):
        sums = sums + got[tile]
    state_part = sums[:PART]
    totals = sums[PART : PART + HEADS]
    total[...] = totals
    for index in range(HEADS):
        part = slice(index * HD, (index + 1) * HD)
        positive = relu(query[index])
        inverse = inverse_denominator(positive.astype(F32), totals[index : index + 1])
        cotangent = upstream[:, part].astype(F32) * loss_scale
        numer_low = (cotangent * inverse).astype(BF16)
        numer[index] = numer_low
        state[index * HD : (index + 1) * HD, :] = dot(positive, numer_low, 0, 0)
    for tile in range(TILES):
        sent[tile, :PART, :] = state_part
    store_parts(sent, PART, state)


def total_grad_kernel(loss_scale, got, query, upstream, total, sent, grad_denom, state, totals):
    load_parts(state, got)
    for index in range(HEADS):
        part = slice(index * HD, (index + 1) * HD)
        positive = relu(query[index])
        wide = positive.astype(F32)
        inverse = inverse_denominator(wide, total[index : index + 1, :])
        cotangent = upstream[:, part].astype(F32) * loss_scale
        product = split_dot(positive, head(state, index), 1, 0)
        grad = -(jnp.sum(cotangent * product, axis=1, keepdims=True) * inverse) * inverse
        grad_denom[:, index : index + 1] = grad
        totals[index : index + 1, :] = jnp.sum(wide * grad, axis=0, keepdims=True)
    part_sum = got[0, PART:, :]
    for tile in range(1, TILES):
        part_sum = part_sum + got[tile, PART:, :]
    values = totals[...]
    for tile in range(TILES):
        sent[tile, :PART, :] = part_sum
        sent[tile, PART : PART + HEADS, :] = values


def place_columns(place, blocks, outs, at, first=0, last=COLS):
    for slot, out in enumerate(outs):
        block = blocks[lax.rem(place[0] + slot, REPLICAS)]
        out[:, at : at + last - first] = block[:, first:last]


def split_columns(flat, blocks):
    for block in range(REPLICAS):
        blocks[block] = flat[:, block * COLS : (block + 1) * COLS]


def query_grad_kernel(
    place, got, query, numer, total, grad_denom, grad, own, first, second, third, late, state, flat, blocks
):
    load_parts(state, got)
    for index in range(HEADS):
        part = slice(index * HD, (index + 1) * HD)
        values = split_dot(numer[index], head(state, index), 1, 1)
        values = values + grad_denom[:, index : index + 1] * total[index : index + 1, :]
        values = jnp.where(query[index].astype(F32) > 0, values, 0.0).astype(BF16)
        grad[:, part] = values
        flat[:, part] = values.astype(F32)
    split_columns(flat, blocks)
    place_columns(place, blocks, (own, first, second, third), 0, 0, EARLY)
    for slot in range(REPLICAS):
        late[slot] = blocks[lax.rem(place[0] + slot, REPLICAS)][:, EARLY:]


def key_value_grad_kernel(
    place, got, key, value, late, grad_key, grad_value, own, first, second, third, state, flat_key, flat_value, blocks
):
    load_parts(state, got)
    totals = got[0, PART : PART + HEADS, :]
    for tile in range(1, TILES):
        totals = totals + got[tile, PART : PART + HEADS, :]
    for index in range(HEADS):
        part = slice(index * HD, (index + 1) * HD)
        key_head = key[index]
        positive = relu(key_head)
        state_head = head(state, index)
        values = split_dot(positive, state_head, 1, 0).astype(BF16)
        grad_value[:, part] = values
        flat_value[:, part] = values.astype(F32)
        values = split_dot(value[index], state_head, 1, 1) + totals[index : index + 1]
        values = jnp.where(key_head.astype(F32) > 0, values, 0.0).astype(BF16)
        grad_key[:, part] = values
        flat_key[:, part] = values.astype(F32)
    outs = (own, first, second, third)
    split_columns(flat_key, blocks)
    place_columns(place, blocks, outs, 0)
    split_columns(flat_value, blocks)
    place_columns(place, blocks, outs, COLS)
    for slot, out in enumerate(outs):
        out[:, 2 * COLS :] = late[slot]


def turn_kernel(tokens, top, bottom):
    for start in range(0, D, 128):
        turned = tokens[:, start : min(start + 128, D)].astype(F32).T
        cut = min(max(D // 2 - start, 0), turned.shape[0])
        if cut > 0:
            top[start : start + cut, :] = turned[:cut]
        if cut < turned.shape[0]:
            at = start + cut - D // 2
            bottom[at : at + turned.shape[0] - cut, :] = turned[cut:]


def join_kernel(*refs):
    out = refs[-1]
    for index, half in enumerate(refs[:-1]):
        slot, rows = index // 2, index % 2 * (D // 2)
        at = slice(slot * TOKENS, (slot + 1) * TOKENS)
        out[rows : rows + D // 2, at] = half[...].astype(BF16)


def weight_grad_kernel(normalizer, core, tokens, own, first, second, third, kept, sent, columns):
    for slot, block in enumerate((own, first, second, third)):
        columns[slot * TOKENS : (slot + 1) * TOKENS, :] = block[...].astype(BF16)
    right = columns[...]
    span = PLANE_SIZE // CORES
    for out, which in ((sent, 1 - core[0]), (kept, core[0])):
        for half in range(CORES):
            start = pl.multiple_of((half * CORES + which) * (span * ROWS), 16)
            product = dot(tokens[pl.ds(start, span * ROWS), :], right, 1, 0) * normalizer
            for index in range(span):
                out[half * span + index, :ROWS, :] = product[index * ROWS : (index + 1) * ROWS]


def first_stage_kernel(spot, kept, got, *outs):
    for slot in range(RING):
        across = lax.rem(spot[0] + slot, RING)
        for other in range(RING):
            at = (other // 2) * (2 * RING) + across * 2 + other % 2
            outs[slot][other] = kept[at, :SPLIT, :] + got[at, :SPLIT, :]
            at = (slot // 2) * (2 * RING) + other * 2 + slot % 2
            outs[RING][slot, other] = kept[at, SPLIT:, :] + got[at, SPLIT:, :]


def second_stage_kernel(spot, *refs):
    uppers, lowers, outs = refs[:RING], refs[RING], refs[RING + 1 :]
    for slot in range(RING):
        outs[RING][slot] = sum_at(uppers, slot)
        across = lax.rem(spot[0] + slot, RING)
        outs[slot][...] = (lowers[0, across] + lowers[1, across]) + (
            lowers[2, across] + lowers[3, across]
        )


def sum_at(refs, at):
    return (refs[0][at] + refs[1][at]) + (refs[2][at] + refs[3][at])


def last_kernel(query, *refs):
    lowers, uppers, query_out, key_out, value_out = refs[:RING], *refs[RING:]
    total = query[0]
    for index in range(1, PLANE_SIZE):
        total = total + query[index]
    query_out[:, :EARLY] = total[:ROWS]
    upper = (uppers[0] + uppers[1]) + (uppers[2] + uppers[3])
    lower = (lowers[0][...] + lowers[1][...]) + (lowers[2][...] + lowers[3][...])
    for total, rows, size in ((upper, 0, SPLIT), (lower, SPLIT, ROWS - SPLIT)):
        key_out[rows : rows + size, :] = total[:size, :COLS]
        value_out[rows : rows + size, :] = total[:size, COLS : 2 * COLS]
        query_out[rows : rows + size, EARLY:] = total[:size, 2 * COLS :]


def exchange(blocks, axes):
    return lax.all_to_all(blocks, axes, 0, 0, tiled=True)


def shift(values, by, axis):
    return lax.ppermute(values, axis, [(i, (i + by) % RING) for i in range(RING)])


def shifted(slots, axis):
    return [slots[0]] + [shift(slots[s], s, axis) for s in range(1, RING)]


def swap_cores(values):
    return lax.ppermute(values, "core", [(0, 1), (1, 0)])


def back_project(gradient, weight):
    return dot(gradient, weight, 1, 1)


def body(latent, query_weight, key_weight, value_weight, upstream_grad):
    image_tokens = TOKENS * TILES
    loss_scale = 4.0 * math.sqrt(image_tokens)
    normalizer = 1.0 / math.sqrt(image_tokens * REPLICAS)
    tokens = latent.reshape(TOKENS, D)
    upstream = upstream_grad.reshape(TOKENS, HW)
    place = lax.axis_index("dp").reshape(1)
    core = lax.axis_index("core").reshape(1)
    spot = jnp.stack([lax.axis_index("x"), lax.axis_index(("zh", "zl"))])
    heads = shaped((HEADS, TOKENS, HD), BF16)
    flat = shaped((TOKENS, HW), BF16)
    state = pltpu.VMEM((HW, HD), F32)
    totals = pltpu.VMEM((HEADS, HD), F32)
    weight = pltpu.VMEM((D, HW), BF16)
    wide = pltpu.VMEM((TOKENS, HW), F32)
    blocks = pltpu.VMEM((REPLICAS, TOKENS, COLS), F32)

    key, value, sent = call(
        key_value_kernel,
        "key_value",
        [heads, heads, shaped((TILES, PART + HEADS, HD))],
        [BLOCK, IN_HBM, IN_HBM],
        [weight, weight, state, totals, pltpu.SemaphoreType.DMA((2 * len(CHUNKS),))],
        vmem=20,
    )(tokens, key_weight, value_weight)
    sent, later_tokens = lax.optimization_barrier((sent, tokens))
    half = shaped((D // 2, TOKENS))
    top, bottom = call(turn_kernel, "turn", [half, half], [BLOCK])(later_tokens)
    left_top = shift(top, 1, "dp")
    right_bottom = shift(bottom, 3, "dp")
    got = exchange(sent, IMAGE)
    (query,) = call(
        query_kernel,
        "query",
        [heads],
        [BLOCK, BLOCK],
    )(tokens, query_weight)
    sent, numer, total = call(
        lambda *refs: numerator_kernel(loss_scale, *refs),
        "numerator",
        [shaped((TILES, 2 * PART, HD)), heads, shaped((HEADS, HD))],
        [BLOCK] * 3,
        [state],
        arrived=(0,),
    )(got, query, upstream)
    sent, left_top, right_bottom, later_top, later_bottom = lax.optimization_barrier(
        (sent, left_top, right_bottom, top, bottom)
    )
    far_top = shift(left_top, 1, "dp")
    far_bottom = shift(right_bottom, 3, "dp")
    left_bottom = shift(later_bottom, 1, "dp")
    right_top = shift(later_top, 3, "dp")
    got_state = exchange(sent, IMAGE)
    sent, grad_denom = call(
        lambda *refs: total_grad_kernel(loss_scale, *refs),
        "total_grad",
        [shaped((TILES, PART + HEADS, HD)), shaped((TOKENS, HEADS))],
        [BLOCK] * 4,
        [state, totals],
        arrived=(0,),
    )(got_state, query, upstream, total)
    sent, far_top, far_bottom, left_bottom, right_top = lax.optimization_barrier(
        (sent, far_top, far_bottom, left_bottom, right_top)
    )
    got = exchange(sent, IMAGE)

    block = shaped((TOKENS, EARLY))
    grad_query, *query_columns, late = call(
        query_grad_kernel,
        "query_grad",
        [flat, block, block, block, block, shaped((REPLICAS, TOKENS, LATE))],
        [IN_SMEM] + [BLOCK] * 5,
        [state, wide, blocks],
        arrived=(1,),
    )(place, got_state, query, numer, total, grad_denom)
    query_columns = shifted(query_columns, "dp")
    (all_tokens,) = call(
        join_kernel, "join", [shaped((D, REPLICAS * TOKENS), BF16)], [BLOCK] * 8, arrived=(2, 3, 4, 5, 6, 7)
    )(top, bottom, left_top, left_bottom, far_top, far_bottom, right_top, right_bottom)
    def partial_products(columns):
        width = columns[0].shape[1]
        half = shaped((PLANE_SIZE, PADDED_ROWS, width))
        return call(
            lambda *refs: weight_grad_kernel(normalizer, *refs),
            "weight_grad",
            [half, half],
            [IN_SMEM] + [BLOCK] * 5,
            [pltpu.VMEM((REPLICAS * TOKENS, width), BF16)],
            vmem=24,
            arrived=(3, 4, 5),
        )(core, all_tokens, *columns)

    query_kept, query_given = partial_products(query_columns)
    got, query_kept, query_given = lax.optimization_barrier((got, query_kept, query_given))

    block = shaped((TOKENS, WIDE))
    grad_key, grad_value, *key_value_columns = call(
        key_value_grad_kernel,
        "key_value_grad",
        [flat, flat, block, block, block, block],
        [IN_SMEM] + [BLOCK] * 4,
        [state, wide, wide, blocks],
        arrived=(1,),
    )(place, got, key, value, late)
    key_value_columns, query_given = lax.optimization_barrier((key_value_columns, query_given))
    key_value_columns = shifted(key_value_columns, "dp")

    query_out = exchange(query_kept + swap_cores(query_given), PLANE)
    query_out, key_value_columns = lax.optimization_barrier((query_out, key_value_columns))

    kept, given = partial_products(key_value_columns)
    got = swap_cores(given)
    rest = PADDED_ROWS - SPLIT
    *uppers, lowers = call(
        first_stage_kernel,
        "first_stage",
        [shaped((RING, SPLIT, WIDE))] * RING + [shaped((RING, RING, rest, WIDE))],
        [IN_SMEM, BLOCK, BLOCK],
        vmem=24,
        arrived=(2,),
    )(spot, kept, got)
    lowers = exchange(lowers, ("zh", "zl"))
    uppers = shifted(uppers, "x")
    *lowers, uppers = call(
        second_stage_kernel,
        "second_stage",
        [shaped((rest, WIDE))] * RING + [shaped((RING, SPLIT, WIDE))],
        [IN_SMEM] + [BLOCK] * (RING + 1),
        arrived=(2, 3, 4, 5),
    )(spot, *uppers, lowers)
    uppers = exchange(uppers, ("zh", "zl"))
    lowers = shifted(lowers, "x")
    block = shaped((ROWS, COLS))
    query_out, key_out, value_out = call(
        last_kernel, "last", [block] * 3, [BLOCK] * (RING + 2), arrived=(0, 2, 3, 4, 5)
    )(query_out, *lowers, uppers)

    summed = back_project(grad_query, query_weight) + back_project(grad_key, key_weight)
    summed = summed + back_project(grad_value, value_weight)
    latent_grad = summed.astype(BF16).reshape(latent.shape)
    return latent_grad, query_out, key_out, value_out


def solution(mesh):
    devices = mesh.devices
    fine = Mesh(
        devices.reshape(REPLICAS, 2, CORES, 4, 2), ("dp", "zh", "core", "x", "zl")
    )
    grid = P("dp", ("zh", "core"), ("x", "zl"), None)
    weight_out = P(("zh", "core", "x", "zl"), "dp")
    return jax.shard_map(
        body,
        mesh=fine,
        in_specs=(grid, P(), P(), P(), grid),
        out_specs=(grid, weight_out, weight_out, weight_out),
        check_vma=False,
    )
```

```python
import math

import jax
import jax.numpy as jnp
from jax import lax
from jax.experimental import pallas as pl
from jax.experimental.pallas import tpu as pltpu
from jax.sharding import Mesh, PartitionSpec as P

D = 2240
HD = 112
HEADS = 10
HW = HEADS * HD
TILES = 32
PART = HW // TILES
PLANE_SIZE = 16
CORES = 2
ROWS = D // TILES
PADDED_ROWS = 72
REPLICAS = 4
RING = 4
COLS = HW // REPLICAS
EARLY = 256
LATE = COLS - EARLY
WIDE = 2 * COLS + LATE
TOKENS = 128

EPSILON = 1e-15
IMAGE = ("zh", "core", "x", "zl")
PLANE = ("zh", "x", "zl")
CHUNKS = [(start, min(384, D - start)) for start in range(0, D, 384)]

F32 = jnp.float32
BF16 = jnp.bfloat16
BLOCK = pl.BlockSpec()
IN_SMEM = pl.BlockSpec(memory_space=pltpu.SMEM)
ANYWHERE = pl.BlockSpec(memory_space=pl.ANY)
IN_HBM = pl.BlockSpec(memory_space=pltpu.HBM)


def shaped(shape, dtype=F32):
    return pltpu.HBM(shape, dtype)


def call(kernel, name, outs, in_specs, scratch=(), vmem=12, arrived=()):
    run = pl.pallas_call(
        kernel,
        name=name,
        grid=(1,),
        out_shape=outs,
        in_specs=in_specs,
        out_specs=[BLOCK] * len(outs),
        scratch_shapes=list(scratch),
        compiler_params=pltpu.CompilerParams(vmem_limit_bytes=vmem * 1024 * 1024),
    )

    def with_placed(*operands):
        placed = [
            operand
            if spec is IN_SMEM or index in arrived
            else pltpu.with_memory_space_constraint(operand, pltpu.HBM)
            for index, (operand, spec) in enumerate(zip(operands, in_specs))
        ]
        return run(*placed)

    return with_placed


def dot(left, right, left_dim, right_dim):
    return lax.dot_general(
        left, right, (((left_dim,), (right_dim,)), ((), ())), preferred_element_type=F32
    )


def split_dot(left, right, left_dim, right_dim):
    high = right.astype(BF16)
    low = (right - high.astype(F32)).astype(BF16)
    return dot(left, high, left_dim, right_dim) + dot(left, low, left_dim, right_dim)


def relu(values):
    return jnp.maximum(values, jnp.zeros_like(values))


def weight_copies(weight, buffer, semaphores, first):
    copies = []
    for index, (start, size) in enumerate(CHUNKS):
        copies.append(
            pltpu.make_async_copy(
                weight.at[pl.ds(start, size)],
                buffer.at[pl.ds(start, size)],
                semaphores.at[first + index],
            )
        )
    return copies


def project(tokens, buffer, copies):
    total = None
    for (start, size), copy in zip(CHUNKS, copies):
        copy.wait()
        term = dot(tokens[:, start : start + size], buffer[start : start + size, :], 1, 0)
        total = term if total is None else total + term
    return total.astype(BF16)


def store_parts(sent, at, state):
    for tile in range(TILES):
        sent[tile, at : at + PART, :] = state[tile * PART : (tile + 1) * PART, :]


def load_parts(state, got):
    for tile in range(TILES):
        state[tile * PART : (tile + 1) * PART, :] = got[tile, :PART, :]


def head(ref, index):
    return ref[index * HD : (index + 1) * HD, :]


def key_value_kernel(
    tokens, key_weight, value_weight, key, value, sent, key_buffer, value_buffer, state, total, semaphores
):
    value_copies = weight_copies(value_weight, value_buffer, semaphores, 0)
    key_copies = weight_copies(key_weight, key_buffer, semaphores, len(CHUNKS))
    for copy in value_copies + key_copies:
        copy.start()
    rows = tokens[...]
    value_rows = project(rows, value_buffer, value_copies)
    key_rows = project(rows, key_buffer, key_copies)
    for index in range(HEADS):
        part = slice(index * HD, (index + 1) * HD)
        key_head = key_rows[:, part]
        value_head = value_rows[:, part]
        key[index] = key_head
        value[index] = value_head
        positive = relu(key_head)
        state[index * HD : (index + 1) * HD, :] = dot(positive, value_head, 0, 0)
        total[index : index + 1, :] = jnp.sum(positive.astype(F32), axis=0, keepdims=True)
    store_parts(sent, 0, state)
    totals = total[...]
    for tile in range(TILES):
        sent[tile, PART : PART + HEADS, :] = totals


def query_kernel(tokens, weight, query):
    query_rows = dot(tokens[...], weight[...], 1, 0).astype(BF16)
    for index in range(HEADS):
        query[index] = query_rows[:, index * HD : (index + 1) * HD]


def inverse_denominator(positive, total):
    return 1.0 / (jnp.sum(positive * total, axis=1, keepdims=True) + EPSILON)


def numerator_kernel(loss_scale, got, query, upstream, sent, numer, total, state):
    sums = got[0]
    for tile in range(1, TILES):
        sums = sums + got[tile]
    state_part = sums[:PART]
    totals = sums[PART : PART + HEADS]
    total[...] = totals
    for index in range(HEADS):
        part = slice(index * HD, (index + 1) * HD)
        positive = relu(query[index])
        inverse = inverse_denominator(positive.astype(F32), totals[index : index + 1])
        cotangent = upstream[:, part].astype(F32) * loss_scale
        numer_low = (cotangent * inverse).astype(BF16)
        numer[index] = numer_low
        state[index * HD : (index + 1) * HD, :] = dot(positive, numer_low, 0, 0)
    for tile in range(TILES):
        sent[tile, :PART, :] = state_part
    store_parts(sent, PART, state)


def total_grad_kernel(loss_scale, got, query, upstream, total, sent, grad_denom, state, totals):
    load_parts(state, got)
    for index in range(HEADS):
        part = slice(index * HD, (index + 1) * HD)
        positive = relu(query[index])
        wide = positive.astype(F32)
        inverse = inverse_denominator(wide, total[index : index + 1, :])
        cotangent = upstream[:, part].astype(F32) * loss_scale
        product = split_dot(positive, head(state, index), 1, 0)
        grad = -(jnp.sum(cotangent * product, axis=1, keepdims=True) * inverse) * inverse
        grad_denom[:, index : index + 1] = grad
        totals[index : index + 1, :] = jnp.sum(wide * grad, axis=0, keepdims=True)
    part_sum = got[0, PART:, :]
    for tile in range(1, TILES):
        part_sum = part_sum + got[tile, PART:, :]
    values = totals[...]
    for tile in range(TILES):
        sent[tile, :PART, :] = part_sum
        sent[tile, PART : PART + HEADS, :] = values


def place_columns(place, blocks, outs, at, first=0, last=COLS):
    for slot, out in enumerate(outs):
        block = blocks[lax.rem(place[0] + slot, REPLICAS)]
        out[:, at : at + last - first] = block[:, first:last]


def split_columns(flat, blocks):
    for block in range(REPLICAS):
        blocks[block] = flat[:, block * COLS : (block + 1) * COLS]


def query_grad_kernel(
    place, got, query, numer, total, grad_denom, grad, own, first, second, third, late, state, flat, blocks
):
    load_parts(state, got)
    for index in range(HEADS):
        part = slice(index * HD, (index + 1) * HD)
        values = split_dot(numer[index], head(state, index), 1, 1)
        values = values + grad_denom[:, index : index + 1] * total[index : index + 1, :]
        values = jnp.where(query[index].astype(F32) > 0, values, 0.0).astype(BF16)
        grad[:, part] = values
        flat[:, part] = values.astype(F32)
    split_columns(flat, blocks)
    place_columns(place, blocks, (own, first, second, third), 0, 0, EARLY)
    for slot in range(REPLICAS):
        late[slot] = blocks[lax.rem(place[0] + slot, REPLICAS)][:, EARLY:]


def key_value_grad_kernel(
    place, got, key, value, late, grad_key, grad_value, own, first, second, third, state, flat_key, flat_value, blocks
):
    load_parts(state, got)
    totals = got[0, PART : PART + HEADS, :]
    for tile in range(1, TILES):
        totals = totals + got[tile, PART : PART + HEADS, :]
    for index in range(HEADS):
        part = slice(index * HD, (index + 1) * HD)
        key_head = key[index]
        positive = relu(key_head)
        state_head = head(state, index)
        values = split_dot(positive, state_head, 1, 0).astype(BF16)
        grad_value[:, part] = values
        flat_value[:, part] = values.astype(F32)
        values = split_dot(value[index], state_head, 1, 1) + totals[index : index + 1]
        values = jnp.where(key_head.astype(F32) > 0, values, 0.0).astype(BF16)
        grad_key[:, part] = values
        flat_key[:, part] = values.astype(F32)
    outs = (own, first, second, third)
    split_columns(flat_key, blocks)
    place_columns(place, blocks, outs, 0)
    split_columns(flat_value, blocks)
    place_columns(place, blocks, outs, COLS)
    for slot, out in enumerate(outs):
        out[:, 2 * COLS :] = late[slot]


def turn_kernel(tokens, top, bottom):
    for start in range(0, D, 128):
        turned = tokens[:, start : min(start + 128, D)].astype(F32).T
        cut = min(max(D // 2 - start, 0), turned.shape[0])
        if cut > 0:
            top[start : start + cut, :] = turned[:cut]
        if cut < turned.shape[0]:
            at = start + cut - D // 2
            bottom[at : at + turned.shape[0] - cut, :] = turned[cut:]


def join_kernel(*refs):
    out = refs[-1]
    for index, half in enumerate(refs[:-1]):
        slot, rows = index // 2, index % 2 * (D // 2)
        at = slice(slot * TOKENS, (slot + 1) * TOKENS)
        out[rows : rows + D // 2, at] = half[...].astype(BF16)


def weight_grad_kernel(normalizer, core, tokens, own, first, second, third, after, kept, sent, columns):
    for slot, block in enumerate((own, first, second, third)):
        columns[slot * TOKENS : (slot + 1) * TOKENS, :] = block[...].astype(BF16)
    right = columns[...]
    span = PLANE_SIZE // CORES
    for out, which in ((sent, 1 - core[0]), (kept, core[0])):
        for half in range(CORES):
            start = pl.multiple_of((half * CORES + which) * (span * ROWS), 16)
            product = dot(tokens[pl.ds(start, span * ROWS), :], right, 1, 0) * normalizer
            for index in range(span):
                out[half * span + index, :ROWS, :] = product[index * ROWS : (index + 1) * ROWS]


def first_stage_kernel(spot, kept, got, after, *outs):
    for slot, out in enumerate(outs):
        across = lax.rem(spot[0] + slot, RING)
        for other in range(RING):
            at = (other // 2) * (2 * RING) + across * 2 + other % 2
            out[other] = kept[at] + got[at]


def second_stage_kernel(spot, own, first, second, third, *outs):
    for slot, out in enumerate(outs):
        along = lax.rem(spot[1] + slot, RING)
        out[...] = (own[along] + first[along]) + (second[along] + third[along])


def last_kernel(key_value, own, first, second, third, query_out, key_out, value_out):
    total = key_value[0]
    for index in range(1, PLANE_SIZE):
        total = total + key_value[index]
    key_out[...] = total[:ROWS, :COLS]
    value_out[...] = total[:ROWS, COLS : 2 * COLS]
    query_out[:, EARLY:] = total[:ROWS, 2 * COLS :]
    total = (own[...] + first[...]) + (second[...] + third[...])
    query_out[:, :EARLY] = total[:ROWS]


def exchange(blocks, axes):
    return lax.all_to_all(blocks, axes, 0, 0, tiled=True)


def shift(values, by, axis):
    return lax.ppermute(values, axis, [(i, (i + by) % RING) for i in range(RING)])


def shifted(slots, axis):
    return [slots[0]] + [shift(slots[s], s, axis) for s in range(1, RING)]


def swap_cores(values):
    return lax.ppermute(values, "core", [(0, 1), (1, 0)])


def back_project(gradient, weight):
    return dot(gradient, weight, 1, 1)


def body(latent, query_weight, key_weight, value_weight, upstream_grad):
    image_tokens = TOKENS * TILES
    loss_scale = 4.0 * math.sqrt(image_tokens)
    normalizer = 1.0 / math.sqrt(image_tokens * REPLICAS)
    tokens = latent.reshape(TOKENS, D)
    upstream = upstream_grad.reshape(TOKENS, HW)
    place = lax.axis_index("dp").reshape(1)
    core = lax.axis_index("core").reshape(1)
    spot = jnp.stack([lax.axis_index("x"), lax.axis_index(("zh", "zl"))])
    heads = shaped((HEADS, TOKENS, HD), BF16)
    flat = shaped((TOKENS, HW), BF16)
    state = pltpu.VMEM((HW, HD), F32)
    totals = pltpu.VMEM((HEADS, HD), F32)
    weight = pltpu.VMEM((D, HW), BF16)
    wide = pltpu.VMEM((TOKENS, HW), F32)
    blocks = pltpu.VMEM((REPLICAS, TOKENS, COLS), F32)

    key, value, sent = call(
        key_value_kernel,
        "key_value",
        [heads, heads, shaped((TILES, PART + HEADS, HD))],
        [BLOCK, IN_HBM, IN_HBM],
        [weight, weight, state, totals, pltpu.SemaphoreType.DMA((2 * len(CHUNKS),))],
        vmem=20,
    )(tokens, key_weight, value_weight)
    sent, later_tokens = lax.optimization_barrier((sent, tokens))
    half = shaped((D // 2, TOKENS))
    top, bottom = call(turn_kernel, "turn", [half, half], [BLOCK])(later_tokens)
    left_top = shift(top, 1, "dp")
    right_bottom = shift(bottom, 3, "dp")
    got = exchange(sent, IMAGE)
    (query,) = call(
        query_kernel,
        "query",
        [heads],
        [BLOCK, BLOCK],
    )(tokens, query_weight)
    sent, numer, total = call(
        lambda *refs: numerator_kernel(loss_scale, *refs),
        "numerator",
        [shaped((TILES, 2 * PART, HD)), heads, shaped((HEADS, HD))],
        [BLOCK] * 3,
        [state],
        arrived=(0, 1, 2),
    )(got, query, upstream)
    sent, left_top, right_bottom, later_top, later_bottom = lax.optimization_barrier(
        (sent, left_top, right_bottom, top, bottom)
    )
    far_top = shift(left_top, 1, "dp")
    far_bottom = shift(right_bottom, 3, "dp")
    left_bottom = shift(later_bottom, 1, "dp")
    right_top = shift(later_top, 3, "dp")
    got_state = exchange(sent, IMAGE)
    sent, grad_denom = call(
        lambda *refs: total_grad_kernel(loss_scale, *refs),
        "total_grad",
        [shaped((TILES, PART + HEADS, HD)), shaped((TOKENS, HEADS))],
        [BLOCK] * 4,
        [state, totals],
        arrived=(0, 1, 2, 3),
    )(got_state, query, upstream, total)
    sent, far_top, far_bottom, left_bottom, right_top = lax.optimization_barrier(
        (sent, far_top, far_bottom, left_bottom, right_top)
    )
    got = exchange(sent, IMAGE)

    block = shaped((TOKENS, EARLY))
    grad_query, *query_columns, late = call(
        query_grad_kernel,
        "query_grad",
        [flat, block, block, block, block, shaped((REPLICAS, TOKENS, LATE))],
        [IN_SMEM] + [BLOCK] * 5,
        [state, wide, blocks],
        arrived=(1,),
    )(place, got_state, query, numer, total, grad_denom)
    query_columns = shifted(query_columns, "dp")
    (all_tokens,) = call(
        join_kernel, "join", [shaped((D, REPLICAS * TOKENS), BF16)], [BLOCK] * 8, arrived=(2, 3, 4, 5, 6, 7)
    )(top, bottom, left_top, left_bottom, far_top, far_bottom, right_top, right_bottom)
    def partial_products(all_tokens, columns, after):
        width = columns[0].shape[1]
        half = shaped((PLANE_SIZE, PADDED_ROWS, width))
        return call(
            lambda *refs: weight_grad_kernel(normalizer, *refs),
            "weight_grad",
            [half, half],
            [IN_SMEM] + [BLOCK] * 5 + [ANYWHERE],
            [pltpu.VMEM((REPLICAS * TOKENS, width), BF16)],
            vmem=24,
            arrived=(3, 4, 5, 6),
        )(core, all_tokens, *columns, after)

    got, all_tokens, query_columns = lax.optimization_barrier((got, all_tokens, query_columns))

    block = shaped((TOKENS, WIDE))
    grad_key, grad_value, *key_value_columns = call(
        key_value_grad_kernel,
        "key_value_grad",
        [flat, flat, block, block, block, block],
        [IN_SMEM] + [BLOCK] * 4,
        [state, wide, wide, blocks],
        arrived=(1, 2, 3, 4),
    )(place, got, key, value, late)
    key_value_columns = shifted(key_value_columns, "dp")

    query_kept, query_given = partial_products(all_tokens, query_columns, key_value_columns[1])
    query_got = swap_cores(query_given)
    kept, given = partial_products(all_tokens, key_value_columns, place)
    got = swap_cores(given)
    slots = call(
        first_stage_kernel,
        "first_stage",
        [shaped((RING, PADDED_ROWS, EARLY))] * RING,
        [IN_SMEM, BLOCK, BLOCK, ANYWHERE],
        arrived=(2, 3),
    )(spot, query_kept, query_got, given)
    key_value_out = exchange(kept + got, PLANE)
    slots = call(
        second_stage_kernel,
        "second_stage",
        [shaped((PADDED_ROWS, EARLY))] * RING,
        [IN_SMEM] + [BLOCK] * RING,
        arrived=(2, 3, 4),
    )(spot, *shifted(slots, "x"))
    slots = shifted(slots, ("zh", "zl"))
    block = shaped((ROWS, COLS))
    query_out, key_out, value_out = call(
        last_kernel, "last", [block] * 3, [BLOCK] * 5, arrived=(0, 2, 3, 4)
    )(key_value_out, *slots)

    summed = back_project(grad_query, query_weight) + back_project(grad_key, key_weight)
    summed = summed + back_project(grad_value, value_weight)
    latent_grad = summed.astype(BF16).reshape(latent.shape)
    return latent_grad, query_out, key_out, value_out


def solution(mesh):
    devices = mesh.devices
    fine = Mesh(
        devices.reshape(REPLICAS, 2, CORES, 4, 2), ("dp", "zh", "core", "x", "zl")
    )
    grid = P("dp", ("zh", "core"), ("x", "zl"), None)
    weight_out = P(("zh", "core", "x", "zl"), "dp")
    return jax.shard_map(
        body,
        mesh=fine,
        in_specs=(grid, P(), P(), P(), grid),
        out_specs=(grid, weight_out, weight_out, weight_out),
        check_vma=False,
    )
```

```python
import math

import jax
import jax.numpy as jnp
from jax import lax
from jax.experimental import pallas as pl
from jax.experimental.pallas import tpu as pltpu
from jax.sharding import Mesh, PartitionSpec as P

D = 2240
HD = 112
HEADS = 10
HW = HEADS * HD
TILES = 32
PART = HW // TILES
PLANE_SIZE = 16
CORES = 2
ROWS = D // TILES
PADDED_ROWS = 72
HALF = D // 4
REPLICAS = 4
RING = 4
COLS = HW // REPLICAS
EARLY = 256
LATE = COLS - EARLY
WIDE = 2 * COLS + LATE
TOKENS = 128

EPSILON = 1e-15
IMAGE = ("zh", "core", "x", "zl")
PLANE = ("zh", "x", "zl")
CHUNKS = [(start, min(384, D - start)) for start in range(0, D, 384)]

F32 = jnp.float32
BF16 = jnp.bfloat16
BLOCK = pl.BlockSpec()
IN_SMEM = pl.BlockSpec(memory_space=pltpu.SMEM)
ANYWHERE = pl.BlockSpec(memory_space=pl.ANY)
IN_HBM = pl.BlockSpec(memory_space=pltpu.HBM)


def shaped(shape, dtype=F32):
    return pltpu.HBM(shape, dtype)


def call(kernel, name, outs, in_specs, scratch=(), vmem=12, arrived=()):
    run = pl.pallas_call(
        kernel,
        name=name,
        grid=(1,),
        out_shape=outs,
        in_specs=in_specs,
        out_specs=[BLOCK] * len(outs),
        scratch_shapes=list(scratch),
        compiler_params=pltpu.CompilerParams(vmem_limit_bytes=vmem * 1024 * 1024),
    )

    def with_placed(*operands):
        placed = [
            operand
            if spec is IN_SMEM or index in arrived
            else pltpu.with_memory_space_constraint(operand, pltpu.HBM)
            for index, (operand, spec) in enumerate(zip(operands, in_specs))
        ]
        return run(*placed)

    return with_placed


def dot(left, right, left_dim, right_dim):
    return lax.dot_general(
        left, right, (((left_dim,), (right_dim,)), ((), ())), preferred_element_type=F32
    )


def split_dot(left, right, left_dim, right_dim):
    high = right.astype(BF16)
    low = (right - high.astype(F32)).astype(BF16)
    return dot(left, high, left_dim, right_dim) + dot(left, low, left_dim, right_dim)


def relu(values):
    return jnp.maximum(values, jnp.zeros_like(values))


def weight_copies(weight, buffer, semaphores, first):
    copies = []
    for index, (start, size) in enumerate(CHUNKS):
        copies.append(
            pltpu.make_async_copy(
                weight.at[pl.ds(start, size)],
                buffer.at[pl.ds(start, size)],
                semaphores.at[first + index],
            )
        )
    return copies


def project(tokens, buffer, copies):
    total = None
    for (start, size), copy in zip(CHUNKS, copies):
        copy.wait()
        term = dot(tokens[:, start : start + size], buffer[start : start + size, :], 1, 0)
        total = term if total is None else total + term
    return total.astype(BF16)


def store_parts(sent, at, state):
    for tile in range(TILES):
        sent[tile, at : at + PART, :] = state[tile * PART : (tile + 1) * PART, :]


def load_parts(state, got):
    for tile in range(TILES):
        state[tile * PART : (tile + 1) * PART, :] = got[tile, :PART, :]


def head(ref, index):
    return ref[index * HD : (index + 1) * HD, :]


def key_value_kernel(
    tokens, key_weight, value_weight, key, value, sent, key_buffer, value_buffer, state, total, semaphores
):
    value_copies = weight_copies(value_weight, value_buffer, semaphores, 0)
    key_copies = weight_copies(key_weight, key_buffer, semaphores, len(CHUNKS))
    for copy in value_copies + key_copies:
        copy.start()
    rows = tokens[...]
    value_rows = project(rows, value_buffer, value_copies)
    key_rows = project(rows, key_buffer, key_copies)
    for index in range(HEADS):
        part = slice(index * HD, (index + 1) * HD)
        key_head = key_rows[:, part]
        value_head = value_rows[:, part]
        key[index] = key_head
        value[index] = value_head
        positive = relu(key_head)
        state[index * HD : (index + 1) * HD, :] = dot(positive, value_head, 0, 0)
        total[index : index + 1, :] = jnp.sum(positive.astype(F32), axis=0, keepdims=True)
    store_parts(sent, 0, state)
    totals = total[...]
    for tile in range(TILES):
        sent[tile, PART : PART + HEADS, :] = totals


def query_kernel(tokens, weight, query):
    query_rows = dot(tokens[...], weight[...], 1, 0).astype(BF16)
    for index in range(HEADS):
        query[index] = query_rows[:, index * HD : (index + 1) * HD]


def inverse_denominator(positive, total):
    return 1.0 / (jnp.sum(positive * total, axis=1, keepdims=True) + EPSILON)


def numerator_kernel(loss_scale, got, query, upstream, sent, numer, total, state):
    sums = got[0]
    for tile in range(1, TILES):
        sums = sums + got[tile]
    state_part = sums[:PART]
    totals = sums[PART : PART + HEADS]
    total[...] = totals
    for index in range(HEADS):
        part = slice(index * HD, (index + 1) * HD)
        positive = relu(query[index])
        inverse = inverse_denominator(positive.astype(F32), totals[index : index + 1])
        cotangent = upstream[:, part].astype(F32) * loss_scale
        numer_low = (cotangent * inverse).astype(BF16)
        numer[index] = numer_low
        state[index * HD : (index + 1) * HD, :] = dot(positive, numer_low, 0, 0)
    for tile in range(TILES):
        sent[tile, :PART, :] = state_part
    store_parts(sent, PART, state)


def total_grad_kernel(loss_scale, got, query, upstream, total, sent, grad_denom, state, totals):
    load_parts(state, got)
    for index in range(HEADS):
        part = slice(index * HD, (index + 1) * HD)
        positive = relu(query[index])
        wide = positive.astype(F32)
        inverse = inverse_denominator(wide, total[index : index + 1, :])
        cotangent = upstream[:, part].astype(F32) * loss_scale
        product = split_dot(positive, head(state, index), 1, 0)
        grad = -(jnp.sum(cotangent * product, axis=1, keepdims=True) * inverse) * inverse
        grad_denom[:, index : index + 1] = grad
        totals[index : index + 1, :] = jnp.sum(wide * grad, axis=0, keepdims=True)
    part_sum = got[0, PART:, :]
    for tile in range(1, TILES):
        part_sum = part_sum + got[tile, PART:, :]
    values = totals[...]
    for tile in range(TILES):
        sent[tile, :PART, :] = part_sum
        sent[tile, PART : PART + HEADS, :] = values


def place_columns(place, blocks, outs, at, first=0, last=COLS):
    for slot, out in enumerate(outs):
        block = blocks[lax.rem(place[0] + slot, REPLICAS)]
        out[:, at : at + last - first] = block[:, first:last]


def split_columns(flat, blocks):
    for block in range(REPLICAS):
        blocks[block] = flat[:, block * COLS : (block + 1) * COLS]


def query_grad_kernel(
    place, got, query, numer, total, grad_denom, grad, own, first, second, third, late, state, flat, blocks
):
    load_parts(state, got)
    for index in range(HEADS):
        part = slice(index * HD, (index + 1) * HD)
        values = split_dot(numer[index], head(state, index), 1, 1)
        values = values + grad_denom[:, index : index + 1] * total[index : index + 1, :]
        values = jnp.where(query[index].astype(F32) > 0, values, 0.0).astype(BF16)
        grad[:, part] = values
        flat[:, part] = values.astype(F32)
    split_columns(flat, blocks)
    place_columns(place, blocks, (own, first, second, third), 0, 0, EARLY)
    for slot in range(REPLICAS):
        late[slot] = blocks[lax.rem(place[0] + slot, REPLICAS)][:, EARLY:]


def key_value_grad_kernel(
    place, got, key, value, late, grad_key, grad_value, own, first, second, third, state, flat_key, flat_value, blocks
):
    load_parts(state, got)
    totals = got[0, PART : PART + HEADS, :]
    for tile in range(1, TILES):
        totals = totals + got[tile, PART : PART + HEADS, :]
    for index in range(HEADS):
        part = slice(index * HD, (index + 1) * HD)
        key_head = key[index]
        positive = relu(key_head)
        state_head = head(state, index)
        values = split_dot(positive, state_head, 1, 0).astype(BF16)
        grad_value[:, part] = values
        flat_value[:, part] = values.astype(F32)
        values = split_dot(value[index], state_head, 1, 1) + totals[index : index + 1]
        values = jnp.where(key_head.astype(F32) > 0, values, 0.0).astype(BF16)
        grad_key[:, part] = values
        flat_key[:, part] = values.astype(F32)
    outs = (own, first, second, third)
    split_columns(flat_key, blocks)
    place_columns(place, blocks, outs, 0)
    split_columns(flat_value, blocks)
    place_columns(place, blocks, outs, COLS)
    for slot, out in enumerate(outs):
        out[:, 2 * COLS :] = late[slot]


def turn_kernel(tokens, top, bottom):
    for start in range(0, D, 128):
        turned = tokens[:, start : min(start + 128, D)].astype(F32).T
        cut = min(max(D // 2 - start, 0), turned.shape[0])
        if cut > 0:
            top[start : start + cut, :] = turned[:cut]
        if cut < turned.shape[0]:
            at = start + cut - D // 2
            bottom[at : at + turned.shape[0] - cut, :] = turned[cut:]


def join_kernel(core, *refs):
    parts, kept, given = refs[:-2], refs[-2], refs[-1]
    mine = pl.multiple_of(core[0] * HALF, 16)
    other = pl.multiple_of((1 - core[0]) * HALF, 16)
    for index, part in enumerate(parts):
        slot, rows = index // 2, slice(index % 2 * HALF, (index % 2 + 1) * HALF)
        at = slice(slot * TOKENS, (slot + 1) * TOKENS)
        kept[rows, at] = part[pl.ds(mine, HALF), :].astype(BF16)
        given[rows, at] = part[pl.ds(other, HALF), :]


def fill_columns(columns, blocks):
    for index, block in enumerate(blocks):
        columns[index * TOKENS : (index + 1) * TOKENS, :] = block[...].astype(BF16)


def row_products(normalizer, kept, got, columns, rows):
    own = dot(kept[rows, :], columns[: REPLICAS * TOKENS, :], 1, 0)
    other = dot(got[rows, :].astype(BF16), columns[REPLICAS * TOKENS :, :], 1, 0)
    return (own + other) * normalizer


def query_product_kernel(normalizer, across, kept, got, *refs):
    blocks, outs, columns, product = refs[: 2 * REPLICAS], refs[2 * REPLICAS : -2], refs[-2], refs[-1]
    fill_columns(columns, blocks)
    span = PLANE_SIZE // CORES
    for half in range(CORES):
        values = row_products(normalizer, kept, got, columns, slice(half * HALF, (half + 1) * HALF))
        for index in range(span):
            product[half * span + index, :ROWS, :] = values[index * ROWS : (index + 1) * ROWS]
    for slot, out in enumerate(outs):
        at = lax.rem(across[0] + slot, RING)
        for other in range(RING):
            out[other] = product[(other // 2) * span + at * 2 + other % 2]


def key_value_product_kernel(normalizer, kept, got, *refs):
    blocks, out, columns = refs[: 2 * REPLICAS], refs[-2], refs[-1]
    fill_columns(columns, blocks)
    span = PLANE_SIZE // CORES
    for half in range(CORES):
        values = row_products(normalizer, kept, got, columns, slice(half * HALF, (half + 1) * HALF))
        for index in range(span):
            out[half * span + index, :ROWS, :] = values[index * ROWS : (index + 1) * ROWS]


def second_stage_kernel(along, own, first, second, third, *outs):
    for slot, out in enumerate(outs):
        at = lax.rem(along[0] + slot, RING)
        out[...] = (own[at] + first[at]) + (second[at] + third[at])


def last_kernel(key_value, own, first, second, third, query_out, key_out, value_out):
    total = key_value[0]
    for index in range(1, PLANE_SIZE):
        total = total + key_value[index]
    key_out[...] = total[:ROWS, :COLS]
    value_out[...] = total[:ROWS, COLS : 2 * COLS]
    query_out[:, EARLY:] = total[:ROWS, 2 * COLS :]
    total = (own[...] + first[...]) + (second[...] + third[...])
    query_out[:, :EARLY] = total[:ROWS]


def exchange(blocks, axes):
    return lax.all_to_all(blocks, axes, 0, 0, tiled=True)


def shift(values, by, axis):
    return lax.ppermute(values, axis, [(i, (i + by) % RING) for i in range(RING)])


def shifted(slots, axis):
    return [slots[0]] + [shift(slots[s], s, axis) for s in range(1, RING)]


def swap_cores(values):
    return lax.ppermute(values, "core", [(0, 1), (1, 0)])


def both_cores(blocks):
    return blocks + [swap_cores(block) for block in blocks]


def back_project(gradient, weight):
    return dot(gradient, weight, 1, 1)


def body(latent, query_weight, key_weight, value_weight, upstream_grad):
    image_tokens = TOKENS * TILES
    loss_scale = 4.0 * math.sqrt(image_tokens)
    normalizer = 1.0 / math.sqrt(image_tokens * REPLICAS)
    tokens = latent.reshape(TOKENS, D)
    upstream = upstream_grad.reshape(TOKENS, HW)
    place = lax.axis_index("dp").reshape(1)
    core = lax.axis_index("core").reshape(1)
    across = lax.axis_index("x").reshape(1)
    along = lax.axis_index(("zh", "zl")).reshape(1)
    heads = shaped((HEADS, TOKENS, HD), BF16)
    flat = shaped((TOKENS, HW), BF16)
    state = pltpu.VMEM((HW, HD), F32)
    totals = pltpu.VMEM((HEADS, HD), F32)
    weight = pltpu.VMEM((D, HW), BF16)
    wide = pltpu.VMEM((TOKENS, HW), F32)
    blocks = pltpu.VMEM((REPLICAS, TOKENS, COLS), F32)

    key, value, sent = call(
        key_value_kernel,
        "key_value",
        [heads, heads, shaped((TILES, PART + HEADS, HD))],
        [BLOCK, IN_HBM, IN_HBM],
        [weight, weight, state, totals, pltpu.SemaphoreType.DMA((2 * len(CHUNKS),))],
        vmem=20,
    )(tokens, key_weight, value_weight)
    sent, later_tokens = lax.optimization_barrier((sent, tokens))
    half = shaped((D // 2, TOKENS))
    top, bottom = call(turn_kernel, "turn", [half, half], [BLOCK])(later_tokens)
    left_top = shift(top, 1, "dp")
    right_bottom = shift(bottom, 3, "dp")
    got = exchange(sent, IMAGE)
    (query,) = call(
        query_kernel,
        "query",
        [heads],
        [BLOCK, BLOCK],
    )(tokens, query_weight)
    sent, numer, total = call(
        lambda *refs: numerator_kernel(loss_scale, *refs),
        "numerator",
        [shaped((TILES, 2 * PART, HD)), heads, shaped((HEADS, HD))],
        [BLOCK] * 3,
        [state],
        arrived=(0, 1, 2),
    )(got, query, upstream)
    sent, left_top, right_bottom, later_top, later_bottom = lax.optimization_barrier(
        (sent, left_top, right_bottom, top, bottom)
    )
    far_top = shift(left_top, 1, "dp")
    far_bottom = shift(right_bottom, 3, "dp")
    left_bottom = shift(later_bottom, 1, "dp")
    right_top = shift(later_top, 3, "dp")
    got_state = exchange(sent, IMAGE)
    sent, grad_denom = call(
        lambda *refs: total_grad_kernel(loss_scale, *refs),
        "total_grad",
        [shaped((TILES, PART + HEADS, HD)), shaped((TOKENS, HEADS))],
        [BLOCK] * 4,
        [state, totals],
        arrived=(0, 1, 2, 3),
    )(got_state, query, upstream, total)
    sent, far_top, far_bottom, left_bottom, right_top = lax.optimization_barrier(
        (sent, far_top, far_bottom, left_bottom, right_top)
    )
    got = exchange(sent, IMAGE)

    block = shaped((TOKENS, EARLY))
    grad_query, *query_columns, late = call(
        query_grad_kernel,
        "query_grad",
        [flat, block, block, block, block, shaped((REPLICAS, TOKENS, LATE))],
        [IN_SMEM] + [BLOCK] * 5,
        [state, wide, blocks],
        arrived=(1,),
    )(place, got_state, query, numer, total, grad_denom)
    query_columns = shifted(query_columns, "dp")
    half_rows = CORES * HALF
    kept_rows, given_rows = call(
        join_kernel,
        "join",
        [shaped((half_rows, REPLICAS * TOKENS), BF16), shaped((half_rows, REPLICAS * TOKENS))],
        [IN_SMEM] + [BLOCK] * 8,
        arrived=(3, 4, 5, 6, 7, 8),
    )(core, top, bottom, left_top, left_bottom, far_top, far_bottom, right_top, right_bottom)
    got_rows = swap_cores(given_rows)
    query_columns = both_cores(query_columns)
    got, kept_rows, got_rows, query_columns = lax.optimization_barrier(
        (got, kept_rows, got_rows, query_columns)
    )
    block = shaped((TOKENS, WIDE))
    grad_key, grad_value, *key_value_columns = call(
        key_value_grad_kernel,
        "key_value_grad",
        [flat, flat, block, block, block, block],
        [IN_SMEM] + [BLOCK] * 4,
        [state, wide, wide, blocks],
        arrived=(1, 2, 3, 4),
    )(place, got, key, value, late)
    slots = call(
        lambda *refs: query_product_kernel(normalizer, *refs),
        "query_product",
        [shaped((RING, PADDED_ROWS, EARLY))] * RING,
        [IN_SMEM] + [BLOCK] * (2 + 2 * REPLICAS),
        [
            pltpu.VMEM((2 * REPLICAS * TOKENS, EARLY), BF16),
            pltpu.VMEM((PLANE_SIZE, PADDED_ROWS, EARLY), F32),
        ],
        vmem=24,
        arrived=tuple(range(2, 11)),
    )(across, kept_rows, got_rows, *query_columns)
    slots = shifted(slots, "x")

    key_value_columns = both_cores(shifted(key_value_columns, "dp"))
    (product,) = call(
        lambda *refs: key_value_product_kernel(normalizer, *refs[:10], *refs[13:]),
        "key_value_product",
        [shaped((PLANE_SIZE, PADDED_ROWS, WIDE))],
        [BLOCK] * (2 + 2 * REPLICAS) + [ANYWHERE] * 3,
        [pltpu.VMEM((2 * REPLICAS * TOKENS, WIDE), BF16)],
        vmem=24,
        arrived=tuple(range(1, 13)),
    )(kept_rows, got_rows, *key_value_columns, *slots[1:])
    key_value_out = exchange(product, PLANE)
    slots = call(
        second_stage_kernel,
        "second_stage",
        [shaped((PADDED_ROWS, EARLY))] * RING,
        [IN_SMEM] + [BLOCK] * RING,
        arrived=(2, 3, 4),
    )(along, *slots)
    slots = shifted(slots, ("zh", "zl"))
    block = shaped((ROWS, COLS))
    query_out, key_out, value_out = call(
        last_kernel, "last", [block] * 3, [BLOCK] * 5, arrived=(0, 2, 3, 4)
    )(key_value_out, *slots)

    summed = back_project(grad_query, query_weight) + back_project(grad_key, key_weight)
    summed = summed + back_project(grad_value, value_weight)
    latent_grad = summed.astype(BF16).reshape(latent.shape)
    return latent_grad, query_out, key_out, value_out


def solution(mesh):
    devices = mesh.devices
    fine = Mesh(
        devices.reshape(REPLICAS, 2, CORES, 4, 2), ("dp", "zh", "core", "x", "zl")
    )
    grid = P("dp", ("zh", "core"), ("x", "zl"), None)
    weight_out = P(("zh", "core", "x", "zl"), "dp")
    return jax.shard_map(
        body,
        mesh=fine,
        in_specs=(grid, P(), P(), P(), grid),
        out_specs=(grid, weight_out, weight_out, weight_out),
        check_vma=False,
    )
```

```python
import math

import jax
import jax.numpy as jnp
from jax import lax
from jax.experimental import pallas as pl
from jax.experimental.pallas import tpu as pltpu
from jax.sharding import Mesh, PartitionSpec as P

D = 2240
HD = 112
HEADS = 10
HW = HEADS * HD
TILES = 32
PART = HW // TILES
PLANE_SIZE = 16
CORES = 2
ROWS = D // TILES
PADDED_ROWS = 72
HALF = D // 4
REPLICAS = 4
RING = 4
COLS = HW // REPLICAS
EARLY = 256
LATE = COLS - EARLY
WIDE = 2 * COLS + LATE
LANES = 640
TOKENS = 128

EPSILON = 1e-15
IMAGE = ("zh", "core", "x", "zl")
PLANE = ("zh", "x", "zl")
CHUNKS = [(start, min(384, D - start)) for start in range(0, D, 384)]

F32 = jnp.float32
BF16 = jnp.bfloat16
BLOCK = pl.BlockSpec()
IN_SMEM = pl.BlockSpec(memory_space=pltpu.SMEM)
ANYWHERE = pl.BlockSpec(memory_space=pl.ANY)
IN_HBM = pl.BlockSpec(memory_space=pltpu.HBM)


def shaped(shape, dtype=F32):
    return pltpu.HBM(shape, dtype)


def call(kernel, name, outs, in_specs, scratch=(), vmem=12, arrived=()):
    run = pl.pallas_call(
        kernel,
        name=name,
        grid=(1,),
        out_shape=outs,
        in_specs=in_specs,
        out_specs=[BLOCK] * len(outs),
        scratch_shapes=list(scratch),
        compiler_params=pltpu.CompilerParams(vmem_limit_bytes=vmem * 1024 * 1024),
    )

    def with_placed(*operands):
        placed = [
            operand
            if spec is IN_SMEM or index in arrived
            else pltpu.with_memory_space_constraint(operand, pltpu.HBM)
            for index, (operand, spec) in enumerate(zip(operands, in_specs))
        ]
        return run(*placed)

    return with_placed


def dot(left, right, left_dim, right_dim):
    return lax.dot_general(
        left, right, (((left_dim,), (right_dim,)), ((), ())), preferred_element_type=F32
    )


def split_dot(left, right, left_dim, right_dim):
    high = right.astype(BF16)
    low = (right - high.astype(F32)).astype(BF16)
    return dot(left, high, left_dim, right_dim) + dot(left, low, left_dim, right_dim)


def relu(values):
    return jnp.maximum(values, jnp.zeros_like(values))


def weight_copies(weight, buffer, semaphores, first):
    copies = []
    for index, (start, size) in enumerate(CHUNKS):
        copies.append(
            pltpu.make_async_copy(
                weight.at[pl.ds(start, size)],
                buffer.at[pl.ds(start, size)],
                semaphores.at[first + index],
            )
        )
    return copies


def project(tokens, buffer, copies):
    total = None
    for (start, size), copy in zip(CHUNKS, copies):
        copy.wait()
        term = dot(tokens[:, start : start + size], buffer[start : start + size, :], 1, 0)
        total = term if total is None else total + term
    return total.astype(BF16)


def store_parts(sent, at, state):
    for tile in range(TILES):
        sent[tile, at : at + PART, :] = state[tile * PART : (tile + 1) * PART, :]


def load_parts(state, got):
    for tile in range(TILES):
        state[tile * PART : (tile + 1) * PART, :] = got[tile, :PART, :]


def head(ref, index):
    return ref[index * HD : (index + 1) * HD, :]


def key_value_kernel(
    tokens, key_weight, value_weight, key, value, sent, key_buffer, value_buffer, state, total, semaphores
):
    value_copies = weight_copies(value_weight, value_buffer, semaphores, 0)
    key_copies = weight_copies(key_weight, key_buffer, semaphores, len(CHUNKS))
    for copy in value_copies + key_copies:
        copy.start()
    rows = tokens[...]
    value_rows = project(rows, value_buffer, value_copies)
    key_rows = project(rows, key_buffer, key_copies)
    for index in range(HEADS):
        part = slice(index * HD, (index + 1) * HD)
        key_head = key_rows[:, part]
        value_head = value_rows[:, part]
        key[index] = key_head
        value[index] = value_head
        positive = relu(key_head)
        state[index * HD : (index + 1) * HD, :] = dot(positive, value_head, 0, 0)
        total[index : index + 1, :] = jnp.sum(positive.astype(F32), axis=0, keepdims=True)
    store_parts(sent, 0, state)
    totals = total[...]
    for tile in range(TILES):
        sent[tile, PART : PART + HEADS, :] = totals


def query_kernel(tokens, weight, query):
    query_rows = dot(tokens[...], weight[...], 1, 0).astype(BF16)
    for index in range(HEADS):
        query[index] = query_rows[:, index * HD : (index + 1) * HD]


def inverse_denominator(positive, total):
    return 1.0 / (jnp.sum(positive * total, axis=1, keepdims=True) + EPSILON)


def numerator_kernel(loss_scale, got, query, upstream, sent, numer, total, state):
    sums = got[0]
    for tile in range(1, TILES):
        sums = sums + got[tile]
    state_part = sums[:PART]
    totals = sums[PART : PART + HEADS]
    total[...] = totals
    for index in range(HEADS):
        part = slice(index * HD, (index + 1) * HD)
        positive = relu(query[index])
        inverse = inverse_denominator(positive.astype(F32), totals[index : index + 1])
        cotangent = upstream[:, part].astype(F32) * loss_scale
        numer_low = (cotangent * inverse).astype(BF16)
        numer[index] = numer_low
        state[index * HD : (index + 1) * HD, :] = dot(positive, numer_low, 0, 0)
    for tile in range(TILES):
        sent[tile, :PART, :] = state_part
    store_parts(sent, PART, state)


def total_grad_kernel(loss_scale, got, query, upstream, total, sent, grad_denom, state, totals):
    load_parts(state, got)
    for index in range(HEADS):
        part = slice(index * HD, (index + 1) * HD)
        positive = relu(query[index])
        wide = positive.astype(F32)
        inverse = inverse_denominator(wide, total[index : index + 1, :])
        cotangent = upstream[:, part].astype(F32) * loss_scale
        product = split_dot(positive, head(state, index), 1, 0)
        grad = -(jnp.sum(cotangent * product, axis=1, keepdims=True) * inverse) * inverse
        grad_denom[:, index : index + 1] = grad
        totals[index : index + 1, :] = jnp.sum(wide * grad, axis=0, keepdims=True)
    part_sum = got[0, PART:, :]
    for tile in range(1, TILES):
        part_sum = part_sum + got[tile, PART:, :]
    values = totals[...]
    for tile in range(TILES):
        sent[tile, :PART, :] = part_sum
        sent[tile, PART : PART + HEADS, :] = values


def place_columns(place, blocks, outs, at, first=0, last=COLS):
    for slot, out in enumerate(outs):
        block = blocks[lax.rem(place[0] + slot, REPLICAS)]
        out[:, at : at + last - first] = block[:, first:last]


def split_columns(flat, blocks):
    for block in range(REPLICAS):
        blocks[block] = flat[:, block * COLS : (block + 1) * COLS]


def query_grad_kernel(
    place, got, query, numer, total, grad_denom, grad, own, first, second, third, late, state, flat, blocks
):
    load_parts(state, got)
    for index in range(HEADS):
        part = slice(index * HD, (index + 1) * HD)
        values = split_dot(numer[index], head(state, index), 1, 1)
        values = values + grad_denom[:, index : index + 1] * total[index : index + 1, :]
        values = jnp.where(query[index].astype(F32) > 0, values, 0.0).astype(BF16)
        grad[:, part] = values
        flat[:, part] = values.astype(F32)
    split_columns(flat, blocks)
    place_columns(place, blocks, (own, first, second, third), 0, 0, EARLY)
    for block in range(REPLICAS):
        late[block] = blocks[block][:, EARLY:]


def key_value_grad_kernel(got, key, value, late, grad_key, grad_value, sent, state, flat_key, flat_value):
    load_parts(state, got)
    totals = got[0, PART : PART + HEADS, :]
    for tile in range(1, TILES):
        totals = totals + got[tile, PART : PART + HEADS, :]
    for index in range(HEADS):
        part = slice(index * HD, (index + 1) * HD)
        key_head = key[index]
        positive = relu(key_head)
        state_head = head(state, index)
        values = split_dot(positive, state_head, 1, 0).astype(BF16)
        grad_value[:, part] = values
        flat_value[:, part] = values.astype(F32)
        values = split_dot(value[index], state_head, 1, 1) + totals[index : index + 1]
        values = jnp.where(key_head.astype(F32) > 0, values, 0.0).astype(BF16)
        grad_key[:, part] = values
        flat_key[:, part] = values.astype(F32)
    for block in range(REPLICAS):
        part = slice(block * COLS, (block + 1) * COLS)
        sent[block, :, :COLS] = flat_key[:, part]
        sent[block, :, COLS : 2 * COLS] = flat_value[:, part]
        sent[block, :, 2 * COLS : WIDE] = late[block]
        sent[block, :, WIDE:] = jnp.zeros((TOKENS, LANES - WIDE), F32)


def turn_kernel(core, tokens, mine, other, turned):
    for start in range(0, D, 128):
        size = min(128, D - start)
        turned[start : start + size, :] = tokens[:, start : start + size].astype(F32).T
    for half in range(CORES):
        rows = slice(half * HALF, (half + 1) * HALF)
        for out, which in ((mine, core[0]), (other, 1 - core[0])):
            start = pl.multiple_of((half * CORES + which) * HALF, 16)
            out[rows, :] = turned[pl.ds(start, HALF), :]


def join_kernel(*refs):
    for slot, part in enumerate(refs[:-1]):
        refs[-1][:, slot * TOKENS : (slot + 1) * TOKENS] = part[...].astype(BF16)


def pack_kernel(*refs):
    out = refs[-1]
    for slot, part in enumerate(refs[:-1]):
        out[slot * TOKENS : (slot + 1) * TOKENS, :] = part[...].astype(out.dtype)


def query_product_kernel(normalizer, across, rows, own, other, *refs):
    outs, columns, product = refs[:-2], refs[-2], refs[-1]
    columns[: REPLICAS * TOKENS, :] = own[...].astype(BF16)
    columns[REPLICAS * TOKENS :, :] = other[...].astype(BF16)
    span = PLANE_SIZE // CORES
    for half in range(CORES):
        values = dot(rows[half * HALF : (half + 1) * HALF, :], columns[...], 1, 0) * normalizer
        for index in range(span):
            product[half * span + index, :ROWS, :] = values[index * ROWS : (index + 1) * ROWS]
    for slot, out in enumerate(outs):
        at = lax.rem(across[0] + slot, RING)
        for block in range(RING):
            out[block] = product[(block // 2) * span + at * 2 + block % 2]


def key_value_product_kernel(normalizer, place, rows, own, other, out, columns):
    for core, blocks in enumerate((own, other)):
        for slot in range(REPLICAS):
            at = (core * REPLICAS + slot) * TOKENS
            source = lax.rem(place[0] + REPLICAS - slot, REPLICAS)
            columns[at : at + TOKENS, :] = blocks[source].astype(BF16)
    span = PLANE_SIZE // CORES
    for half in range(CORES):
        values = dot(rows[half * HALF : (half + 1) * HALF, :], columns[...], 1, 0) * normalizer
        for index in range(span):
            out[half * span + index, :ROWS, :] = values[index * ROWS : (index + 1) * ROWS]


def second_stage_kernel(along, own, first, second, third, *outs):
    for slot, out in enumerate(outs):
        at = lax.rem(along[0] + slot, RING)
        out[...] = (own[at] + first[at]) + (second[at] + third[at])


def last_kernel(key_value, own, first, second, third, query_out, key_out, value_out):
    total = key_value[0]
    for index in range(1, PLANE_SIZE):
        total = total + key_value[index]
    key_out[...] = total[:ROWS, :COLS]
    value_out[...] = total[:ROWS, COLS : 2 * COLS]
    query_out[:, EARLY:] = total[:ROWS, 2 * COLS : WIDE]
    total = (own[...] + first[...]) + (second[...] + third[...])
    query_out[:, :EARLY] = total[:ROWS]


def exchange(blocks, axes):
    return lax.all_to_all(blocks, axes, 0, 0, tiled=True)


def shift(values, by, axis):
    return lax.ppermute(values, axis, [(i, (i + by) % RING) for i in range(RING)])


def shifted(slots, axis):
    return [slots[0]] + [shift(slots[s], s, axis) for s in range(1, RING)]


def swap_cores(values):
    return lax.ppermute(values, "core", [(0, 1), (1, 0)])


def both_cores(blocks):
    return blocks + [swap_cores(block) for block in blocks]


def back_project(gradient, weight):
    return dot(gradient, weight, 1, 1)


def body(latent, query_weight, key_weight, value_weight, upstream_grad):
    image_tokens = TOKENS * TILES
    loss_scale = 4.0 * math.sqrt(image_tokens)
    normalizer = 1.0 / math.sqrt(image_tokens * REPLICAS)
    tokens = latent.reshape(TOKENS, D)
    upstream = upstream_grad.reshape(TOKENS, HW)
    place = lax.axis_index("dp").reshape(1)
    core = lax.axis_index("core").reshape(1)
    across = lax.axis_index("x").reshape(1)
    along = lax.axis_index(("zh", "zl")).reshape(1)
    heads = shaped((HEADS, TOKENS, HD), BF16)
    flat = shaped((TOKENS, HW), BF16)
    state = pltpu.VMEM((HW, HD), F32)
    totals = pltpu.VMEM((HEADS, HD), F32)
    weight = pltpu.VMEM((D, HW), BF16)
    wide = pltpu.VMEM((TOKENS, HW), F32)
    blocks = pltpu.VMEM((REPLICAS, TOKENS, COLS), F32)

    key, value, sent = call(
        key_value_kernel,
        "key_value",
        [heads, heads, shaped((TILES, PART + HEADS, HD))],
        [BLOCK, IN_HBM, IN_HBM],
        [weight, weight, state, totals, pltpu.SemaphoreType.DMA((2 * len(CHUNKS),))],
        vmem=20,
    )(tokens, key_weight, value_weight)
    sent, later_tokens = lax.optimization_barrier((sent, tokens))
    half = shaped((D // 2, TOKENS))
    top, bottom = call(
        turn_kernel, "turn", [half, half], [IN_SMEM, BLOCK], [pltpu.VMEM((D, TOKENS), F32)]
    )(core, later_tokens)
    bottom = swap_cores(bottom)
    left_top = shift(top, 1, "dp")
    right_bottom = shift(bottom, 3, "dp")
    got = exchange(sent, IMAGE)
    (query,) = call(
        query_kernel,
        "query",
        [heads],
        [BLOCK, BLOCK],
    )(tokens, query_weight)
    sent, numer, total = call(
        lambda *refs: numerator_kernel(loss_scale, *refs),
        "numerator",
        [shaped((TILES, 2 * PART, HD)), heads, shaped((HEADS, HD))],
        [BLOCK] * 3,
        [state],
        arrived=(0, 1, 2),
    )(got, query, upstream)
    sent, left_top, right_bottom, later_top, later_bottom = lax.optimization_barrier(
        (sent, left_top, right_bottom, top, bottom)
    )
    far_top = shift(left_top, 1, "dp")
    far_bottom = shift(right_bottom, 3, "dp")
    left_bottom = shift(later_bottom, 1, "dp")
    right_top = shift(later_top, 3, "dp")
    got_state = exchange(sent, IMAGE)
    sent, grad_denom = call(
        lambda *refs: total_grad_kernel(loss_scale, *refs),
        "total_grad",
        [shaped((TILES, PART + HEADS, HD)), shaped((TOKENS, HEADS))],
        [BLOCK] * 4,
        [state, totals],
        arrived=(0, 1, 2, 3),
    )(got_state, query, upstream, total)
    sent, far_top, far_bottom, left_bottom, right_top = lax.optimization_barrier(
        (sent, far_top, far_bottom, left_bottom, right_top)
    )
    got = exchange(sent, IMAGE)

    block = shaped((TOKENS, EARLY))
    grad_query, *query_columns, late = call(
        query_grad_kernel,
        "query_grad",
        [flat, block, block, block, block, shaped((REPLICAS, TOKENS, LATE))],
        [IN_SMEM] + [BLOCK] * 5,
        [state, wide, blocks],
        arrived=(1,),
    )(place, got_state, query, numer, total, grad_denom)
    query_columns = shifted(query_columns, "dp")
    (rows,) = call(
        join_kernel,
        "join",
        [shaped((CORES * HALF, 2 * REPLICAS * TOKENS), BF16)],
        [BLOCK] * 8,
        arrived=tuple(range(1, 8)),
    )(top, left_top, far_top, right_top, bottom, left_bottom, far_bottom, right_bottom)
    (query_columns,) = call(
        pack_kernel,
        "pack_query",
        [shaped((REPLICAS * TOKENS, EARLY))],
        [BLOCK] * RING,
        arrived=(1, 2, 3),
    )(*query_columns)
    got, rows, query_columns = lax.optimization_barrier((got, rows, query_columns))

    grad_key, grad_value, sent = call(
        key_value_grad_kernel,
        "key_value_grad",
        [flat, flat, shaped((REPLICAS, TOKENS, LANES))],
        [BLOCK] * 4,
        [state, wide, wide],
        arrived=(0, 1, 2, 3),
    )(got, key, value, late)
    own_columns = exchange(sent, "dp")
    slots = call(
        lambda *refs: query_product_kernel(normalizer, *refs[:4], *refs[5:]),
        "query_product",
        [shaped((RING, PADDED_ROWS, EARLY))] * RING,
        [IN_SMEM, BLOCK, BLOCK, BLOCK, ANYWHERE],
        [
            pltpu.VMEM((2 * REPLICAS * TOKENS, EARLY), BF16),
            pltpu.VMEM((PLANE_SIZE, PADDED_ROWS, EARLY), F32),
        ],
        vmem=24,
        arrived=(3,),
    )(across, rows, query_columns, swap_cores(query_columns), sent)
    slots = shifted(slots, "x")
    own_columns, slots = lax.optimization_barrier((own_columns, slots))
    slots = call(
        second_stage_kernel,
        "second_stage",
        [shaped((PADDED_ROWS, EARLY))] * RING,
        [IN_SMEM] + [BLOCK] * RING,
        arrived=(2, 3, 4),
    )(along, *slots)
    (product,) = call(
        lambda *refs: key_value_product_kernel(normalizer, *refs[:4], *refs[5:]),
        "key_value_product",
        [shaped((PLANE_SIZE, PADDED_ROWS, LANES))],
        [IN_SMEM, BLOCK, BLOCK, BLOCK, ANYWHERE],
        [pltpu.VMEM((2 * REPLICAS * TOKENS, LANES), BF16)],
        vmem=24,
        arrived=(2, 3),
    )(place, rows, own_columns, swap_cores(own_columns), slots[0])
    key_value_out = exchange(product, PLANE)
    slots = shifted(slots, ("zh", "zl"))
    block = shaped((ROWS, COLS))
    query_out, key_out, value_out = call(
        last_kernel, "last", [block] * 3, [BLOCK] * 5, arrived=(0, 2, 3, 4)
    )(key_value_out, *slots)

    summed = back_project(grad_query, query_weight) + back_project(grad_key, key_weight)
    summed = summed + back_project(grad_value, value_weight)
    latent_grad = summed.astype(BF16).reshape(latent.shape)
    return latent_grad, query_out, key_out, value_out


def solution(mesh):
    devices = mesh.devices
    fine = Mesh(
        devices.reshape(REPLICAS, 2, CORES, 4, 2), ("dp", "zh", "core", "x", "zl")
    )
    grid = P("dp", ("zh", "core"), ("x", "zl"), None)
    weight_out = P(("zh", "core", "x", "zl"), "dp")
    return jax.shard_map(
        body,
        mesh=fine,
        in_specs=(grid, P(), P(), P(), grid),
        out_specs=(grid, weight_out, weight_out, weight_out),
        check_vma=False,
    )
```

```python
import math

import jax
import jax.numpy as jnp
from jax import lax
from jax.experimental import pallas as pl
from jax.experimental.pallas import tpu as pltpu
from jax.sharding import Mesh, PartitionSpec as P

D = 2240
HD = 112
HEADS = 10
HW = HEADS * HD
TILES = 32
PART = HW // TILES
PLANE_SIZE = 16
CORES = 2
ROWS = D // TILES
PADDED_ROWS = 72
HALF = D // 4
REPLICAS = 4
RING = 4
COLS = HW // REPLICAS
EARLY = 256
LATE = COLS - EARLY
WIDE = 2 * COLS + LATE
LANES = 640
TOKENS = 128

EPSILON = 1e-15
IMAGE = ("zh", "core", "x", "zl")
PLANE = ("zh", "x", "zl")
CHUNKS = [(start, min(384, D - start)) for start in range(0, D, 384)]

F32 = jnp.float32
BF16 = jnp.bfloat16
BLOCK = pl.BlockSpec()
IN_SMEM = pl.BlockSpec(memory_space=pltpu.SMEM)
ANYWHERE = pl.BlockSpec(memory_space=pl.ANY)
IN_HBM = pl.BlockSpec(memory_space=pltpu.HBM)


def shaped(shape, dtype=F32):
    return pltpu.HBM(shape, dtype)


def call(kernel, name, outs, in_specs, scratch=(), vmem=12, arrived=()):
    run = pl.pallas_call(
        kernel,
        name=name,
        grid=(1,),
        out_shape=outs,
        in_specs=in_specs,
        out_specs=[BLOCK] * len(outs),
        scratch_shapes=list(scratch),
        compiler_params=pltpu.CompilerParams(vmem_limit_bytes=vmem * 1024 * 1024),
    )

    def with_placed(*operands):
        placed = [
            operand
            if spec is IN_SMEM or index in arrived
            else pltpu.with_memory_space_constraint(operand, pltpu.HBM)
            for index, (operand, spec) in enumerate(zip(operands, in_specs))
        ]
        return run(*placed)

    return with_placed


def dot(left, right, left_dim, right_dim):
    return lax.dot_general(
        left, right, (((left_dim,), (right_dim,)), ((), ())), preferred_element_type=F32
    )


def split_dot(left, right, left_dim, right_dim):
    high = right.astype(BF16)
    low = (right - high.astype(F32)).astype(BF16)
    return dot(left, high, left_dim, right_dim) + dot(left, low, left_dim, right_dim)


def relu(values):
    return jnp.maximum(values, jnp.zeros_like(values))


def weight_copies(weight, buffer, semaphores, first):
    copies = []
    for index, (start, size) in enumerate(CHUNKS):
        copies.append(
            pltpu.make_async_copy(
                weight.at[pl.ds(start, size)],
                buffer.at[pl.ds(start, size)],
                semaphores.at[first + index],
            )
        )
    return copies


def project(tokens, buffer, copies):
    total = None
    for (start, size), copy in zip(CHUNKS, copies):
        copy.wait()
        term = dot(tokens[:, start : start + size], buffer[start : start + size, :], 1, 0)
        total = term if total is None else total + term
    return total.astype(BF16)


def store_parts(sent, at, state):
    for tile in range(TILES):
        sent[tile, at : at + PART, :] = state[tile * PART : (tile + 1) * PART, :]


def load_parts(state, got):
    for tile in range(TILES):
        state[tile * PART : (tile + 1) * PART, :] = got[tile, :PART, :]


def head(ref, index):
    return ref[index * HD : (index + 1) * HD, :]


def key_value_kernel(
    tokens, key_weight, value_weight, key, value, sent, key_buffer, value_buffer, state, total, semaphores
):
    value_copies = weight_copies(value_weight, value_buffer, semaphores, 0)
    key_copies = weight_copies(key_weight, key_buffer, semaphores, len(CHUNKS))
    for copy in value_copies + key_copies:
        copy.start()
    rows = tokens[...]
    value_rows = project(rows, value_buffer, value_copies)
    key_rows = project(rows, key_buffer, key_copies)
    for index in range(HEADS):
        part = slice(index * HD, (index + 1) * HD)
        key_head = key_rows[:, part]
        value_head = value_rows[:, part]
        key[index] = key_head
        value[index] = value_head
        positive = relu(key_head)
        state[index * HD : (index + 1) * HD, :] = dot(positive, value_head, 0, 0)
        total[index : index + 1, :] = jnp.sum(positive.astype(F32), axis=0, keepdims=True)
    store_parts(sent, 0, state)
    totals = total[...]
    for tile in range(TILES):
        sent[tile, PART : PART + HEADS, :] = totals


def query_kernel(tokens, weight, query):
    query_rows = dot(tokens[...], weight[...], 1, 0).astype(BF16)
    for index in range(HEADS):
        query[index] = query_rows[:, index * HD : (index + 1) * HD]


def inverse_denominator(positive, total):
    return 1.0 / (jnp.sum(positive * total, axis=1, keepdims=True) + EPSILON)


def numerator_kernel(loss_scale, got, query, upstream, sent, numer, total, state):
    sums = got[0]
    for tile in range(1, TILES):
        sums = sums + got[tile]
    state_part = sums[:PART]
    totals = sums[PART : PART + HEADS]
    total[...] = totals
    for index in range(HEADS):
        part = slice(index * HD, (index + 1) * HD)
        positive = relu(query[index])
        inverse = inverse_denominator(positive.astype(F32), totals[index : index + 1])
        cotangent = upstream[:, part].astype(F32) * loss_scale
        numer_low = (cotangent * inverse).astype(BF16)
        numer[index] = numer_low
        state[index * HD : (index + 1) * HD, :] = dot(positive, numer_low, 0, 0)
    for tile in range(TILES):
        sent[tile, :PART, :] = state_part
    store_parts(sent, PART, state)


def total_grad_kernel(loss_scale, got, query, upstream, total, sent, grad_denom, state, totals):
    load_parts(state, got)
    for index in range(HEADS):
        part = slice(index * HD, (index + 1) * HD)
        positive = relu(query[index])
        wide = positive.astype(F32)
        inverse = inverse_denominator(wide, total[index : index + 1, :])
        cotangent = upstream[:, part].astype(F32) * loss_scale
        product = split_dot(positive, head(state, index), 1, 0)
        grad = -(jnp.sum(cotangent * product, axis=1, keepdims=True) * inverse) * inverse
        grad_denom[:, index : index + 1] = grad
        totals[index : index + 1, :] = jnp.sum(wide * grad, axis=0, keepdims=True)
    part_sum = got[0, PART:, :]
    for tile in range(1, TILES):
        part_sum = part_sum + got[tile, PART:, :]
    values = totals[...]
    for tile in range(TILES):
        sent[tile, :PART, :] = part_sum
        sent[tile, PART : PART + HEADS, :] = values


def place_columns(place, blocks, outs, at, first=0, last=COLS):
    for slot, out in enumerate(outs):
        block = blocks[lax.rem(place[0] + slot, REPLICAS)]
        out[:, at : at + last - first] = block[:, first:last]


def split_columns(flat, blocks):
    for block in range(REPLICAS):
        blocks[block] = flat[:, block * COLS : (block + 1) * COLS]


def query_grad_kernel(
    place, got, query, numer, total, grad_denom, grad, own, first, second, third, late, state, flat, blocks
):
    load_parts(state, got)
    for index in range(HEADS):
        part = slice(index * HD, (index + 1) * HD)
        values = split_dot(numer[index], head(state, index), 1, 1)
        values = values + grad_denom[:, index : index + 1] * total[index : index + 1, :]
        values = jnp.where(query[index].astype(F32) > 0, values, 0.0).astype(BF16)
        grad[:, part] = values
        flat[:, part] = values.astype(F32)
    split_columns(flat, blocks)
    place_columns(place, blocks, (own, first, second, third), 0, 0, EARLY)
    for block in range(REPLICAS):
        late[block] = blocks[block][:, EARLY:]


def key_value_grad_kernel(got, key, value, late, grad_key, grad_value, sent, state, flat_key, flat_value):
    load_parts(state, got)
    totals = got[0, PART : PART + HEADS, :]
    for tile in range(1, TILES):
        totals = totals + got[tile, PART : PART + HEADS, :]
    for index in range(HEADS):
        part = slice(index * HD, (index + 1) * HD)
        key_head = key[index]
        positive = relu(key_head)
        state_head = head(state, index)
        values = split_dot(positive, state_head, 1, 0).astype(BF16)
        grad_value[:, part] = values
        flat_value[:, part] = values.astype(F32)
        values = split_dot(value[index], state_head, 1, 1) + totals[index : index + 1]
        values = jnp.where(key_head.astype(F32) > 0, values, 0.0).astype(BF16)
        grad_key[:, part] = values
        flat_key[:, part] = values.astype(F32)
    for block in range(REPLICAS):
        part = slice(block * COLS, (block + 1) * COLS)
        sent[block, :, :COLS] = flat_key[:, part]
        sent[block, :, COLS : 2 * COLS] = flat_value[:, part]
        sent[block, :, 2 * COLS : WIDE] = late[block]
        sent[block, :, WIDE:] = jnp.zeros((TOKENS, LANES - WIDE), F32)


def turn_kernel(core, tokens, mine, other, turned):
    for start in range(0, D, 128):
        size = min(128, D - start)
        turned[start : start + size, :] = tokens[:, start : start + size].astype(F32).T
    for half in range(CORES):
        rows = slice(half * HALF, (half + 1) * HALF)
        for out, which in ((mine, core[0]), (other, 1 - core[0])):
            start = pl.multiple_of((half * CORES + which) * HALF, 16)
            out[rows, :] = turned[pl.ds(start, HALF), :]


def join_kernel(*refs):
    for slot, part in enumerate(refs[:-1]):
        refs[-1][:, slot * TOKENS : (slot + 1) * TOKENS] = part[...].astype(BF16)


def pack_kernel(*refs):
    out = refs[-1]
    for slot, part in enumerate(refs[:-1]):
        out[slot * TOKENS : (slot + 1) * TOKENS, :] = part[...].astype(out.dtype)


def query_product_kernel(normalizer, across, rows, own, other, *refs):
    outs, columns, product = refs[:-2], refs[-2], refs[-1]
    columns[: REPLICAS * TOKENS, :] = own[...].astype(BF16)
    columns[REPLICAS * TOKENS :, :] = other[...].astype(BF16)
    span = PLANE_SIZE // CORES
    for half in range(CORES):
        values = dot(rows[half * HALF : (half + 1) * HALF, :], columns[...], 1, 0) * normalizer
        for index in range(span):
            product[half * span + index, :ROWS, :] = values[index * ROWS : (index + 1) * ROWS]
    for slot, out in enumerate(outs):
        at = lax.rem(across[0] + slot, RING)
        for block in range(RING):
            out[block] = product[(block // 2) * span + at * 2 + block % 2]


def key_value_product_kernel(normalizer, place, rows, own, other, out, columns):
    for core, blocks in enumerate((own, other)):
        for slot in range(REPLICAS):
            at = (core * REPLICAS + slot) * TOKENS
            source = lax.rem(place[0] + REPLICAS - slot, REPLICAS)
            columns[at : at + TOKENS, :] = blocks[source].astype(BF16)
    span = PLANE_SIZE // CORES
    for half in range(CORES):
        values = dot(rows[half * HALF : (half + 1) * HALF, :], columns[...], 1, 0) * normalizer
        for index in range(span):
            out[half * span + index, :ROWS, :] = values[index * ROWS : (index + 1) * ROWS]


def second_stage_kernel(along, own, first, second, third, *outs):
    for slot, out in enumerate(outs):
        at = lax.rem(along[0] + slot, RING)
        out[...] = (own[at] + first[at]) + (second[at] + third[at])


def last_kernel(key_value, own, first, second, third, query_out, key_out, value_out):
    total = key_value[0]
    for index in range(1, PLANE_SIZE):
        total = total + key_value[index]
    key_out[...] = total[:ROWS, :COLS]
    value_out[...] = total[:ROWS, COLS : 2 * COLS]
    query_out[:, EARLY:] = total[:ROWS, 2 * COLS : WIDE]
    total = (own[...] + first[...]) + (second[...] + third[...])
    query_out[:, :EARLY] = total[:ROWS]


def exchange(blocks, axes):
    return lax.all_to_all(blocks, axes, 0, 0, tiled=True)


def shift(values, by, axis):
    return lax.ppermute(values, axis, [(i, (i + by) % RING) for i in range(RING)])


def shifted(slots, axis):
    return [slots[0]] + [shift(slots[s], s, axis) for s in range(1, RING)]


def swap_cores(values):
    return lax.ppermute(values, "core", [(0, 1), (1, 0)])


def both_cores(blocks):
    return blocks + [swap_cores(block) for block in blocks]


def back_project(gradient, weight):
    return dot(gradient, weight, 1, 1)


def body(latent, query_weight, key_weight, value_weight, upstream_grad):
    image_tokens = TOKENS * TILES
    loss_scale = 4.0 * math.sqrt(image_tokens)
    normalizer = 1.0 / math.sqrt(image_tokens * REPLICAS)
    tokens = latent.reshape(TOKENS, D)
    upstream = upstream_grad.reshape(TOKENS, HW)
    place = lax.axis_index("dp").reshape(1)
    core = lax.axis_index("core").reshape(1)
    across = lax.axis_index("x").reshape(1)
    along = lax.axis_index(("zh", "zl")).reshape(1)
    heads = shaped((HEADS, TOKENS, HD), BF16)
    flat = shaped((TOKENS, HW), BF16)
    state = pltpu.VMEM((HW, HD), F32)
    totals = pltpu.VMEM((HEADS, HD), F32)
    weight = pltpu.VMEM((D, HW), BF16)
    wide = pltpu.VMEM((TOKENS, HW), F32)
    blocks = pltpu.VMEM((REPLICAS, TOKENS, COLS), F32)

    key, value, sent = call(
        key_value_kernel,
        "key_value",
        [heads, heads, shaped((TILES, PART + HEADS, HD))],
        [BLOCK, IN_HBM, IN_HBM],
        [weight, weight, state, totals, pltpu.SemaphoreType.DMA((2 * len(CHUNKS),))],
        vmem=20,
    )(tokens, key_weight, value_weight)
    sent, later_tokens = lax.optimization_barrier((sent, tokens))
    half = shaped((D // 2, TOKENS))
    top, bottom = call(
        turn_kernel, "turn", [half, half], [IN_SMEM, BLOCK], [pltpu.VMEM((D, TOKENS), F32)]
    )(core, later_tokens)
    bottom = swap_cores(bottom)
    left_top = shift(top, 1, "dp")
    right_bottom = shift(bottom, 3, "dp")
    got = exchange(sent, IMAGE)
    (query,) = call(
        query_kernel,
        "query",
        [heads],
        [BLOCK, BLOCK],
    )(tokens, query_weight)
    sent, numer, total = call(
        lambda *refs: numerator_kernel(loss_scale, *refs),
        "numerator",
        [shaped((TILES, 2 * PART, HD)), heads, shaped((HEADS, HD))],
        [BLOCK] * 3,
        [state],
        arrived=(0, 1, 2),
    )(got, query, upstream)
    sent, left_top, right_bottom, later_top, later_bottom = lax.optimization_barrier(
        (sent, left_top, right_bottom, top, bottom)
    )
    far_top = shift(left_top, 1, "dp")
    far_bottom = shift(right_bottom, 3, "dp")
    got_state = exchange(sent, IMAGE)
    sent, grad_denom = call(
        lambda *refs: total_grad_kernel(loss_scale, *refs),
        "total_grad",
        [shaped((TILES, PART + HEADS, HD)), shaped((TOKENS, HEADS))],
        [BLOCK] * 4,
        [state, totals],
        arrived=(0, 1, 2, 3),
    )(got_state, query, upstream, total)
    sent, far_top, far_bottom, later_top, later_bottom = lax.optimization_barrier(
        (sent, far_top, far_bottom, later_top, later_bottom)
    )
    left_bottom = shift(later_bottom, 1, "dp")
    right_top = shift(later_top, 3, "dp")
    got = exchange(sent, IMAGE)

    block = shaped((TOKENS, EARLY))
    grad_query, *query_columns, late = call(
        query_grad_kernel,
        "query_grad",
        [flat, block, block, block, block, shaped((REPLICAS, TOKENS, LATE))],
        [IN_SMEM] + [BLOCK] * 5,
        [state, wide, blocks],
        arrived=(1,),
    )(place, got_state, query, numer, total, grad_denom)
    query_columns = shifted(query_columns, "dp")
    (rows,) = call(
        join_kernel,
        "join",
        [shaped((CORES * HALF, 2 * REPLICAS * TOKENS), BF16)],
        [BLOCK] * 8,
        arrived=tuple(range(1, 8)),
    )(top, left_top, far_top, right_top, bottom, left_bottom, far_bottom, right_bottom)
    (query_columns,) = call(
        pack_kernel,
        "pack_query",
        [shaped((REPLICAS * TOKENS, EARLY))],
        [BLOCK] * RING,
        arrived=(1, 2, 3),
    )(*query_columns)
    got, rows, query_columns = lax.optimization_barrier((got, rows, query_columns))

    grad_key, grad_value, sent = call(
        key_value_grad_kernel,
        "key_value_grad",
        [flat, flat, shaped((REPLICAS, TOKENS, LANES))],
        [BLOCK] * 4,
        [state, wide, wide],
        arrived=(0, 1, 2, 3),
    )(got, key, value, late)
    own_columns = exchange(sent, "dp")
    slots = call(
        lambda *refs: query_product_kernel(normalizer, *refs[:4], *refs[5:]),
        "query_product",
        [shaped((RING, PADDED_ROWS, EARLY))] * RING,
        [IN_SMEM, BLOCK, BLOCK, BLOCK, ANYWHERE],
        [
            pltpu.VMEM((2 * REPLICAS * TOKENS, EARLY), BF16),
            pltpu.VMEM((PLANE_SIZE, PADDED_ROWS, EARLY), F32),
        ],
        vmem=24,
        arrived=(3,),
    )(across, rows, query_columns, swap_cores(query_columns), sent)
    slots = shifted(slots, "x")
    own_columns, slots = lax.optimization_barrier((own_columns, slots))
    slots = call(
        second_stage_kernel,
        "second_stage",
        [shaped((PADDED_ROWS, EARLY))] * RING,
        [IN_SMEM] + [BLOCK] * RING,
        arrived=(2, 3, 4),
    )(along, *slots)
    (product,) = call(
        lambda *refs: key_value_product_kernel(normalizer, *refs[:4], *refs[5:]),
        "key_value_product",
        [shaped((PLANE_SIZE, PADDED_ROWS, LANES))],
        [IN_SMEM, BLOCK, BLOCK, BLOCK, ANYWHERE],
        [pltpu.VMEM((2 * REPLICAS * TOKENS, LANES), BF16)],
        vmem=24,
        arrived=(2, 3),
    )(place, rows, own_columns, swap_cores(own_columns), slots[0])
    key_value_out = exchange(product, PLANE)
    slots = shifted(slots, ("zh", "zl"))
    block = shaped((ROWS, COLS))
    query_out, key_out, value_out = call(
        last_kernel, "last", [block] * 3, [BLOCK] * 5, arrived=(0, 2, 3, 4)
    )(key_value_out, *slots)

    summed = back_project(grad_query, query_weight) + back_project(grad_key, key_weight)
    summed = summed + back_project(grad_value, value_weight)
    latent_grad = summed.astype(BF16).reshape(latent.shape)
    return latent_grad, query_out, key_out, value_out


def solution(mesh):
    devices = mesh.devices
    fine = Mesh(
        devices.reshape(REPLICAS, 2, CORES, 4, 2), ("dp", "zh", "core", "x", "zl")
    )
    grid = P("dp", ("zh", "core"), ("x", "zl"), None)
    weight_out = P(("zh", "core", "x", "zl"), "dp")
    return jax.shard_map(
        body,
        mesh=fine,
        in_specs=(grid, P(), P(), P(), grid),
        out_specs=(grid, weight_out, weight_out, weight_out),
        check_vma=False,
    )
```

```python
import math

import jax
import jax.numpy as jnp
from jax import lax
from jax.experimental import pallas as pl
from jax.experimental.pallas import tpu as pltpu
from jax.sharding import Mesh, PartitionSpec as P

D = 2240
HD = 112
HEADS = 10
HW = HEADS * HD
TILES = 32
PART = HW // TILES
PLANE_SIZE = 16
CORES = 2
ROWS = D // TILES
PADDED_ROWS = 72
HALF = D // 4
REPLICAS = 4
RING = 4
COLS = HW // REPLICAS
EARLY = 256
LATE = COLS - EARLY
WIDE = 2 * COLS + LATE
LANES = 640
TOKENS = 128

EPSILON = 1e-15
IMAGE = ("zh", "core", "x", "zl")
PLANE = ("zh", "x", "zl")
CHUNKS = [(start, min(384, D - start)) for start in range(0, D, 384)]

F32 = jnp.float32
BF16 = jnp.bfloat16
BLOCK = pl.BlockSpec()
IN_SMEM = pl.BlockSpec(memory_space=pltpu.SMEM)
ANYWHERE = pl.BlockSpec(memory_space=pl.ANY)
IN_HBM = pl.BlockSpec(memory_space=pltpu.HBM)


def shaped(shape, dtype=F32):
    return pltpu.HBM(shape, dtype)


def call(kernel, name, outs, in_specs, scratch=(), vmem=12, arrived=()):
    run = pl.pallas_call(
        kernel,
        name=name,
        grid=(1,),
        out_shape=outs,
        in_specs=in_specs,
        out_specs=[BLOCK] * len(outs),
        scratch_shapes=list(scratch),
        compiler_params=pltpu.CompilerParams(vmem_limit_bytes=vmem * 1024 * 1024),
    )

    def with_placed(*operands):
        placed = [
            operand
            if spec is IN_SMEM or index in arrived
            else pltpu.with_memory_space_constraint(operand, pltpu.HBM)
            for index, (operand, spec) in enumerate(zip(operands, in_specs))
        ]
        return run(*placed)

    return with_placed


def dot(left, right, left_dim, right_dim):
    return lax.dot_general(
        left, right, (((left_dim,), (right_dim,)), ((), ())), preferred_element_type=F32
    )


def split_dot(left, right, left_dim, right_dim):
    high = right.astype(BF16)
    low = (right - high.astype(F32)).astype(BF16)
    return dot(left, high, left_dim, right_dim) + dot(left, low, left_dim, right_dim)


def relu(values):
    return jnp.maximum(values, jnp.zeros_like(values))


def weight_copies(weight, buffer, semaphores, first):
    copies = []
    for index, (start, size) in enumerate(CHUNKS):
        copies.append(
            pltpu.make_async_copy(
                weight.at[pl.ds(start, size)],
                buffer.at[pl.ds(start, size)],
                semaphores.at[first + index],
            )
        )
    return copies


def project(tokens, buffer, copies):
    total = None
    for (start, size), copy in zip(CHUNKS, copies):
        copy.wait()
        term = dot(tokens[:, start : start + size], buffer[start : start + size, :], 1, 0)
        total = term if total is None else total + term
    return total.astype(BF16)


def store_parts(sent, at, state):
    for tile in range(TILES):
        sent[tile, at : at + PART, :] = state[tile * PART : (tile + 1) * PART, :]


def load_parts(state, got):
    for tile in range(TILES):
        state[tile * PART : (tile + 1) * PART, :] = got[tile, :PART, :]


def head(ref, index):
    return ref[index * HD : (index + 1) * HD, :]


def key_value_kernel(
    tokens, key_weight, value_weight, key, value, sent, key_buffer, value_buffer, state, total, semaphores
):
    value_copies = weight_copies(value_weight, value_buffer, semaphores, 0)
    key_copies = weight_copies(key_weight, key_buffer, semaphores, len(CHUNKS))
    for copy in value_copies + key_copies:
        copy.start()
    rows = tokens[...]
    value_rows = project(rows, value_buffer, value_copies)
    key_rows = project(rows, key_buffer, key_copies)
    for index in range(HEADS):
        part = slice(index * HD, (index + 1) * HD)
        key_head = key_rows[:, part]
        value_head = value_rows[:, part]
        key[index] = key_head
        value[index] = value_head
        positive = relu(key_head)
        state[index * HD : (index + 1) * HD, :] = dot(positive, value_head, 0, 0)
        total[index : index + 1, :] = jnp.sum(positive.astype(F32), axis=0, keepdims=True)
    store_parts(sent, 0, state)
    totals = total[...]
    for tile in range(TILES):
        sent[tile, PART : PART + HEADS, :] = totals


def query_kernel(tokens, weight, query):
    query_rows = dot(tokens[...], weight[...], 1, 0).astype(BF16)
    for index in range(HEADS):
        query[index] = query_rows[:, index * HD : (index + 1) * HD]


def inverse_denominator(positive, total):
    return 1.0 / (jnp.sum(positive * total, axis=1, keepdims=True) + EPSILON)


def numerator_kernel(loss_scale, got, query, upstream, sent, numer, total, state):
    sums = got[0]
    for tile in range(1, TILES):
        sums = sums + got[tile]
    state_part = sums[:PART]
    totals = sums[PART : PART + HEADS]
    total[...] = totals
    for index in range(HEADS):
        part = slice(index * HD, (index + 1) * HD)
        positive = relu(query[index])
        inverse = inverse_denominator(positive.astype(F32), totals[index : index + 1])
        cotangent = upstream[:, part].astype(F32) * loss_scale
        numer_low = (cotangent * inverse).astype(BF16)
        numer[index] = numer_low
        state[index * HD : (index + 1) * HD, :] = dot(positive, numer_low, 0, 0)
    for tile in range(TILES):
        sent[tile, :PART, :] = state_part
    store_parts(sent, PART, state)


def total_grad_kernel(loss_scale, got, query, upstream, total, sent, grad_denom, state, totals):
    load_parts(state, got)
    for index in range(HEADS):
        part = slice(index * HD, (index + 1) * HD)
        positive = relu(query[index])
        wide = positive.astype(F32)
        inverse = inverse_denominator(wide, total[index : index + 1, :])
        cotangent = upstream[:, part].astype(F32) * loss_scale
        product = split_dot(positive, head(state, index), 1, 0)
        grad = -(jnp.sum(cotangent * product, axis=1, keepdims=True) * inverse) * inverse
        grad_denom[:, index : index + 1] = grad
        totals[index : index + 1, :] = jnp.sum(wide * grad, axis=0, keepdims=True)
    part_sum = got[0, PART:, :]
    for tile in range(1, TILES):
        part_sum = part_sum + got[tile, PART:, :]
    values = totals[...]
    for tile in range(TILES):
        sent[tile, :PART, :] = part_sum
        sent[tile, PART : PART + HEADS, :] = values


def place_columns(place, blocks, outs, at, first=0, last=COLS):
    for slot, out in enumerate(outs):
        block = blocks[lax.rem(place[0] + slot, REPLICAS)]
        out[:, at : at + last - first] = block[:, first:last]


def split_columns(flat, blocks):
    for block in range(REPLICAS):
        blocks[block] = flat[:, block * COLS : (block + 1) * COLS]


def query_grad_kernel(
    place, got, query, numer, total, grad_denom, grad, own, first, second, third, late, state, flat, blocks
):
    load_parts(state, got)
    for index in range(HEADS):
        part = slice(index * HD, (index + 1) * HD)
        values = split_dot(numer[index], head(state, index), 1, 1)
        values = values + grad_denom[:, index : index + 1] * total[index : index + 1, :]
        values = jnp.where(query[index].astype(F32) > 0, values, 0.0).astype(BF16)
        grad[:, part] = values
        flat[:, part] = values.astype(F32)
    split_columns(flat, blocks)
    place_columns(place, blocks, (own, first, second, third), 0, 0, EARLY)
    for block in range(REPLICAS):
        late[block] = blocks[block][:, EARLY:]


def key_value_grad_kernel(got, key, value, late, grad_key, grad_value, sent, state, flat_key, flat_value):
    load_parts(state, got)
    totals = got[0, PART : PART + HEADS, :]
    for tile in range(1, TILES):
        totals = totals + got[tile, PART : PART + HEADS, :]
    for index in range(HEADS):
        part = slice(index * HD, (index + 1) * HD)
        key_head = key[index]
        positive = relu(key_head)
        state_head = head(state, index)
        values = split_dot(positive, state_head, 1, 0).astype(BF16)
        grad_value[:, part] = values
        flat_value[:, part] = values.astype(F32)
        values = split_dot(value[index], state_head, 1, 1) + totals[index : index + 1]
        values = jnp.where(key_head.astype(F32) > 0, values, 0.0).astype(BF16)
        grad_key[:, part] = values
        flat_key[:, part] = values.astype(F32)
    for block in range(REPLICAS):
        part = slice(block * COLS, (block + 1) * COLS)
        sent[block, :, :COLS] = flat_key[:, part]
        sent[block, :, COLS : 2 * COLS] = flat_value[:, part]
        sent[block, :, 2 * COLS : WIDE] = late[block]
        sent[block, :, WIDE:] = jnp.zeros((TOKENS, LANES - WIDE), F32)


def turn_kernel(core, tokens, mine, other, turned):
    for start in range(0, D, 128):
        size = min(128, D - start)
        turned[start : start + size, :] = tokens[:, start : start + size].astype(F32).T
    for half in range(CORES):
        rows = slice(half * HALF, (half + 1) * HALF)
        for out, which in ((mine, core[0]), (other, 1 - core[0])):
            start = pl.multiple_of((half * CORES + which) * HALF, 16)
            out[rows, :] = turned[pl.ds(start, HALF), :]


def join_kernel(*refs):
    parts, out = refs[:-1], refs[-1]
    for core in range(CORES):
        own, left, far_upper, far_lower, right = parts[core * 5 : core * 5 + 5]
        at = core * REPLICAS * TOKENS
        out[:, at : at + TOKENS] = own[...].astype(BF16)
        out[:, at + TOKENS : at + 2 * TOKENS] = left[...].astype(BF16)
        out[:HALF, at + 2 * TOKENS : at + 3 * TOKENS] = far_upper[...].astype(BF16)
        out[HALF:, at + 2 * TOKENS : at + 3 * TOKENS] = far_lower[...].astype(BF16)
        out[:, at + 3 * TOKENS : at + 4 * TOKENS] = right[...].astype(BF16)


def pack_kernel(*refs):
    out = refs[-1]
    for slot, part in enumerate(refs[:-1]):
        out[slot * TOKENS : (slot + 1) * TOKENS, :] = part[...].astype(out.dtype)


def query_product_kernel(normalizer, across, rows, own, other, *refs):
    outs, columns, product = refs[:-2], refs[-2], refs[-1]
    columns[: REPLICAS * TOKENS, :] = own[...].astype(BF16)
    columns[REPLICAS * TOKENS :, :] = other[...].astype(BF16)
    span = PLANE_SIZE // CORES
    for half in range(CORES):
        values = dot(rows[half * HALF : (half + 1) * HALF, :], columns[...], 1, 0) * normalizer
        for index in range(span):
            product[half * span + index, :ROWS, :] = values[index * ROWS : (index + 1) * ROWS]
    for slot, out in enumerate(outs):
        at = lax.rem(across[0] + slot, RING)
        for block in range(RING):
            out[block] = product[(block // 2) * span + at * 2 + block % 2]


def key_value_product_kernel(normalizer, place, rows, own, other, out, columns):
    for core, blocks in enumerate((own, other)):
        for slot in range(REPLICAS):
            at = (core * REPLICAS + slot) * TOKENS
            source = lax.rem(place[0] + REPLICAS - slot, REPLICAS)
            columns[at : at + TOKENS, :] = blocks[source].astype(BF16)
    span = PLANE_SIZE // CORES
    for half in range(CORES):
        values = dot(rows[half * HALF : (half + 1) * HALF, :], columns[...], 1, 0) * normalizer
        for index in range(span):
            out[half * span + index, :ROWS, :] = values[index * ROWS : (index + 1) * ROWS]


def second_stage_kernel(along, own, first, second, third, *outs):
    for slot, out in enumerate(outs):
        at = lax.rem(along[0] + slot, RING)
        out[...] = (own[at] + first[at]) + (second[at] + third[at])


def last_kernel(key_value, own, first, second, third, query_out, key_out, value_out):
    total = key_value[0]
    for index in range(1, PLANE_SIZE):
        total = total + key_value[index]
    key_out[...] = total[:ROWS, :COLS]
    value_out[...] = total[:ROWS, COLS : 2 * COLS]
    query_out[:, EARLY:] = total[:ROWS, 2 * COLS : WIDE]
    total = (own[...] + first[...]) + (second[...] + third[...])
    query_out[:, :EARLY] = total[:ROWS]


def exchange(blocks, axes):
    return lax.all_to_all(blocks, axes, 0, 0, tiled=True)


def shift(values, by, axis):
    return lax.ppermute(values, axis, [(i, (i + by) % RING) for i in range(RING)])


def shifted(slots, axis):
    return [slots[0]] + [shift(slots[s], s, axis) for s in range(1, RING)]


def swap_cores(values):
    return lax.ppermute(values, "core", [(0, 1), (1, 0)])


def both_cores(blocks):
    return blocks + [swap_cores(block) for block in blocks]


def back_project(gradient, weight):
    return dot(gradient, weight, 1, 1)


def body(latent, query_weight, key_weight, value_weight, upstream_grad):
    image_tokens = TOKENS * TILES
    loss_scale = 4.0 * math.sqrt(image_tokens)
    normalizer = 1.0 / math.sqrt(image_tokens * REPLICAS)
    tokens = latent.reshape(TOKENS, D)
    upstream = upstream_grad.reshape(TOKENS, HW)
    place = lax.axis_index("dp").reshape(1)
    core = lax.axis_index("core").reshape(1)
    across = lax.axis_index("x").reshape(1)
    along = lax.axis_index(("zh", "zl")).reshape(1)
    heads = shaped((HEADS, TOKENS, HD), BF16)
    flat = shaped((TOKENS, HW), BF16)
    state = pltpu.VMEM((HW, HD), F32)
    totals = pltpu.VMEM((HEADS, HD), F32)
    weight = pltpu.VMEM((D, HW), BF16)
    wide = pltpu.VMEM((TOKENS, HW), F32)
    blocks = pltpu.VMEM((REPLICAS, TOKENS, COLS), F32)

    key, value, sent = call(
        key_value_kernel,
        "key_value",
        [heads, heads, shaped((TILES, PART + HEADS, HD))],
        [BLOCK, IN_HBM, IN_HBM],
        [weight, weight, state, totals, pltpu.SemaphoreType.DMA((2 * len(CHUNKS),))],
        vmem=20,
    )(tokens, key_weight, value_weight)
    sent, later_tokens = lax.optimization_barrier((sent, tokens))
    half = shaped((D // 2, TOKENS))
    top, bottom = call(
        turn_kernel, "turn", [half, half], [IN_SMEM, BLOCK], [pltpu.VMEM((D, TOKENS), F32)]
    )(core, later_tokens)
    bottom = swap_cores(bottom)
    top_left, top_right = shift(top, 1, "dp"), shift(top, 3, "dp")
    got = exchange(sent, IMAGE)
    (query,) = call(
        query_kernel,
        "query",
        [heads],
        [BLOCK, BLOCK],
    )(tokens, query_weight)
    sent, numer, total = call(
        lambda *refs: numerator_kernel(loss_scale, *refs),
        "numerator",
        [shaped((TILES, 2 * PART, HD)), heads, shaped((HEADS, HD))],
        [BLOCK] * 3,
        [state],
        arrived=(0, 2),
    )(got, query, upstream)
    sent, top_left, top_right, bottom = lax.optimization_barrier(
        (sent, top_left, top_right, bottom)
    )
    bottom_left, bottom_right = shift(bottom, 1, "dp"), shift(bottom, 3, "dp")
    top_far = shift(top_left[:HALF], 1, "dp"), shift(top_right[HALF:], 3, "dp")
    got_state = exchange(sent, IMAGE)
    sent, grad_denom = call(
        lambda *refs: total_grad_kernel(loss_scale, *refs),
        "total_grad",
        [shaped((TILES, PART + HEADS, HD)), shaped((TOKENS, HEADS))],
        [BLOCK] * 4,
        [state, totals],
        arrived=(0, 1, 2, 3),
    )(got_state, query, upstream, total)
    sent, top_far, bottom_left, bottom_right = lax.optimization_barrier(
        (sent, top_far, bottom_left, bottom_right)
    )
    bottom_far = shift(bottom_left[:HALF], 1, "dp"), shift(bottom_right[HALF:], 3, "dp")
    got = exchange(sent, IMAGE)

    block = shaped((TOKENS, EARLY))
    grad_query, *query_columns, late = call(
        query_grad_kernel,
        "query_grad",
        [flat, block, block, block, block, shaped((REPLICAS, TOKENS, LATE))],
        [IN_SMEM] + [BLOCK] * 5,
        [state, wide, blocks],
        arrived=(1,),
    )(place, got_state, query, numer, total, grad_denom)
    query_columns = shifted(query_columns, "dp")
    (rows,) = call(
        join_kernel,
        "join",
        [shaped((CORES * HALF, 2 * REPLICAS * TOKENS), BF16)],
        [BLOCK] * 10,
        arrived=tuple(range(1, 10)),
    )(top, top_left, *top_far, top_right, bottom, bottom_left, *bottom_far, bottom_right)
    (query_columns,) = call(
        lambda *refs: pack_kernel(*refs[:RING], refs[-1]),
        "pack_query",
        [shaped((REPLICAS * TOKENS, EARLY))],
        [BLOCK] * RING + [ANYWHERE],
        arrived=(1, 2, 3),
    )(*query_columns, rows)
    got, rows, query_columns = lax.optimization_barrier((got, rows, query_columns))

    grad_key, grad_value, sent = call(
        key_value_grad_kernel,
        "key_value_grad",
        [flat, flat, shaped((REPLICAS, TOKENS, LANES))],
        [BLOCK] * 4,
        [state, wide, wide],
        arrived=(0, 1, 2, 3),
    )(got, key, value, late)
    own_columns = exchange(sent, "dp")
    slots = call(
        lambda *refs: query_product_kernel(normalizer, *refs[:4], *refs[5:]),
        "query_product",
        [shaped((RING, PADDED_ROWS, EARLY))] * RING,
        [IN_SMEM, BLOCK, BLOCK, BLOCK, ANYWHERE],
        [
            pltpu.VMEM((2 * REPLICAS * TOKENS, EARLY), BF16),
            pltpu.VMEM((PLANE_SIZE, PADDED_ROWS, EARLY), F32),
        ],
        vmem=24,
        arrived=(3,),
    )(across, rows, query_columns, swap_cores(query_columns), sent)
    slots = shifted(slots, "x")
    own_columns, slots = lax.optimization_barrier((own_columns, slots))
    slots = call(
        second_stage_kernel,
        "second_stage",
        [shaped((PADDED_ROWS, EARLY))] * RING,
        [IN_SMEM] + [BLOCK] * RING,
        arrived=(2, 3, 4),
    )(along, *slots)
    (product,) = call(
        lambda *refs: key_value_product_kernel(normalizer, *refs[:4], *refs[5:]),
        "key_value_product",
        [shaped((PLANE_SIZE, PADDED_ROWS, LANES))],
        [IN_SMEM, BLOCK, BLOCK, BLOCK, ANYWHERE],
        [pltpu.VMEM((2 * REPLICAS * TOKENS, LANES), BF16)],
        vmem=24,
        arrived=(2, 3),
    )(place, rows, own_columns, swap_cores(own_columns), slots[0])
    key_value_out = exchange(product, PLANE)
    slots = shifted(slots, ("zh", "zl"))
    block = shaped((ROWS, COLS))
    query_out, key_out, value_out = call(
        last_kernel, "last", [block] * 3, [BLOCK] * 5, arrived=(0, 2, 3, 4)
    )(key_value_out, *slots)

    summed = back_project(grad_query, query_weight) + back_project(grad_key, key_weight)
    summed = summed + back_project(grad_value, value_weight)
    latent_grad = summed.astype(BF16).reshape(latent.shape)
    return latent_grad, query_out, key_out, value_out


def solution(mesh):
    devices = mesh.devices
    fine = Mesh(
        devices.reshape(REPLICAS, 2, CORES, 4, 2), ("dp", "zh", "core", "x", "zl")
    )
    grid = P("dp", ("zh", "core"), ("x", "zl"), None)
    weight_out = P(("zh", "core", "x", "zl"), "dp")
    return jax.shard_map(
        body,
        mesh=fine,
        in_specs=(grid, P(), P(), P(), grid),
        out_specs=(grid, weight_out, weight_out, weight_out),
        check_vma=False,
    )
```

```python
import math

import jax
import jax.numpy as jnp
from jax import lax
from jax.experimental import pallas as pl
from jax.experimental.pallas import tpu as pltpu
from jax.sharding import Mesh, PartitionSpec as P

D = 2240
HD = 112
HEADS = 10
HW = HEADS * HD
TILES = 32
PART = HW // TILES
PLANE_SIZE = 16
CORES = 2
ROWS = D // TILES
PADDED_ROWS = 72
SPLIT = 40
HALF = D // 4
REPLICAS = 4
RING = 4
COLS = HW // REPLICAS
EARLY = 256
LATE = COLS - EARLY
WIDE = 2 * COLS + LATE
LANES = 640
TOKENS = 128

EPSILON = 1e-15
IMAGE = ("zh", "core", "x", "zl")
PLANE = ("zh", "x", "zl")
CHUNKS = [(0, 1152), (1152, D - 1152)]

F32 = jnp.float32
BF16 = jnp.bfloat16
BLOCK = pl.BlockSpec()
IN_SMEM = pl.BlockSpec(memory_space=pltpu.SMEM)
ANYWHERE = pl.BlockSpec(memory_space=pl.ANY)
IN_HBM = pl.BlockSpec(memory_space=pltpu.HBM)


def shaped(shape, dtype=F32):
    return pltpu.HBM(shape, dtype)


def call(kernel, name, outs, in_specs, scratch=(), vmem=12, arrived=(), steps=1, out_specs=None):
    run = pl.pallas_call(
        kernel,
        name=name,
        grid=(steps,),
        out_shape=outs,
        in_specs=in_specs,
        out_specs=out_specs or [BLOCK] * len(outs),
        scratch_shapes=list(scratch),
        compiler_params=pltpu.CompilerParams(vmem_limit_bytes=vmem * 1024 * 1024),
    )

    def with_placed(*operands):
        placed = [
            operand
            if spec is IN_SMEM or index in arrived
            else pltpu.with_memory_space_constraint(operand, pltpu.HBM)
            for index, (operand, spec) in enumerate(zip(operands, in_specs))
        ]
        return run(*placed)

    return with_placed


def dot(left, right, left_dim, right_dim):
    return lax.dot_general(
        left, right, (((left_dim,), (right_dim,)), ((), ())), preferred_element_type=F32
    )


def split_dot(left, right, left_dim, right_dim):
    high = right.astype(BF16)
    low = (right - high.astype(F32)).astype(BF16)
    return dot(left, high, left_dim, right_dim) + dot(left, low, left_dim, right_dim)


def relu(values):
    return jnp.maximum(values, jnp.zeros_like(values))


def weight_copies(weight, buffer, semaphores, first):
    copies = []
    for index, (start, size) in enumerate(CHUNKS):
        copies.append(
            pltpu.make_async_copy(
                weight.at[pl.ds(start, size)],
                buffer.at[pl.ds(start, size)],
                semaphores.at[first + index],
            )
        )
    return copies


def project(tokens, buffer, copies):
    total = None
    for (start, size), copy in zip(CHUNKS, copies):
        copy.wait()
        term = dot(tokens[:, start : start + size], buffer[start : start + size, :], 1, 0)
        total = term if total is None else total + term
    return total.astype(BF16)


def store_parts(sent, at, state):
    for tile in range(TILES):
        sent[tile, at : at + PART, :] = state[tile * PART : (tile + 1) * PART, :]


def load_parts(state, got):
    for tile in range(TILES):
        state[tile * PART : (tile + 1) * PART, :] = got[tile, :PART, :]


def head(ref, index):
    return ref[index * HD : (index + 1) * HD, :]


def key_value_kernel(
    tokens, key_weight, value_weight, key, value, sent, key_buffer, value_buffer, state, total, semaphores
):
    value_copies = weight_copies(value_weight, value_buffer, semaphores, 0)
    key_copies = weight_copies(key_weight, key_buffer, semaphores, len(CHUNKS))
    for copy in value_copies + key_copies:
        copy.start()
    rows = tokens[...]
    value_rows = project(rows, value_buffer, value_copies)
    key_rows = project(rows, key_buffer, key_copies)
    for index in range(HEADS):
        part = slice(index * HD, (index + 1) * HD)
        key_head = key_rows[:, part]
        value_head = value_rows[:, part]
        key[index] = key_head
        value[index] = value_head
        positive = relu(key_head)
        state[index * HD : (index + 1) * HD, :] = dot(positive, value_head, 0, 0)
        total[index : index + 1, :] = jnp.sum(positive.astype(F32), axis=0, keepdims=True)
    store_parts(sent, 0, state)
    totals = total[...]
    for tile in range(TILES):
        sent[tile, PART : PART + HEADS, :] = totals


def query_kernel(tokens, weight, query):
    query_rows = dot(tokens[...], weight[...], 1, 0).astype(BF16)
    for index in range(HEADS):
        query[index] = query_rows[:, index * HD : (index + 1) * HD]


def inverse_denominator(positive, total):
    return 1.0 / (jnp.sum(positive * total, axis=1, keepdims=True) + EPSILON)


def numerator_kernel(loss_scale, got, query, upstream, sent, numer, total, state):
    sums = got[0]
    for tile in range(1, TILES):
        sums = sums + got[tile]
    state_part = sums[:PART]
    totals = sums[PART : PART + HEADS]
    total[...] = totals
    for index in range(HEADS):
        part = slice(index * HD, (index + 1) * HD)
        positive = relu(query[index])
        inverse = inverse_denominator(positive.astype(F32), totals[index : index + 1])
        cotangent = upstream[:, part].astype(F32) * loss_scale
        numer_low = (cotangent * inverse).astype(BF16)
        numer[index] = numer_low
        state[index * HD : (index + 1) * HD, :] = dot(positive, numer_low, 0, 0)
    for tile in range(TILES):
        sent[tile, :PART, :] = state_part
    store_parts(sent, PART, state)


def total_grad_kernel(loss_scale, got, query, upstream, total, sent, grad_denom, state, totals):
    load_parts(state, got)
    for index in range(HEADS):
        part = slice(index * HD, (index + 1) * HD)
        positive = relu(query[index])
        wide = positive.astype(F32)
        inverse = inverse_denominator(wide, total[index : index + 1, :])
        cotangent = upstream[:, part].astype(F32) * loss_scale
        product = split_dot(positive, head(state, index), 1, 0)
        grad = -(jnp.sum(cotangent * product, axis=1, keepdims=True) * inverse) * inverse
        grad_denom[:, index : index + 1] = grad
        totals[index : index + 1, :] = jnp.sum(wide * grad, axis=0, keepdims=True)
    part_sum = got[0, PART:, :]
    for tile in range(1, TILES):
        part_sum = part_sum + got[tile, PART:, :]
    values = totals[...]
    for tile in range(TILES):
        sent[tile, :PART, :] = part_sum
        sent[tile, PART : PART + HEADS, :] = values


def place_columns(place, blocks, outs, at, first=0, last=COLS):
    for slot, out in enumerate(outs):
        block = blocks[lax.rem(place[0] + slot, REPLICAS)]
        out[:, at : at + last - first] = block[:, first:last]


def split_columns(flat, blocks):
    for block in range(REPLICAS):
        blocks[block] = flat[:, block * COLS : (block + 1) * COLS]


def query_grad_kernel(
    place, got, query, numer, total, grad_denom, grad, own, first, second, third, late, state, flat, blocks
):
    load_parts(state, got)
    for index in range(HEADS):
        part = slice(index * HD, (index + 1) * HD)
        values = split_dot(numer[index], head(state, index), 1, 1)
        values = values + grad_denom[:, index : index + 1] * total[index : index + 1, :]
        values = jnp.where(query[index].astype(F32) > 0, values, 0.0).astype(BF16)
        grad[:, part] = values
        flat[:, part] = values.astype(F32)
    split_columns(flat, blocks)
    place_columns(place, blocks, (own, first, second, third), 0, 0, EARLY)
    for block in range(REPLICAS):
        late[block] = blocks[block][:, EARLY:]


def key_value_grad_kernel(got, key, value, late, grad_key, grad_value, sent, state, flat_key, flat_value):
    load_parts(state, got)
    totals = got[0, PART : PART + HEADS, :]
    for tile in range(1, TILES):
        totals = totals + got[tile, PART : PART + HEADS, :]
    for index in range(HEADS):
        part = slice(index * HD, (index + 1) * HD)
        key_head = key[index]
        positive = relu(key_head)
        state_head = head(state, index)
        values = split_dot(positive, state_head, 1, 0).astype(BF16)
        grad_value[:, part] = values
        flat_value[:, part] = values.astype(F32)
        values = split_dot(value[index], state_head, 1, 1) + totals[index : index + 1]
        values = jnp.where(key_head.astype(F32) > 0, values, 0.0).astype(BF16)
        grad_key[:, part] = values
        flat_key[:, part] = values.astype(F32)
    for block in range(REPLICAS):
        part = slice(block * COLS, (block + 1) * COLS)
        sent[block, :, :COLS] = flat_key[:, part]
        sent[block, :, COLS : 2 * COLS] = flat_value[:, part]
        sent[block, :, 2 * COLS : WIDE] = late[block]
        sent[block, :, WIDE:] = jnp.zeros((TOKENS, LANES - WIDE), F32)


def turn_kernel(core, tokens, mine, other, turned):
    for start in range(0, D, 128):
        size = min(128, D - start)
        turned[start : start + size, :] = tokens[:, start : start + size].astype(F32).T
    for half in range(CORES):
        rows = slice(half * HALF, (half + 1) * HALF)
        for out, which in ((mine, core[0]), (other, 1 - core[0])):
            start = pl.multiple_of((half * CORES + which) * HALF, 16)
            out[rows, :] = turned[pl.ds(start, HALF), :]


def join_kernel(*refs):
    for slot, part in enumerate(refs[:-1]):
        refs[-1][:, slot * TOKENS : (slot + 1) * TOKENS] = part[...].astype(BF16)


def pack_kernel(*refs):
    out = refs[-1]
    for slot, part in enumerate(refs[:-1]):
        out[slot * TOKENS : (slot + 1) * TOKENS, :] = part[...].astype(out.dtype)


def query_product_kernel(normalizer, across, rows, own, other, *refs):
    outs, columns, product = refs[:-2], refs[-2], refs[-1]
    columns[: REPLICAS * TOKENS, :] = own[...].astype(BF16)
    columns[REPLICAS * TOKENS :, :] = other[...].astype(BF16)
    span = PLANE_SIZE // CORES
    for half in range(CORES):
        values = dot(rows[half * HALF : (half + 1) * HALF, :], columns[...], 1, 0) * normalizer
        for index in range(span):
            product[half * span + index, :ROWS, :] = values[index * ROWS : (index + 1) * ROWS]
    for slot in range(RING):
        at = lax.rem(across[0] + slot, RING)
        for block in range(RING):
            values = product[(block // 2) * span + at * 2 + block % 2]
            if slot == 2:
                outs[2][block] = values[:SPLIT]
                outs[4][block] = values[SPLIT:]
            else:
                outs[slot][block] = values


def key_value_product_kernel(normalizer, place, rows, own, other, out, columns):
    @pl.when(pl.program_id(0) == 0)
    def _():
        for core, blocks in enumerate((own, other)):
            for slot in range(REPLICAS):
                at = (core * REPLICAS + slot) * TOKENS
                source = lax.rem(place[0] + REPLICAS - slot, REPLICAS)
                columns[at : at + TOKENS, :] = blocks[source].astype(BF16)

    values = dot(rows[...], columns[...], 1, 0) * normalizer
    for index in range(PLANE_SIZE // CORES):
        out[index, :ROWS, :] = values[index * ROWS : (index + 1) * ROWS]


def second_stage_kernel(along, own, first, upper, third, lower, *outs):
    for slot, out in enumerate(outs):
        at = lax.rem(along[0] + slot, RING)
        total = (own[at] + first[at]) + third[at]
        out[:SPLIT, :] = total[:SPLIT] + upper[at]
        out[SPLIT:, :] = total[SPLIT:] + lower[at]


def last_kernel(key_value, own, first, second, third, query_out, key_out, value_out):
    total = key_value[0]
    for index in range(1, PLANE_SIZE):
        total = total + key_value[index]
    key_out[...] = total[:ROWS, :COLS]
    value_out[...] = total[:ROWS, COLS : 2 * COLS]
    query_out[:, EARLY:] = total[:ROWS, 2 * COLS : WIDE]
    total = (own[...] + first[...]) + (second[...] + third[...])
    query_out[:, :EARLY] = total[:ROWS]


def exchange(blocks, axes):
    return lax.all_to_all(blocks, axes, 0, 0, tiled=True)


def shift(values, by, axis):
    return lax.ppermute(values, axis, [(i, (i + by) % RING) for i in range(RING)])


def shifted(slots, axis):
    return [slots[0]] + [shift(slots[s], s, axis) for s in range(1, RING)]


def swap_cores(values):
    return lax.ppermute(values, "core", [(0, 1), (1, 0)])


def both_cores(blocks):
    return blocks + [swap_cores(block) for block in blocks]


def back_project(gradient, weight):
    return dot(gradient, weight, 1, 1)


def body(latent, query_weight, key_weight, value_weight, upstream_grad):
    image_tokens = TOKENS * TILES
    loss_scale = 4.0 * math.sqrt(image_tokens)
    normalizer = 1.0 / math.sqrt(image_tokens * REPLICAS)
    tokens = latent.reshape(TOKENS, D)
    upstream = upstream_grad.reshape(TOKENS, HW)
    place = lax.axis_index("dp").reshape(1)
    core = lax.axis_index("core").reshape(1)
    across = lax.axis_index("x").reshape(1)
    along = lax.axis_index(("zh", "zl")).reshape(1)
    heads = shaped((HEADS, TOKENS, HD), BF16)
    flat = shaped((TOKENS, HW), BF16)
    state = pltpu.VMEM((HW, HD), F32)
    totals = pltpu.VMEM((HEADS, HD), F32)
    weight = pltpu.VMEM((D, HW), BF16)
    wide = pltpu.VMEM((TOKENS, HW), F32)
    blocks = pltpu.VMEM((REPLICAS, TOKENS, COLS), F32)

    key, value, sent = call(
        key_value_kernel,
        "key_value",
        [heads, heads, shaped((TILES, PART + HEADS, HD))],
        [BLOCK, IN_HBM, IN_HBM],
        [weight, weight, state, totals, pltpu.SemaphoreType.DMA((2 * len(CHUNKS),))],
        vmem=20,
    )(tokens, key_weight, value_weight)
    sent, later_tokens = lax.optimization_barrier((sent, tokens))
    half = shaped((D // 2, TOKENS))
    top, bottom = call(
        turn_kernel, "turn", [half, half], [IN_SMEM, BLOCK], [pltpu.VMEM((D, TOKENS), F32)]
    )(core, later_tokens)
    bottom = swap_cores(bottom)
    left_top = shift(top, 1, "dp")
    right_bottom = shift(bottom, 3, "dp")
    got = exchange(sent, IMAGE)
    (query,) = call(
        query_kernel,
        "query",
        [heads],
        [BLOCK, BLOCK],
    )(tokens, query_weight)
    sent, numer, total = call(
        lambda *refs: numerator_kernel(loss_scale, *refs),
        "numerator",
        [shaped((TILES, 2 * PART, HD)), heads, shaped((HEADS, HD))],
        [BLOCK] * 3,
        [state],
        arrived=(0, 1, 2),
    )(got, query, upstream)
    sent, left_top, right_bottom, later_top, later_bottom = lax.optimization_barrier(
        (sent, left_top, right_bottom, top, bottom)
    )
    far_top = shift(left_top, 1, "dp")
    far_bottom = shift(right_bottom, 3, "dp")
    left_bottom = shift(later_bottom, 1, "dp")
    right_top = shift(later_top, 3, "dp")
    got_state = exchange(sent, IMAGE)
    sent, grad_denom = call(
        lambda *refs: total_grad_kernel(loss_scale, *refs),
        "total_grad",
        [shaped((TILES, PART + HEADS, HD)), shaped((TOKENS, HEADS))],
        [BLOCK] * 4,
        [state, totals],
        arrived=(0, 1, 2, 3),
    )(got_state, query, upstream, total)
    sent, far_top, far_bottom, left_bottom, right_top = lax.optimization_barrier(
        (sent, far_top, far_bottom, left_bottom, right_top)
    )
    got = exchange(sent, IMAGE)

    block = shaped((TOKENS, EARLY))
    grad_query, *query_columns, late = call(
        query_grad_kernel,
        "query_grad",
        [flat, block, block, block, block, shaped((REPLICAS, TOKENS, LATE))],
        [IN_SMEM] + [BLOCK] * 5,
        [state, wide, blocks],
        arrived=(1,),
    )(place, got_state, query, numer, total, grad_denom)
    query_columns = shifted(query_columns, "dp")
    (rows,) = call(
        join_kernel,
        "join",
        [shaped((CORES * HALF, 2 * REPLICAS * TOKENS), BF16)],
        [BLOCK] * 8,
        arrived=tuple(range(1, 8)),
    )(top, left_top, far_top, right_top, bottom, left_bottom, far_bottom, right_bottom)
    (query_columns,) = call(
        pack_kernel,
        "pack_query",
        [shaped((REPLICAS * TOKENS, EARLY))],
        [BLOCK] * RING,
        arrived=(1, 2, 3),
    )(*query_columns)
    got, rows, query_columns = lax.optimization_barrier((got, rows, query_columns))

    grad_key, grad_value, sent = call(
        key_value_grad_kernel,
        "key_value_grad",
        [flat, flat, shaped((REPLICAS, TOKENS, LANES))],
        [BLOCK] * 4,
        [state, wide, wide],
        arrived=(0, 1, 2, 3),
    )(got, key, value, late)
    own_columns = exchange(sent, "dp")
    slots = call(
        lambda *refs: query_product_kernel(normalizer, *refs[:4], *refs[5:]),
        "query_product",
        [
            shaped((RING, SPLIT if slot == 2 else PADDED_ROWS, EARLY))
            for slot in range(RING)
        ]
        + [shaped((RING, PADDED_ROWS - SPLIT, EARLY))],
        [IN_SMEM, BLOCK, BLOCK, BLOCK, ANYWHERE],
        [
            pltpu.VMEM((2 * REPLICAS * TOKENS, EARLY), BF16),
            pltpu.VMEM((PLANE_SIZE, PADDED_ROWS, EARLY), F32),
        ],
        vmem=24,
        arrived=(3,),
    )(across, rows, query_columns, swap_cores(query_columns), sent)
    upper, lower = slots[2], slots[4]
    lower = shift(shift(lower, 3, "x"), 3, "x")
    slots = [slots[0], shift(slots[1], 1, "x"), shift(upper, 2, "x"), shift(slots[3], 3, "x"), lower]
    own_columns, slots = lax.optimization_barrier((own_columns, slots))
    slots = call(
        second_stage_kernel,
        "second_stage",
        [shaped((PADDED_ROWS, EARLY))] * RING,
        [IN_SMEM] + [BLOCK] * (RING + 1),
        arrived=(2, 3, 4, 5),
    )(along, *slots)
    (product,) = call(
        lambda *refs: key_value_product_kernel(normalizer, *refs[:4], *refs[5:]),
        "key_value_product",
        [shaped((PLANE_SIZE, PADDED_ROWS, LANES))],
        [
            IN_SMEM,
            pl.BlockSpec((HALF, 2 * REPLICAS * TOKENS), lambda half: (half, 0)),
            BLOCK,
            BLOCK,
            ANYWHERE,
        ],
        [pltpu.VMEM((2 * REPLICAS * TOKENS, LANES), BF16)],
        vmem=24,
        arrived=(2, 3),
        steps=CORES,
        out_specs=[
            pl.BlockSpec((PLANE_SIZE // CORES, PADDED_ROWS, LANES), lambda half: (half, 0, 0))
        ],
    )(place, rows, own_columns, swap_cores(own_columns), slots[0])
    key_value_out = exchange(product, PLANE)
    slots = shifted(slots, ("zh", "zl"))
    block = shaped((ROWS, COLS))
    query_out, key_out, value_out = call(
        last_kernel, "last", [block] * 3, [BLOCK] * 5, arrived=(0, 2, 3, 4)
    )(key_value_out, *slots)

    summed = back_project(grad_query, query_weight) + back_project(grad_key, key_weight)
    summed = summed + back_project(grad_value, value_weight)
    latent_grad = summed.astype(BF16).reshape(latent.shape)
    return latent_grad, query_out, key_out, value_out


def solution(mesh):
    devices = mesh.devices
    fine = Mesh(
        devices.reshape(REPLICAS, 2, CORES, 4, 2), ("dp", "zh", "core", "x", "zl")
    )
    grid = P("dp", ("zh", "core"), ("x", "zl"), None)
    weight_out = P(("zh", "core", "x", "zl"), "dp")
    return jax.shard_map(
        body,
        mesh=fine,
        in_specs=(grid, P(), P(), P(), grid),
        out_specs=(grid, weight_out, weight_out, weight_out),
        check_vma=False,
    )
```

```python
import math

import jax
import jax.numpy as jnp
from jax import lax
from jax.experimental import pallas as pl
from jax.experimental.pallas import tpu as pltpu
from jax.sharding import Mesh, PartitionSpec as P

D = 2240
HD = 112
HEADS = 10
HW = HEADS * HD
TILES = 32
PART = HW // TILES
PLANE_SIZE = 16
CORES = 2
ROWS = D // TILES
PADDED_ROWS = 72
HALF = D // 4
REPLICAS = 4
RING = 4
COLS = HW // REPLICAS
EARLY = 256
LATE = COLS - EARLY
WIDE = 2 * COLS + LATE
LANES = 640
TOKENS = 128

EPSILON = 1e-15
IMAGE = ("zh", "core", "x", "zl")
PLANE = ("zh", "x", "zl")
CHUNKS = [(0, 1152), (1152, D - 1152)]

F32 = jnp.float32
BF16 = jnp.bfloat16
BLOCK = pl.BlockSpec()
IN_SMEM = pl.BlockSpec(memory_space=pltpu.SMEM)
ANYWHERE = pl.BlockSpec(memory_space=pl.ANY)
IN_HBM = pl.BlockSpec(memory_space=pltpu.HBM)


def shaped(shape, dtype=F32):
    return pltpu.HBM(shape, dtype)


def call(kernel, name, outs, in_specs, scratch=(), vmem=12, arrived=(), steps=1, out_specs=None):
    run = pl.pallas_call(
        kernel,
        name=name,
        grid=(steps,),
        out_shape=outs,
        in_specs=in_specs,
        out_specs=out_specs or [BLOCK] * len(outs),
        scratch_shapes=list(scratch),
        compiler_params=pltpu.CompilerParams(vmem_limit_bytes=vmem * 1024 * 1024),
    )

    def with_placed(*operands):
        placed = [
            operand
            if spec is IN_SMEM or index in arrived
            else pltpu.with_memory_space_constraint(operand, pltpu.HBM)
            for index, (operand, spec) in enumerate(zip(operands, in_specs))
        ]
        return run(*placed)

    return with_placed


def dot(left, right, left_dim, right_dim):
    return lax.dot_general(
        left, right, (((left_dim,), (right_dim,)), ((), ())), preferred_element_type=F32
    )


def split_dot(left, right, left_dim, right_dim):
    high = right.astype(BF16)
    low = (right - high.astype(F32)).astype(BF16)
    return dot(left, high, left_dim, right_dim) + dot(left, low, left_dim, right_dim)


def relu(values):
    return jnp.maximum(values, jnp.zeros_like(values))


def weight_copies(weight, buffer, semaphores, first):
    copies = []
    for index, (start, size) in enumerate(CHUNKS):
        copies.append(
            pltpu.make_async_copy(
                weight.at[pl.ds(start, size)],
                buffer.at[pl.ds(start, size)],
                semaphores.at[first + index],
            )
        )
    return copies


def project(tokens, buffer, copies):
    total = None
    for (start, size), copy in zip(CHUNKS, copies):
        copy.wait()
        term = dot(tokens[:, start : start + size], buffer[start : start + size, :], 1, 0)
        total = term if total is None else total + term
    return total.astype(BF16)


def store_parts(sent, at, state):
    for tile in range(TILES):
        sent[tile, at : at + PART, :] = state[tile * PART : (tile + 1) * PART, :]


def load_parts(state, got):
    for tile in range(TILES):
        state[tile * PART : (tile + 1) * PART, :] = got[tile, :PART, :]


def head(ref, index):
    return ref[index * HD : (index + 1) * HD, :]


def key_value_kernel(
    tokens, key_weight, value_weight, key, value, sent, key_buffer, value_buffer, state, total, semaphores
):
    value_copies = weight_copies(value_weight, value_buffer, semaphores, 0)
    key_copies = weight_copies(key_weight, key_buffer, semaphores, len(CHUNKS))
    for copy in value_copies + key_copies:
        copy.start()
    rows = tokens[...]
    value_rows = project(rows, value_buffer, value_copies)
    key_rows = project(rows, key_buffer, key_copies)
    for index in range(HEADS):
        part = slice(index * HD, (index + 1) * HD)
        key_head = key_rows[:, part]
        value_head = value_rows[:, part]
        key[index] = key_head
        value[index] = value_head
        positive = relu(key_head)
        state[index * HD : (index + 1) * HD, :] = dot(positive, value_head, 0, 0)
        total[index : index + 1, :] = jnp.sum(positive.astype(F32), axis=0, keepdims=True)
    store_parts(sent, 0, state)
    totals = total[...]
    for tile in range(TILES):
        sent[tile, PART : PART + HEADS, :] = totals


def query_kernel(tokens, weight, query):
    query_rows = dot(tokens[...], weight[...], 1, 0).astype(BF16)
    for index in range(HEADS):
        query[index] = query_rows[:, index * HD : (index + 1) * HD]


def inverse_denominator(positive, total):
    return 1.0 / (jnp.sum(positive * total, axis=1, keepdims=True) + EPSILON)


def numerator_kernel(loss_scale, got, query, upstream, sent, numer, total, state):
    sums = got[0]
    for tile in range(1, TILES):
        sums = sums + got[tile]
    state_part = sums[:PART]
    totals = sums[PART : PART + HEADS]
    total[...] = totals
    for index in range(HEADS):
        part = slice(index * HD, (index + 1) * HD)
        positive = relu(query[index])
        inverse = inverse_denominator(positive.astype(F32), totals[index : index + 1])
        cotangent = upstream[:, part].astype(F32) * loss_scale
        numer_low = (cotangent * inverse).astype(BF16)
        numer[index] = numer_low
        state[index * HD : (index + 1) * HD, :] = dot(positive, numer_low, 0, 0)
    for tile in range(TILES):
        sent[tile, :PART, :] = state_part
    store_parts(sent, PART, state)


def total_grad_kernel(loss_scale, got, query, upstream, total, sent, grad_denom, state, totals):
    load_parts(state, got)
    for index in range(HEADS):
        part = slice(index * HD, (index + 1) * HD)
        positive = relu(query[index])
        wide = positive.astype(F32)
        inverse = inverse_denominator(wide, total[index : index + 1, :])
        cotangent = upstream[:, part].astype(F32) * loss_scale
        product = split_dot(positive, head(state, index), 1, 0)
        grad = -(jnp.sum(cotangent * product, axis=1, keepdims=True) * inverse) * inverse
        grad_denom[:, index : index + 1] = grad
        totals[index : index + 1, :] = jnp.sum(wide * grad, axis=0, keepdims=True)
    part_sum = got[0, PART:, :]
    for tile in range(1, TILES):
        part_sum = part_sum + got[tile, PART:, :]
    values = totals[...]
    for tile in range(TILES):
        sent[tile, :PART, :] = part_sum
        sent[tile, PART : PART + HEADS, :] = values


def place_columns(place, blocks, outs, at, first=0, last=COLS):
    for slot, out in enumerate(outs):
        block = blocks[lax.rem(place[0] + slot, REPLICAS)]
        out[:, at : at + last - first] = block[:, first:last]


def split_columns(flat, blocks):
    for block in range(REPLICAS):
        blocks[block] = flat[:, block * COLS : (block + 1) * COLS]


def query_grad_kernel(
    place, got, query, numer, total, grad_denom, grad, own, first, second, third, late, state, flat, blocks
):
    load_parts(state, got)
    for index in range(HEADS):
        part = slice(index * HD, (index + 1) * HD)
        values = split_dot(numer[index], head(state, index), 1, 1)
        values = values + grad_denom[:, index : index + 1] * total[index : index + 1, :]
        values = jnp.where(query[index].astype(F32) > 0, values, 0.0).astype(BF16)
        grad[:, part] = values
        flat[:, part] = values.astype(F32)
    split_columns(flat, blocks)
    place_columns(place, blocks, (own, first, second, third), 0, 0, EARLY)
    for block in range(REPLICAS):
        late[block] = blocks[block][:, EARLY:]


def key_value_grad_kernel(got, key, value, late, grad_key, grad_value, sent, state, flat_key, flat_value):
    load_parts(state, got)
    totals = got[0, PART : PART + HEADS, :]
    for tile in range(1, TILES):
        totals = totals + got[tile, PART : PART + HEADS, :]
    for index in range(HEADS):
        part = slice(index * HD, (index + 1) * HD)
        key_head = key[index]
        positive = relu(key_head)
        state_head = head(state, index)
        values = split_dot(positive, state_head, 1, 0).astype(BF16)
        grad_value[:, part] = values
        flat_value[:, part] = values.astype(F32)
        values = split_dot(value[index], state_head, 1, 1) + totals[index : index + 1]
        values = jnp.where(key_head.astype(F32) > 0, values, 0.0).astype(BF16)
        grad_key[:, part] = values
        flat_key[:, part] = values.astype(F32)
    for block in range(REPLICAS):
        part = slice(block * COLS, (block + 1) * COLS)
        sent[block, :, :COLS] = flat_key[:, part]
        sent[block, :, COLS : 2 * COLS] = flat_value[:, part]
        sent[block, :, 2 * COLS : WIDE] = late[block]
        sent[block, :, WIDE:] = jnp.zeros((TOKENS, LANES - WIDE), F32)


def turn_kernel(core, tokens, mine, other, turned):
    for start in range(0, D, 128):
        size = min(128, D - start)
        turned[start : start + size, :] = tokens[:, start : start + size].astype(F32).T
    for half in range(CORES):
        rows = slice(half * HALF, (half + 1) * HALF)
        for out, which in ((mine, core[0]), (other, 1 - core[0])):
            start = pl.multiple_of((half * CORES + which) * HALF, 16)
            out[rows, :] = turned[pl.ds(start, HALF), :]


def join_kernel(*refs):
    for slot, part in enumerate(refs[:-1]):
        refs[-1][:, slot * TOKENS : (slot + 1) * TOKENS] = part[...].astype(BF16)


def pack_kernel(*refs):
    out = refs[-1]
    for slot, part in enumerate(refs[:-1]):
        out[slot * TOKENS : (slot + 1) * TOKENS, :] = part[...].astype(out.dtype)


def query_product_kernel(normalizer, across, rows, own, other, *refs):
    outs, columns, product = refs[:-2], refs[-2], refs[-1]
    columns[: REPLICAS * TOKENS, :] = own[...].astype(BF16)
    columns[REPLICAS * TOKENS :, :] = other[...].astype(BF16)
    span = PLANE_SIZE // CORES
    for half in range(CORES):
        values = dot(rows[half * HALF : (half + 1) * HALF, :], columns[...], 1, 0) * normalizer
        for index in range(span):
            product[half * span + index, :ROWS, :] = values[index * ROWS : (index + 1) * ROWS]
    for slot, out in enumerate(outs):
        at = lax.rem(across[0] + slot, RING)
        for block in range(RING):
            out[block] = product[(block // 2) * span + at * 2 + block % 2]


def key_value_product_kernel(normalizer, place, rows, own, other, out, columns):
    @pl.when(pl.program_id(0) == 0)
    def _():
        for core, blocks in enumerate((own, other)):
            for slot in range(REPLICAS):
                at = (core * REPLICAS + slot) * TOKENS
                source = lax.rem(place[0] + REPLICAS - slot, REPLICAS)
                columns[at : at + TOKENS, :] = blocks[source].astype(BF16)

    values = dot(rows[...], columns[...], 1, 0) * normalizer
    for index in range(PLANE_SIZE // CORES):
        out[index, :ROWS, :] = values[index * ROWS : (index + 1) * ROWS]


def second_stage_kernel(along, own, first, second, third, *outs):
    for slot, out in enumerate(outs):
        at = lax.rem(along[0] + slot, RING)
        out[...] = (own[at] + first[at]) + (second[at] + third[at])


def last_kernel(key_value, own, first, second, third, query_out, key_out, value_out):
    total = key_value[0]
    for index in range(1, PLANE_SIZE):
        total = total + key_value[index]
    key_out[...] = total[:ROWS, :COLS]
    value_out[...] = total[:ROWS, COLS : 2 * COLS]
    query_out[:, EARLY:] = total[:ROWS, 2 * COLS : WIDE]
    total = (own[...] + first[...]) + (second[...] + third[...])
    query_out[:, :EARLY] = total[:ROWS]


def exchange(blocks, axes):
    return lax.all_to_all(blocks, axes, 0, 0, tiled=True)


def shift(values, by, axis):
    return lax.ppermute(values, axis, [(i, (i + by) % RING) for i in range(RING)])


def shifted(slots, axis):
    return [slots[0]] + [shift(slots[s], s, axis) for s in range(1, RING)]


def swap_cores(values):
    return lax.ppermute(values, "core", [(0, 1), (1, 0)])


def both_cores(blocks):
    return blocks + [swap_cores(block) for block in blocks]


def back_project(gradient, weight):
    return dot(gradient, weight, 1, 1)


def body(latent, query_weight, key_weight, value_weight, upstream_grad):
    image_tokens = TOKENS * TILES
    loss_scale = 4.0 * math.sqrt(image_tokens)
    normalizer = 1.0 / math.sqrt(image_tokens * REPLICAS)
    tokens = latent.reshape(TOKENS, D)
    upstream = upstream_grad.reshape(TOKENS, HW)
    place = lax.axis_index("dp").reshape(1)
    core = lax.axis_index("core").reshape(1)
    across = lax.axis_index("x").reshape(1)
    along = lax.axis_index(("zh", "zl")).reshape(1)
    heads = shaped((HEADS, TOKENS, HD), BF16)
    flat = shaped((TOKENS, HW), BF16)
    state = pltpu.VMEM((HW, HD), F32)
    totals = pltpu.VMEM((HEADS, HD), F32)
    weight = pltpu.VMEM((D, HW), BF16)
    wide = pltpu.VMEM((TOKENS, HW), F32)
    blocks = pltpu.VMEM((REPLICAS, TOKENS, COLS), F32)

    key, value, sent = call(
        key_value_kernel,
        "key_value",
        [heads, heads, shaped((TILES, PART + HEADS, HD))],
        [BLOCK, IN_HBM, IN_HBM],
        [weight, weight, state, totals, pltpu.SemaphoreType.DMA((2 * len(CHUNKS),))],
        vmem=20,
    )(tokens, key_weight, value_weight)
    sent, later_tokens = lax.optimization_barrier((sent, tokens))
    half = shaped((D // 2, TOKENS))
    top, bottom = call(
        turn_kernel, "turn", [half, half], [IN_SMEM, BLOCK], [pltpu.VMEM((D, TOKENS), F32)]
    )(core, later_tokens)
    bottom = swap_cores(bottom)
    left_top = shift(top, 1, "dp")
    right_bottom = shift(bottom, 3, "dp")
    got = exchange(sent, IMAGE)
    (query,) = call(
        query_kernel,
        "query",
        [heads],
        [BLOCK, BLOCK],
    )(tokens, query_weight)
    sent, numer, total = call(
        lambda *refs: numerator_kernel(loss_scale, *refs),
        "numerator",
        [shaped((TILES, 2 * PART, HD)), heads, shaped((HEADS, HD))],
        [BLOCK] * 3,
        [state],
        arrived=(0, 1, 2),
    )(got, query, upstream)
    sent, left_top, right_bottom, later_top, later_bottom = lax.optimization_barrier(
        (sent, left_top, right_bottom, top, bottom)
    )
    far_top = shift(left_top, 1, "dp")
    far_bottom = shift(right_bottom, 3, "dp")
    left_bottom = shift(later_bottom, 1, "dp")
    right_top = shift(later_top, 3, "dp")
    got_state = exchange(sent, IMAGE)
    sent, grad_denom = call(
        lambda *refs: total_grad_kernel(loss_scale, *refs[:4], *refs[6:]),
        "total_grad",
        [shaped((TILES, PART + HEADS, HD)), shaped((TOKENS, HEADS))],
        [BLOCK] * 4 + [ANYWHERE] * 2,
        [state, totals],
        arrived=(0, 1, 2, 3, 4, 5),
    )(got_state, query, upstream, total, swap_cores(left_bottom), swap_cores(right_top))
    sent, far_top, far_bottom, left_bottom, right_top = lax.optimization_barrier(
        (sent, far_top, far_bottom, left_bottom, right_top)
    )
    got = exchange(sent, IMAGE)

    block = shaped((TOKENS, EARLY))
    grad_query, *query_columns, late = call(
        query_grad_kernel,
        "query_grad",
        [flat, block, block, block, block, shaped((REPLICAS, TOKENS, LATE))],
        [IN_SMEM] + [BLOCK] * 5,
        [state, wide, blocks],
        arrived=(1,),
    )(place, got_state, query, numer, total, grad_denom)
    query_columns = shifted(query_columns, "dp")
    (rows,) = call(
        join_kernel,
        "join",
        [shaped((CORES * HALF, 2 * REPLICAS * TOKENS), BF16)],
        [BLOCK] * 8,
        arrived=tuple(range(1, 8)),
    )(top, left_top, far_top, right_top, bottom, left_bottom, far_bottom, right_bottom)
    (query_columns,) = call(
        pack_kernel,
        "pack_query",
        [shaped((REPLICAS * TOKENS, EARLY))],
        [BLOCK] * RING,
        arrived=(1, 2, 3),
    )(*query_columns)
    got, rows, query_columns = lax.optimization_barrier((got, rows, query_columns))

    grad_key, grad_value, sent = call(
        key_value_grad_kernel,
        "key_value_grad",
        [flat, flat, shaped((REPLICAS, TOKENS, LANES))],
        [BLOCK] * 4,
        [state, wide, wide],
        arrived=(0, 1, 2, 3),
    )(got, key, value, late)
    own_columns = exchange(sent, "dp")
    slots = call(
        lambda *refs: query_product_kernel(normalizer, *refs[:4], *refs[5:]),
        "query_product",
        [shaped((RING, PADDED_ROWS, EARLY))] * RING,
        [IN_SMEM, BLOCK, BLOCK, BLOCK, ANYWHERE],
        [
            pltpu.VMEM((2 * REPLICAS * TOKENS, EARLY), BF16),
            pltpu.VMEM((PLANE_SIZE, PADDED_ROWS, EARLY), F32),
        ],
        vmem=24,
        arrived=(3,),
    )(across, rows, query_columns, swap_cores(query_columns), sent)
    slots = shifted(slots, "x")
    own_columns, slots = lax.optimization_barrier((own_columns, slots))
    slots = call(
        second_stage_kernel,
        "second_stage",
        [shaped((PADDED_ROWS, EARLY))] * RING,
        [IN_SMEM] + [BLOCK] * RING,
        arrived=(2, 3, 4),
    )(along, *slots)
    (product,) = call(
        lambda *refs: key_value_product_kernel(normalizer, *refs[:4], *refs[5:]),
        "key_value_product",
        [shaped((PLANE_SIZE, PADDED_ROWS, LANES))],
        [
            IN_SMEM,
            pl.BlockSpec((HALF, 2 * REPLICAS * TOKENS), lambda half: (half, 0)),
            BLOCK,
            BLOCK,
            ANYWHERE,
        ],
        [pltpu.VMEM((2 * REPLICAS * TOKENS, LANES), BF16)],
        vmem=24,
        arrived=(2, 3),
        steps=CORES,
        out_specs=[
            pl.BlockSpec((PLANE_SIZE // CORES, PADDED_ROWS, LANES), lambda half: (half, 0, 0))
        ],
    )(place, rows, own_columns, swap_cores(own_columns), slots[0])
    key_value_out = exchange(product, PLANE)
    slots = shifted(slots, ("zh", "zl"))
    block = shaped((ROWS, COLS))
    query_out, key_out, value_out = call(
        last_kernel, "last", [block] * 3, [BLOCK] * 5, arrived=(0, 2, 3, 4)
    )(key_value_out, *slots)

    summed = back_project(grad_query, query_weight) + back_project(grad_key, key_weight)
    summed = summed + back_project(grad_value, value_weight)
    latent_grad = summed.astype(BF16).reshape(latent.shape)
    return latent_grad, query_out, key_out, value_out


def solution(mesh):
    devices = mesh.devices
    fine = Mesh(
        devices.reshape(REPLICAS, 2, CORES, 4, 2), ("dp", "zh", "core", "x", "zl")
    )
    grid = P("dp", ("zh", "core"), ("x", "zl"), None)
    weight_out = P(("zh", "core", "x", "zl"), "dp")
    return jax.shard_map(
        body,
        mesh=fine,
        in_specs=(grid, P(), P(), P(), grid),
        out_specs=(grid, weight_out, weight_out, weight_out),
        check_vma=False,
    )
```

```python
import math

import jax
import jax.numpy as jnp
from jax import lax
from jax.experimental import pallas as pl
from jax.experimental.pallas import tpu as pltpu
from jax.sharding import Mesh, PartitionSpec as P

D = 2240
HD = 112
HEADS = 10
HW = HEADS * HD
TILES = 32
PART = HW // TILES
PLANE_SIZE = 16
CORES = 2
ROWS = D // TILES
PADDED_ROWS = 72
HALF = D // 4
REPLICAS = 4
RING = 4
COLS = HW // REPLICAS
EARLY = 256
LATE = COLS - EARLY
WIDE = 2 * COLS + LATE
LANES = 640
TOKENS = 128

EPSILON = 1e-15
IMAGE = ("zh", "core", "x", "zl")
PLANE = ("zh", "x", "zl")
CHUNKS = [(0, 1152), (1152, D - 1152)]

F32 = jnp.float32
BF16 = jnp.bfloat16
BLOCK = pl.BlockSpec()
IN_SMEM = pl.BlockSpec(memory_space=pltpu.SMEM)
ANYWHERE = pl.BlockSpec(memory_space=pl.ANY)
IN_HBM = pl.BlockSpec(memory_space=pltpu.HBM)


def shaped(shape, dtype=F32):
    return pltpu.HBM(shape, dtype)


def call(kernel, name, outs, in_specs, scratch=(), vmem=12, arrived=(), steps=1, out_specs=None):
    run = pl.pallas_call(
        kernel,
        name=name,
        grid=(steps,),
        out_shape=outs,
        in_specs=in_specs,
        out_specs=out_specs or [BLOCK] * len(outs),
        scratch_shapes=list(scratch),
        compiler_params=pltpu.CompilerParams(vmem_limit_bytes=vmem * 1024 * 1024),
    )

    def with_placed(*operands):
        placed = [
            operand
            if spec is IN_SMEM or index in arrived
            else pltpu.with_memory_space_constraint(operand, pltpu.HBM)
            for index, (operand, spec) in enumerate(zip(operands, in_specs))
        ]
        return run(*placed)

    return with_placed


def dot(left, right, left_dim, right_dim):
    return lax.dot_general(
        left, right, (((left_dim,), (right_dim,)), ((), ())), preferred_element_type=F32
    )


def split_dot(left, right, left_dim, right_dim):
    high = right.astype(BF16)
    low = (right - high.astype(F32)).astype(BF16)
    return dot(left, high, left_dim, right_dim) + dot(left, low, left_dim, right_dim)


def relu(values):
    return jnp.maximum(values, jnp.zeros_like(values))


def weight_copies(weight, buffer, semaphores, first):
    copies = []
    for index, (start, size) in enumerate(CHUNKS):
        copies.append(
            pltpu.make_async_copy(
                weight.at[pl.ds(start, size)],
                buffer.at[pl.ds(start, size)],
                semaphores.at[first + index],
            )
        )
    return copies


def project(tokens, buffer, copies):
    total = None
    for (start, size), copy in zip(CHUNKS, copies):
        copy.wait()
        term = dot(tokens[:, start : start + size], buffer[start : start + size, :], 1, 0)
        total = term if total is None else total + term
    return total.astype(BF16)


def store_parts(sent, at, state):
    for tile in range(TILES):
        sent[tile, at : at + PART, :] = state[tile * PART : (tile + 1) * PART, :]


def load_parts(state, got):
    for tile in range(TILES):
        state[tile * PART : (tile + 1) * PART, :] = got[tile, :PART, :]


def head(ref, index):
    return ref[index * HD : (index + 1) * HD, :]


def key_value_kernel(
    tokens, key_weight, value_weight, key, value, sent, key_buffer, value_buffer, state, total, semaphores
):
    value_copies = weight_copies(value_weight, value_buffer, semaphores, 0)
    key_copies = weight_copies(key_weight, key_buffer, semaphores, len(CHUNKS))
    for copy in value_copies + key_copies:
        copy.start()
    rows = tokens[...]
    value_rows = project(rows, value_buffer, value_copies)
    key_rows = project(rows, key_buffer, key_copies)
    for index in range(HEADS):
        part = slice(index * HD, (index + 1) * HD)
        key_head = key_rows[:, part]
        value_head = value_rows[:, part]
        key[index] = key_head
        value[index] = value_head
        positive = relu(key_head)
        state[index * HD : (index + 1) * HD, :] = dot(positive, value_head, 0, 0)
        total[index : index + 1, :] = jnp.sum(positive.astype(F32), axis=0, keepdims=True)
    store_parts(sent, 0, state)
    totals = total[...]
    for tile in range(TILES):
        sent[tile, PART : PART + HEADS, :] = totals


def query_kernel(tokens, weight, query):
    query_rows = dot(tokens[...], weight[...], 1, 0).astype(BF16)
    for index in range(HEADS):
        query[index] = query_rows[:, index * HD : (index + 1) * HD]


def inverse_denominator(positive, total):
    return 1.0 / (jnp.sum(positive * total, axis=1, keepdims=True) + EPSILON)


def numerator_kernel(loss_scale, got, query, upstream, sent, numer, total, state):
    sums = got[0]
    for tile in range(1, TILES):
        sums = sums + got[tile]
    state_part = sums[:PART]
    totals = sums[PART : PART + HEADS]
    total[...] = totals
    for index in range(HEADS):
        part = slice(index * HD, (index + 1) * HD)
        positive = relu(query[index])
        inverse = inverse_denominator(positive.astype(F32), totals[index : index + 1])
        cotangent = upstream[:, part].astype(F32) * loss_scale
        numer_low = (cotangent * inverse).astype(BF16)
        numer[index] = numer_low
        state[index * HD : (index + 1) * HD, :] = dot(positive, numer_low, 0, 0)
    for tile in range(TILES):
        sent[tile, :PART, :] = state_part
    store_parts(sent, PART, state)


def total_grad_kernel(loss_scale, got, query, upstream, total, sent, grad_denom, state, totals):
    load_parts(state, got)
    for index in range(HEADS):
        part = slice(index * HD, (index + 1) * HD)
        positive = relu(query[index])
        wide = positive.astype(F32)
        inverse = inverse_denominator(wide, total[index : index + 1, :])
        cotangent = upstream[:, part].astype(F32) * loss_scale
        product = split_dot(positive, head(state, index), 1, 0)
        grad = -(jnp.sum(cotangent * product, axis=1, keepdims=True) * inverse) * inverse
        grad_denom[:, index : index + 1] = grad
        totals[index : index + 1, :] = jnp.sum(wide * grad, axis=0, keepdims=True)
    part_sum = got[0, PART:, :]
    for tile in range(1, TILES):
        part_sum = part_sum + got[tile, PART:, :]
    values = totals[...]
    for tile in range(TILES):
        sent[tile, :PART, :] = part_sum
        sent[tile, PART : PART + HEADS, :] = values


def place_columns(place, blocks, outs, at, first=0, last=COLS):
    for slot, out in enumerate(outs):
        block = blocks[lax.rem(place[0] + slot, REPLICAS)]
        out[:, at : at + last - first] = block[:, first:last]


def split_columns(flat, blocks):
    for block in range(REPLICAS):
        blocks[block] = flat[:, block * COLS : (block + 1) * COLS]


def query_grad_kernel(
    place, got, query, numer, total, grad_denom, grad, own, first, second, third, late, state, flat, blocks
):
    load_parts(state, got)
    for index in range(HEADS):
        part = slice(index * HD, (index + 1) * HD)
        values = split_dot(numer[index], head(state, index), 1, 1)
        values = values + grad_denom[:, index : index + 1] * total[index : index + 1, :]
        values = jnp.where(query[index].astype(F32) > 0, values, 0.0).astype(BF16)
        grad[:, part] = values
        flat[:, part] = values.astype(F32)
    split_columns(flat, blocks)
    place_columns(place, blocks, (own, first, second, third), 0, 0, EARLY)
    for block in range(REPLICAS):
        late[block] = blocks[block][:, EARLY:]


def key_value_grad_kernel(got, key, value, late, grad_key, grad_value, sent, state, flat_key, flat_value):
    load_parts(state, got)
    totals = got[0, PART : PART + HEADS, :]
    for tile in range(1, TILES):
        totals = totals + got[tile, PART : PART + HEADS, :]
    for index in range(HEADS):
        part = slice(index * HD, (index + 1) * HD)
        key_head = key[index]
        positive = relu(key_head)
        state_head = head(state, index)
        values = split_dot(positive, state_head, 1, 0).astype(BF16)
        grad_value[:, part] = values
        flat_value[:, part] = values.astype(F32)
        values = split_dot(value[index], state_head, 1, 1) + totals[index : index + 1]
        values = jnp.where(key_head.astype(F32) > 0, values, 0.0).astype(BF16)
        grad_key[:, part] = values
        flat_key[:, part] = values.astype(F32)
    for block in range(REPLICAS):
        part = slice(block * COLS, (block + 1) * COLS)
        sent[block, :, :COLS] = flat_key[:, part]
        sent[block, :, COLS : 2 * COLS] = flat_value[:, part]
        sent[block, :, 2 * COLS : WIDE] = late[block]
        sent[block, :, WIDE:] = jnp.zeros((TOKENS, LANES - WIDE), F32)


def turn_kernel(core, tokens, mine, other, turned):
    for start in range(0, D, 128):
        size = min(128, D - start)
        turned[start : start + size, :] = tokens[:, start : start + size].astype(F32).T
    for half in range(CORES):
        rows = slice(half * HALF, (half + 1) * HALF)
        for out, which in ((mine, core[0]), (other, 1 - core[0])):
            start = pl.multiple_of((half * CORES + which) * HALF, 16)
            out[rows, :] = turned[pl.ds(start, HALF), :]


def join_kernel(*refs):
    for slot, part in enumerate(refs[:-1]):
        refs[-1][:, slot * TOKENS : (slot + 1) * TOKENS] = part[...].astype(BF16)


def pack_kernel(*refs):
    out = refs[-1]
    for slot, part in enumerate(refs[:-1]):
        out[slot * TOKENS : (slot + 1) * TOKENS, :] = part[...].astype(out.dtype)


def query_product_kernel(normalizer, across, rows, own, other, *refs):
    outs, columns, product = refs[:-2], refs[-2], refs[-1]

    @pl.when(pl.program_id(0) == 0)
    def _():
        columns[: REPLICAS * TOKENS, :] = own[...].astype(BF16)
        columns[REPLICAS * TOKENS :, :] = other[...].astype(BF16)

    values = dot(rows[...], columns[...], 1, 0) * normalizer
    for index in range(PLANE_SIZE // CORES):
        product[index, :ROWS, :] = values[index * ROWS : (index + 1) * ROWS]
    for slot, out in enumerate(outs):
        at = lax.rem(across[0] + slot, RING)
        for block in range(2):
            out[block] = product[at * 2 + block]


def key_value_product_kernel(normalizer, place, rows, own, other, out, columns):
    @pl.when(pl.program_id(0) == 0)
    def _():
        for core, blocks in enumerate((own, other)):
            for slot in range(REPLICAS):
                at = (core * REPLICAS + slot) * TOKENS
                source = lax.rem(place[0] + REPLICAS - slot, REPLICAS)
                columns[at : at + TOKENS, :] = blocks[source].astype(BF16)

    values = dot(rows[...], columns[...], 1, 0) * normalizer
    for index in range(PLANE_SIZE // CORES):
        out[index, :ROWS, :] = values[index * ROWS : (index + 1) * ROWS]


def second_stage_kernel(along, own, first, second, third, *outs):
    for slot, out in enumerate(outs):
        at = lax.rem(along[0] + slot, RING)
        out[...] = (own[at] + first[at]) + (second[at] + third[at])


def last_kernel(key_value, own, first, second, third, query_out, key_out, value_out):
    total = key_value[0]
    for index in range(1, PLANE_SIZE):
        total = total + key_value[index]
    key_out[...] = total[:ROWS, :COLS]
    value_out[...] = total[:ROWS, COLS : 2 * COLS]
    query_out[:, EARLY:] = total[:ROWS, 2 * COLS : WIDE]
    total = (own[...] + first[...]) + (second[...] + third[...])
    query_out[:, :EARLY] = total[:ROWS]


def exchange(blocks, axes):
    return lax.all_to_all(blocks, axes, 0, 0, tiled=True)


def shift(values, by, axis):
    return lax.ppermute(values, axis, [(i, (i + by) % RING) for i in range(RING)])


def shifted(slots, axis):
    return [slots[0]] + [shift(slots[s], s, axis) for s in range(1, RING)]


def swap_cores(values):
    return lax.ppermute(values, "core", [(0, 1), (1, 0)])


def both_cores(blocks):
    return blocks + [swap_cores(block) for block in blocks]


def back_project(gradient, weight):
    return dot(gradient, weight, 1, 1)


def body(latent, query_weight, key_weight, value_weight, upstream_grad):
    image_tokens = TOKENS * TILES
    loss_scale = 4.0 * math.sqrt(image_tokens)
    normalizer = 1.0 / math.sqrt(image_tokens * REPLICAS)
    tokens = latent.reshape(TOKENS, D)
    upstream = upstream_grad.reshape(TOKENS, HW)
    place = lax.axis_index("dp").reshape(1)
    core = lax.axis_index("core").reshape(1)
    across = lax.axis_index("x").reshape(1)
    along = lax.axis_index(("zh", "zl")).reshape(1)
    heads = shaped((HEADS, TOKENS, HD), BF16)
    flat = shaped((TOKENS, HW), BF16)
    state = pltpu.VMEM((HW, HD), F32)
    totals = pltpu.VMEM((HEADS, HD), F32)
    weight = pltpu.VMEM((D, HW), BF16)
    wide = pltpu.VMEM((TOKENS, HW), F32)
    blocks = pltpu.VMEM((REPLICAS, TOKENS, COLS), F32)

    key, value, sent = call(
        key_value_kernel,
        "key_value",
        [heads, heads, shaped((TILES, PART + HEADS, HD))],
        [BLOCK, IN_HBM, IN_HBM],
        [weight, weight, state, totals, pltpu.SemaphoreType.DMA((2 * len(CHUNKS),))],
        vmem=20,
    )(tokens, key_weight, value_weight)
    sent, later_tokens = lax.optimization_barrier((sent, tokens))
    half = shaped((D // 2, TOKENS))
    top, bottom = call(
        turn_kernel, "turn", [half, half], [IN_SMEM, BLOCK], [pltpu.VMEM((D, TOKENS), F32)]
    )(core, later_tokens)
    bottom = swap_cores(bottom)
    left_top = shift(top, 1, "dp")
    right_bottom = shift(bottom, 3, "dp")
    got = exchange(sent, IMAGE)
    (query,) = call(
        query_kernel,
        "query",
        [heads],
        [BLOCK, BLOCK],
    )(tokens, query_weight)
    sent, numer, total = call(
        lambda *refs: numerator_kernel(loss_scale, *refs),
        "numerator",
        [shaped((TILES, 2 * PART, HD)), heads, shaped((HEADS, HD))],
        [BLOCK] * 3,
        [state],
        arrived=(0, 1, 2),
    )(got, query, upstream)
    sent, left_top, right_bottom, later_top, later_bottom = lax.optimization_barrier(
        (sent, left_top, right_bottom, top, bottom)
    )
    far_top = shift(left_top, 1, "dp")
    far_bottom = shift(right_bottom, 3, "dp")
    left_bottom = shift(later_bottom, 1, "dp")
    right_top = shift(later_top, 3, "dp")
    got_state = exchange(sent, IMAGE)
    sent, grad_denom = call(
        lambda *refs: total_grad_kernel(loss_scale, *refs[:4], *refs[6:]),
        "total_grad",
        [shaped((TILES, PART + HEADS, HD)), shaped((TOKENS, HEADS))],
        [BLOCK] * 4 + [ANYWHERE] * 2,
        [state, totals],
        arrived=(0, 1, 2, 3, 4, 5),
    )(got_state, query, upstream, total, swap_cores(left_bottom), swap_cores(right_top))
    sent, far_top, far_bottom, left_bottom, right_top = lax.optimization_barrier(
        (sent, far_top, far_bottom, left_bottom, right_top)
    )
    got = exchange(sent, IMAGE)

    block = shaped((TOKENS, EARLY))
    grad_query, *query_columns, late = call(
        query_grad_kernel,
        "query_grad",
        [flat, block, block, block, block, shaped((REPLICAS, TOKENS, LATE))],
        [IN_SMEM] + [BLOCK] * 5,
        [state, wide, blocks],
        arrived=(1,),
    )(place, got_state, query, numer, total, grad_denom)
    query_columns = shifted(query_columns, "dp")
    (rows,) = call(
        join_kernel,
        "join",
        [shaped((CORES * HALF, 2 * REPLICAS * TOKENS), BF16)],
        [BLOCK] * 8,
        arrived=tuple(range(1, 8)),
    )(top, left_top, far_top, right_top, bottom, left_bottom, far_bottom, right_bottom)
    (query_columns,) = call(
        pack_kernel,
        "pack_query",
        [shaped((REPLICAS * TOKENS, EARLY))],
        [BLOCK] * RING,
        arrived=(1, 2, 3),
    )(*query_columns)
    got, rows, query_columns = lax.optimization_barrier((got, rows, query_columns))

    grad_key, grad_value, sent = call(
        key_value_grad_kernel,
        "key_value_grad",
        [flat, flat, shaped((REPLICAS, TOKENS, LANES))],
        [BLOCK] * 4,
        [state, wide, wide],
        arrived=(0, 1, 2, 3),
    )(got, key, value, late)
    own_columns = exchange(sent, "dp")
    slots = call(
        lambda *refs: query_product_kernel(normalizer, *refs[:4], *refs[5:]),
        "query_product",
        [shaped((RING, PADDED_ROWS, EARLY))] * RING,
        [
            IN_SMEM,
            pl.BlockSpec((HALF, 2 * REPLICAS * TOKENS), lambda half: (half, 0)),
            BLOCK,
            BLOCK,
            ANYWHERE,
        ],
        [
            pltpu.VMEM((2 * REPLICAS * TOKENS, EARLY), BF16),
            pltpu.VMEM((PLANE_SIZE // CORES, PADDED_ROWS, EARLY), F32),
        ],
        vmem=24,
        arrived=(3,),
        steps=CORES,
        out_specs=[pl.BlockSpec((2, PADDED_ROWS, EARLY), lambda half: (half, 0, 0))] * RING,
    )(across, rows, query_columns, swap_cores(query_columns), sent)
    far_slot = shift(slots[2], 2, "x")
    slots = [slots[0], far_slot, shift(slots[1], 1, "x"), shift(slots[3], 3, "x")]
    own_columns, slots = lax.optimization_barrier((own_columns, slots))
    slots = call(
        second_stage_kernel,
        "second_stage",
        [shaped((PADDED_ROWS, EARLY))] * RING,
        [IN_SMEM] + [BLOCK] * RING,
        arrived=(2, 3, 4),
    )(along, *slots)
    (product,) = call(
        lambda *refs: key_value_product_kernel(normalizer, *refs[:4], *refs[5:]),
        "key_value_product",
        [shaped((PLANE_SIZE, PADDED_ROWS, LANES))],
        [
            IN_SMEM,
            pl.BlockSpec((HALF, 2 * REPLICAS * TOKENS), lambda half: (half, 0)),
            BLOCK,
            BLOCK,
            ANYWHERE,
        ],
        [pltpu.VMEM((2 * REPLICAS * TOKENS, LANES), BF16)],
        vmem=24,
        arrived=(2, 3),
        steps=CORES,
        out_specs=[
            pl.BlockSpec((PLANE_SIZE // CORES, PADDED_ROWS, LANES), lambda half: (half, 0, 0))
        ],
    )(place, rows, own_columns, swap_cores(own_columns), slots[0])
    key_value_out = exchange(product, PLANE)
    slots = shifted(slots, ("zh", "zl"))
    block = shaped((ROWS, COLS))
    query_out, key_out, value_out = call(
        last_kernel, "last", [block] * 3, [BLOCK] * 5, arrived=(0, 2, 3, 4)
    )(key_value_out, *slots)

    summed = back_project(grad_query, query_weight) + back_project(grad_key, key_weight)
    summed = summed + back_project(grad_value, value_weight)
    latent_grad = summed.astype(BF16).reshape(latent.shape)
    return latent_grad, query_out, key_out, value_out


def solution(mesh):
    devices = mesh.devices
    fine = Mesh(
        devices.reshape(REPLICAS, 2, CORES, 4, 2), ("dp", "zh", "core", "x", "zl")
    )
    grid = P("dp", ("zh", "core"), ("x", "zl"), None)
    weight_out = P(("zh", "core", "x", "zl"), "dp")
    return jax.shard_map(
        body,
        mesh=fine,
        in_specs=(grid, P(), P(), P(), grid),
        out_specs=(grid, weight_out, weight_out, weight_out),
        check_vma=False,
    )
```

```python
import math

import jax
import jax.numpy as jnp
from jax import lax
from jax.experimental import pallas as pl
from jax.experimental.pallas import tpu as pltpu
from jax.sharding import Mesh, PartitionSpec as P

D = 2240
HD = 112
HEADS = 10
HW = HEADS * HD
TILES = 32
PART = HW // TILES
PLANE_SIZE = 16
CORES = 2
ROWS = D // TILES
PADDED_ROWS = 72
HALF = D // 4
REPLICAS = 4
RING = 4
COLS = HW // REPLICAS
EARLY = 256
LATE = COLS - EARLY
WIDE = 2 * COLS + LATE
LANES = 640
TOKENS = 128

EPSILON = 1e-15
IMAGE = ("zh", "core", "x", "zl")
PLANE = ("zh", "x", "zl")
CHUNKS = [(0, 1152), (1152, D - 1152)]

F32 = jnp.float32
BF16 = jnp.bfloat16
BLOCK = pl.BlockSpec()
IN_SMEM = pl.BlockSpec(memory_space=pltpu.SMEM)
ANYWHERE = pl.BlockSpec(memory_space=pl.ANY)
IN_HBM = pl.BlockSpec(memory_space=pltpu.HBM)


def shaped(shape, dtype=F32):
    return pltpu.HBM(shape, dtype)


def call(kernel, name, outs, in_specs, scratch=(), vmem=12, arrived=(), steps=1, out_specs=None):
    run = pl.pallas_call(
        kernel,
        name=name,
        grid=(steps,),
        out_shape=outs,
        in_specs=in_specs,
        out_specs=out_specs or [BLOCK] * len(outs),
        scratch_shapes=list(scratch),
        compiler_params=pltpu.CompilerParams(vmem_limit_bytes=vmem * 1024 * 1024),
    )

    def with_placed(*operands):
        placed = [
            operand
            if spec is IN_SMEM or index in arrived
            else pltpu.with_memory_space_constraint(operand, pltpu.HBM)
            for index, (operand, spec) in enumerate(zip(operands, in_specs))
        ]
        return run(*placed)

    return with_placed


def dot(left, right, left_dim, right_dim):
    return lax.dot_general(
        left, right, (((left_dim,), (right_dim,)), ((), ())), preferred_element_type=F32
    )


def split_dot(left, right, left_dim, right_dim):
    high = right.astype(BF16)
    low = (right - high.astype(F32)).astype(BF16)
    return dot(left, high, left_dim, right_dim) + dot(left, low, left_dim, right_dim)


def relu(values):
    return jnp.maximum(values, jnp.zeros_like(values))


def weight_copies(weight, buffer, semaphores, first):
    copies = []
    for index, (start, size) in enumerate(CHUNKS):
        copies.append(
            pltpu.make_async_copy(
                weight.at[pl.ds(start, size)],
                buffer.at[pl.ds(start, size)],
                semaphores.at[first + index],
            )
        )
    return copies


def project(tokens, buffer, copies):
    total = None
    for (start, size), copy in zip(CHUNKS, copies):
        copy.wait()
        term = dot(tokens[:, start : start + size], buffer[start : start + size, :], 1, 0)
        total = term if total is None else total + term
    return total.astype(BF16)


def store_parts(sent, at, state):
    for tile in range(TILES):
        sent[tile, at : at + PART, :] = state[tile * PART : (tile + 1) * PART, :]


def load_parts(state, got):
    for tile in range(TILES):
        state[tile * PART : (tile + 1) * PART, :] = got[tile, :PART, :]


def head(ref, index):
    return ref[index * HD : (index + 1) * HD, :]


def key_value_kernel(
    tokens, key_weight, value_weight, key, value, sent, key_buffer, value_buffer, state, total, semaphores
):
    value_copies = weight_copies(value_weight, value_buffer, semaphores, 0)
    key_copies = weight_copies(key_weight, key_buffer, semaphores, len(CHUNKS))
    for copy in value_copies + key_copies:
        copy.start()
    rows = tokens[...]
    value_rows = project(rows, value_buffer, value_copies)
    key_rows = project(rows, key_buffer, key_copies)
    for index in range(HEADS):
        part = slice(index * HD, (index + 1) * HD)
        key_head = key_rows[:, part]
        value_head = value_rows[:, part]
        key[index] = key_head
        value[index] = value_head
        positive = relu(key_head)
        state[index * HD : (index + 1) * HD, :] = dot(positive, value_head, 0, 0)
        total[index : index + 1, :] = jnp.sum(positive.astype(F32), axis=0, keepdims=True)
    store_parts(sent, 0, state)
    totals = total[...]
    for tile in range(TILES):
        sent[tile, PART : PART + HEADS, :] = totals


def query_kernel(tokens, weight, query):
    query_rows = dot(tokens[...], weight[...], 1, 0).astype(BF16)
    for index in range(HEADS):
        query[index] = query_rows[:, index * HD : (index + 1) * HD]


def inverse_denominator(positive, total):
    return 1.0 / (jnp.sum(positive * total, axis=1, keepdims=True) + EPSILON)


def numerator_kernel(loss_scale, got, query, upstream, sent, numer, total, state):
    sums = got[0]
    for tile in range(1, TILES):
        sums = sums + got[tile]
    state_part = sums[:PART]
    totals = sums[PART : PART + HEADS]
    total[...] = totals
    for index in range(HEADS):
        part = slice(index * HD, (index + 1) * HD)
        positive = relu(query[index])
        inverse = inverse_denominator(positive.astype(F32), totals[index : index + 1])
        cotangent = upstream[:, part].astype(F32) * loss_scale
        numer_low = (cotangent * inverse).astype(BF16)
        numer[index] = numer_low
        state[index * HD : (index + 1) * HD, :] = dot(positive, numer_low, 0, 0)
    for tile in range(TILES):
        sent[tile, :PART, :] = state_part
    store_parts(sent, PART, state)


def total_grad_kernel(loss_scale, got, query, upstream, total, sent, grad_denom, state, totals):
    load_parts(state, got)
    for index in range(HEADS):
        part = slice(index * HD, (index + 1) * HD)
        positive = relu(query[index])
        wide = positive.astype(F32)
        inverse = inverse_denominator(wide, total[index : index + 1, :])
        cotangent = upstream[:, part].astype(F32) * loss_scale
        product = split_dot(positive, head(state, index), 1, 0)
        grad = -(jnp.sum(cotangent * product, axis=1, keepdims=True) * inverse) * inverse
        grad_denom[:, index : index + 1] = grad
        totals[index : index + 1, :] = jnp.sum(wide * grad, axis=0, keepdims=True)
    part_sum = got[0, PART:, :]
    for tile in range(1, TILES):
        part_sum = part_sum + got[tile, PART:, :]
    values = totals[...]
    for tile in range(TILES):
        sent[tile, :PART, :] = part_sum
        sent[tile, PART : PART + HEADS, :] = values


def place_columns(place, blocks, outs, at, first=0, last=COLS):
    for slot, out in enumerate(outs):
        block = blocks[lax.rem(place[0] + slot, REPLICAS)]
        out[:, at : at + last - first] = block[:, first:last]


def split_columns(flat, blocks):
    for block in range(REPLICAS):
        blocks[block] = flat[:, block * COLS : (block + 1) * COLS]


def query_grad_kernel(
    place, got, query, numer, total, grad_denom, grad, own, first, second, third, late, state, flat, blocks
):
    load_parts(state, got)
    for index in range(HEADS):
        part = slice(index * HD, (index + 1) * HD)
        values = split_dot(numer[index], head(state, index), 1, 1)
        values = values + grad_denom[:, index : index + 1] * total[index : index + 1, :]
        values = jnp.where(query[index].astype(F32) > 0, values, 0.0).astype(BF16)
        grad[:, part] = values
        flat[:, part] = values.astype(F32)
    split_columns(flat, blocks)
    place_columns(place, blocks, (own, first, second, third), 0, 0, EARLY)
    for block in range(REPLICAS):
        late[block] = blocks[block][:, EARLY:]


def key_value_grad_kernel(got, key, value, late, grad_key, grad_value, sent, state, flat_key, flat_value):
    load_parts(state, got)
    totals = got[0, PART : PART + HEADS, :]
    for tile in range(1, TILES):
        totals = totals + got[tile, PART : PART + HEADS, :]
    for index in range(HEADS):
        part = slice(index * HD, (index + 1) * HD)
        key_head = key[index]
        positive = relu(key_head)
        state_head = head(state, index)
        values = split_dot(positive, state_head, 1, 0).astype(BF16)
        grad_value[:, part] = values
        flat_value[:, part] = values.astype(F32)
        values = split_dot(value[index], state_head, 1, 1) + totals[index : index + 1]
        values = jnp.where(key_head.astype(F32) > 0, values, 0.0).astype(BF16)
        grad_key[:, part] = values
        flat_key[:, part] = values.astype(F32)
    for block in range(REPLICAS):
        part = slice(block * COLS, (block + 1) * COLS)
        sent[block, :, :COLS] = flat_key[:, part]
        sent[block, :, COLS : 2 * COLS] = flat_value[:, part]
        sent[block, :, 2 * COLS : WIDE] = late[block]
        sent[block, :, WIDE:] = jnp.zeros((TOKENS, LANES - WIDE), F32)


def turn_kernel(core, tokens, mine, other, turned):
    for start in range(0, D, 128):
        size = min(128, D - start)
        turned[start : start + size, :] = tokens[:, start : start + size].astype(F32).T
    for half in range(CORES):
        rows = slice(half * HALF, (half + 1) * HALF)
        for out, which in ((mine, core[0]), (other, 1 - core[0])):
            start = pl.multiple_of((half * CORES + which) * HALF, 16)
            out[rows, :] = turned[pl.ds(start, HALF), :]


def join_kernel(*refs):
    for slot, part in enumerate(refs[:-1]):
        refs[-1][:, slot * TOKENS : (slot + 1) * TOKENS] = part[...].astype(BF16)


def pack_kernel(*refs):
    out = refs[-1]
    for slot, part in enumerate(refs[:-1]):
        out[slot * TOKENS : (slot + 1) * TOKENS, :] = part[...].astype(out.dtype)


def query_product_kernel(normalizer, across, rows, own, other, *refs):
    outs, columns, product = refs[:-2], refs[-2], refs[-1]

    @pl.when(pl.program_id(0) == 0)
    def _():
        columns[: REPLICAS * TOKENS, :] = own[...].astype(BF16)
        columns[REPLICAS * TOKENS :, :] = other[...].astype(BF16)

    values = dot(rows[...], columns[...], 1, 0) * normalizer
    for index in range(PLANE_SIZE // CORES):
        product[index, :ROWS, :] = values[index * ROWS : (index + 1) * ROWS]
    for slot, out in enumerate(outs):
        at = lax.rem(across[0] + slot, RING)
        for block in range(2):
            out[block] = product[at * 2 + block]


def key_value_product_kernel(normalizer, place, rows, own, other, out, columns):
    @pl.when(pl.program_id(0) == 0)
    def _():
        for core, blocks in enumerate((own, other)):
            for slot in range(REPLICAS):
                at = (core * REPLICAS + slot) * TOKENS
                source = lax.rem(place[0] + REPLICAS - slot, REPLICAS)
                columns[at : at + TOKENS, :] = blocks[source].astype(BF16)

    values = dot(rows[...], columns[...], 1, 0) * normalizer
    for index in range(PLANE_SIZE // CORES):
        out[index, :ROWS, :] = values[index * ROWS : (index + 1) * ROWS]


def second_stage_kernel(along, own, first, second, third, *outs):
    for slot, out in enumerate(outs):
        at = lax.rem(along[0] + slot, RING)
        out[...] = (own[at] + first[at]) + (second[at] + third[at])


def last_kernel(key_value, own, first, second, third, query_out, key_out, value_out):
    total = key_value[0]
    for index in range(1, PLANE_SIZE):
        total = total + key_value[index]
    key_out[...] = total[:ROWS, :COLS]
    value_out[...] = total[:ROWS, COLS : 2 * COLS]
    query_out[:, EARLY:] = total[:ROWS, 2 * COLS : WIDE]
    total = (own[...] + first[...]) + (second[...] + third[...])
    query_out[:, :EARLY] = total[:ROWS]


def exchange(blocks, axes):
    return lax.all_to_all(blocks, axes, 0, 0, tiled=True)


def shift(values, by, axis):
    return lax.ppermute(values, axis, [(i, (i + by) % RING) for i in range(RING)])


def shifted(slots, axis):
    return [slots[0]] + [shift(slots[s], s, axis) for s in range(1, RING)]


def swap_cores(values):
    return lax.ppermute(values, "core", [(0, 1), (1, 0)])


def both_cores(blocks):
    return blocks + [swap_cores(block) for block in blocks]


def back_project(gradient, weight):
    return dot(gradient, weight, 1, 1)


def body(latent, query_weight, key_weight, value_weight, upstream_grad):
    image_tokens = TOKENS * TILES
    loss_scale = 4.0 * math.sqrt(image_tokens)
    normalizer = 1.0 / math.sqrt(image_tokens * REPLICAS)
    tokens = latent.reshape(TOKENS, D)
    upstream = upstream_grad.reshape(TOKENS, HW)
    place = lax.axis_index("dp").reshape(1)
    core = lax.axis_index("core").reshape(1)
    across = lax.axis_index("x").reshape(1)
    along = lax.axis_index(("zh", "zl")).reshape(1)
    heads = shaped((HEADS, TOKENS, HD), BF16)
    flat = shaped((TOKENS, HW), BF16)
    state = pltpu.VMEM((HW, HD), F32)
    totals = pltpu.VMEM((HEADS, HD), F32)
    weight = pltpu.VMEM((D, HW), BF16)
    wide = pltpu.VMEM((TOKENS, HW), F32)
    blocks = pltpu.VMEM((REPLICAS, TOKENS, COLS), F32)

    key, value, sent = call(
        key_value_kernel,
        "key_value",
        [heads, heads, shaped((TILES, PART + HEADS, HD))],
        [BLOCK, IN_HBM, IN_HBM],
        [weight, weight, state, totals, pltpu.SemaphoreType.DMA((2 * len(CHUNKS),))],
        vmem=20,
    )(tokens, key_weight, value_weight)
    sent, later_tokens = lax.optimization_barrier((sent, tokens))
    half = shaped((D // 2, TOKENS))
    top, other = call(
        turn_kernel, "turn", [half, half], [IN_SMEM, BLOCK], [pltpu.VMEM((D, TOKENS), F32)]
    )(core, later_tokens)
    left_top = shift(top, 1, "dp")
    right_other = shift(other, 3, "dp")
    got = exchange(sent, IMAGE)
    (query,) = call(
        query_kernel,
        "query",
        [heads],
        [BLOCK, BLOCK],
    )(tokens, query_weight)
    sent, numer, total = call(
        lambda *refs: numerator_kernel(loss_scale, *refs),
        "numerator",
        [shaped((TILES, 2 * PART, HD)), heads, shaped((HEADS, HD))],
        [BLOCK] * 3,
        [state],
        arrived=(0, 1, 2),
    )(got, query, upstream)
    sent, left_top, right_other, later_top, later_other = lax.optimization_barrier(
        (sent, left_top, right_other, top, other)
    )
    far_top = shift(left_top, 1, "dp")
    far_other = shift(right_other, 3, "dp")
    left_bottom = swap_cores(shift(later_other, 1, "dp"))
    right_top = shift(later_top, 3, "dp")
    got_state = exchange(sent, IMAGE)
    sent, grad_denom = call(
        lambda *refs: total_grad_kernel(loss_scale, *refs[:4], *refs[6:]),
        "total_grad",
        [shaped((TILES, PART + HEADS, HD)), shaped((TOKENS, HEADS))],
        [BLOCK] * 4 + [ANYWHERE] * 2,
        [state, totals],
        arrived=(0, 1, 2, 3, 4, 5),
    )(got_state, query, upstream, total, left_bottom, swap_cores(right_top))
    sent, far_top, far_other, left_bottom, right_top = lax.optimization_barrier(
        (sent, far_top, far_other, left_bottom, right_top)
    )
    bottom, right_bottom, far_bottom = (
        swap_cores(rows) for rows in (later_other, right_other, far_other)
    )
    got = exchange(sent, IMAGE)

    block = shaped((TOKENS, EARLY))
    grad_query, *query_columns, late = call(
        query_grad_kernel,
        "query_grad",
        [flat, block, block, block, block, shaped((REPLICAS, TOKENS, LATE))],
        [IN_SMEM] + [BLOCK] * 5,
        [state, wide, blocks],
        arrived=(1,),
    )(place, got_state, query, numer, total, grad_denom)
    query_columns = shifted(query_columns, "dp")
    (rows,) = call(
        join_kernel,
        "join",
        [shaped((CORES * HALF, 2 * REPLICAS * TOKENS), BF16)],
        [BLOCK] * 8,
        arrived=tuple(range(1, 8)),
    )(top, left_top, far_top, right_top, bottom, left_bottom, far_bottom, right_bottom)
    (query_columns,) = call(
        lambda *refs: pack_kernel(*refs[:RING], refs[-1]),
        "pack_query",
        [shaped((REPLICAS * TOKENS, EARLY))],
        [BLOCK] * RING + [ANYWHERE],
        arrived=(1, 2, 3),
    )(*query_columns, rows)
    got, rows, query_columns = lax.optimization_barrier((got, rows, query_columns))

    grad_key, grad_value, sent = call(
        key_value_grad_kernel,
        "key_value_grad",
        [flat, flat, shaped((REPLICAS, TOKENS, LANES))],
        [BLOCK] * 4,
        [state, wide, wide],
        arrived=(0, 1, 2, 3),
    )(got, key, value, late)
    own_columns = exchange(sent, "dp")
    slots = call(
        lambda *refs: query_product_kernel(normalizer, *refs[:4], *refs[5:]),
        "query_product",
        [shaped((RING, PADDED_ROWS, EARLY))] * RING,
        [
            IN_SMEM,
            pl.BlockSpec((HALF, 2 * REPLICAS * TOKENS), lambda half: (half, 0)),
            BLOCK,
            BLOCK,
            ANYWHERE,
        ],
        [
            pltpu.VMEM((2 * REPLICAS * TOKENS, EARLY), BF16),
            pltpu.VMEM((PLANE_SIZE // CORES, PADDED_ROWS, EARLY), F32),
        ],
        vmem=24,
        arrived=(3,),
        steps=CORES,
        out_specs=[pl.BlockSpec((2, PADDED_ROWS, EARLY), lambda half: (half, 0, 0))] * RING,
    )(across, rows, query_columns, swap_cores(query_columns), sent)
    far_slot = shift(slots[2], 2, "x")
    slots = [slots[0], far_slot, shift(slots[1], 1, "x"), shift(slots[3], 3, "x")]
    own_columns, slots = lax.optimization_barrier((own_columns, slots))
    slots = call(
        second_stage_kernel,
        "second_stage",
        [shaped((PADDED_ROWS, EARLY))] * RING,
        [IN_SMEM] + [BLOCK] * RING,
        arrived=(2, 3, 4),
    )(along, *slots)
    (product,) = call(
        lambda *refs: key_value_product_kernel(normalizer, *refs[:4], *refs[5:]),
        "key_value_product",
        [shaped((PLANE_SIZE, PADDED_ROWS, LANES))],
        [
            IN_SMEM,
            pl.BlockSpec((HALF, 2 * REPLICAS * TOKENS), lambda half: (half, 0)),
            BLOCK,
            BLOCK,
            ANYWHERE,
        ],
        [pltpu.VMEM((2 * REPLICAS * TOKENS, LANES), BF16)],
        vmem=24,
        arrived=(2, 3),
        steps=CORES,
        out_specs=[
            pl.BlockSpec((PLANE_SIZE // CORES, PADDED_ROWS, LANES), lambda half: (half, 0, 0))
        ],
    )(place, rows, own_columns, swap_cores(own_columns), slots[0])
    key_value_out = exchange(product, PLANE)
    slots = shifted(slots, ("zh", "zl"))
    block = shaped((ROWS, COLS))
    query_out, key_out, value_out = call(
        last_kernel, "last", [block] * 3, [BLOCK] * 5, arrived=(0, 2, 3, 4)
    )(key_value_out, *slots)

    summed = back_project(grad_query, query_weight) + back_project(grad_key, key_weight)
    summed = summed + back_project(grad_value, value_weight)
    latent_grad = summed.astype(BF16).reshape(latent.shape)
    return latent_grad, query_out, key_out, value_out


def solution(mesh):
    devices = mesh.devices
    fine = Mesh(
        devices.reshape(REPLICAS, 2, CORES, 4, 2), ("dp", "zh", "core", "x", "zl")
    )
    grid = P("dp", ("zh", "core"), ("x", "zl"), None)
    weight_out = P(("zh", "core", "x", "zl"), "dp")
    return jax.shard_map(
        body,
        mesh=fine,
        in_specs=(grid, P(), P(), P(), grid),
        out_specs=(grid, weight_out, weight_out, weight_out),
        check_vma=False,
    )
```

```python
import math

import jax
import jax.numpy as jnp
from jax import lax
from jax.experimental import pallas as pl
from jax.experimental.pallas import tpu as pltpu
from jax.sharding import Mesh, PartitionSpec as P

D = 2240
HD = 112
HEADS = 10
HW = HEADS * HD
TILES = 32
PART = HW // TILES
PLANE_SIZE = 16
CORES = 2
ROWS = D // TILES
PADDED_ROWS = 72
HALF = D // 4
REPLICAS = 4
RING = 4
COLS = HW // REPLICAS
EARLY = 256
LATE = COLS - EARLY
WIDE = 2 * COLS + LATE
LANES = 640
TOKENS = 128

EPSILON = 1e-15
IMAGE = ("zh", "core", "x", "zl")
PLANE = ("zh", "x", "zl")
CHUNKS = [(0, 1152), (1152, D - 1152)]

F32 = jnp.float32
BF16 = jnp.bfloat16
BLOCK = pl.BlockSpec()
IN_SMEM = pl.BlockSpec(memory_space=pltpu.SMEM)
ANYWHERE = pl.BlockSpec(memory_space=pl.ANY)
IN_HBM = pl.BlockSpec(memory_space=pltpu.HBM)


def shaped(shape, dtype=F32):
    return pltpu.HBM(shape, dtype)


def call(kernel, name, outs, in_specs, scratch=(), vmem=12, arrived=(), steps=1, out_specs=None):
    run = pl.pallas_call(
        kernel,
        name=name,
        grid=(steps,),
        out_shape=outs,
        in_specs=in_specs,
        out_specs=out_specs or [BLOCK] * len(outs),
        scratch_shapes=list(scratch),
        compiler_params=pltpu.CompilerParams(vmem_limit_bytes=vmem * 1024 * 1024),
    )

    def with_placed(*operands):
        placed = [
            operand
            if spec is IN_SMEM or index in arrived
            else pltpu.with_memory_space_constraint(operand, pltpu.HBM)
            for index, (operand, spec) in enumerate(zip(operands, in_specs))
        ]
        return run(*placed)

    return with_placed


def dot(left, right, left_dim, right_dim):
    return lax.dot_general(
        left, right, (((left_dim,), (right_dim,)), ((), ())), preferred_element_type=F32
    )


def split_dot(left, right, left_dim, right_dim):
    high = right.astype(BF16)
    low = (right - high.astype(F32)).astype(BF16)
    return dot(left, high, left_dim, right_dim) + dot(left, low, left_dim, right_dim)


def relu(values):
    return jnp.maximum(values, jnp.zeros_like(values))


def weight_copies(weight, buffer, semaphores, first):
    copies = []
    for index, (start, size) in enumerate(CHUNKS):
        copies.append(
            pltpu.make_async_copy(
                weight.at[pl.ds(start, size)],
                buffer.at[pl.ds(start, size)],
                semaphores.at[first + index],
            )
        )
    return copies


def project(tokens, buffer, copies):
    total = None
    for (start, size), copy in zip(CHUNKS, copies):
        copy.wait()
        term = dot(tokens[:, start : start + size], buffer[start : start + size, :], 1, 0)
        total = term if total is None else total + term
    return total.astype(BF16)


def store_parts(sent, at, state):
    for tile in range(TILES):
        sent[tile, at : at + PART, :] = state[tile * PART : (tile + 1) * PART, :]


def load_parts(state, got):
    for tile in range(TILES):
        state[tile * PART : (tile + 1) * PART, :] = got[tile, :PART, :]


def head(ref, index):
    return ref[index * HD : (index + 1) * HD, :]


def key_value_kernel(
    tokens, key_weight, value_weight, key, value, sent, key_buffer, value_buffer, state, total, semaphores
):
    value_copies = weight_copies(value_weight, value_buffer, semaphores, 0)
    key_copies = weight_copies(key_weight, key_buffer, semaphores, len(CHUNKS))
    for copy in value_copies + key_copies:
        copy.start()
    rows = tokens[...]
    value_rows = project(rows, value_buffer, value_copies)
    key_rows = project(rows, key_buffer, key_copies)
    for index in range(HEADS):
        part = slice(index * HD, (index + 1) * HD)
        key_head = key_rows[:, part]
        value_head = value_rows[:, part]
        key[index] = key_head
        value[index] = value_head
        positive = relu(key_head)
        state[index * HD : (index + 1) * HD, :] = dot(positive, value_head, 0, 0)
        total[index : index + 1, :] = jnp.sum(positive.astype(F32), axis=0, keepdims=True)
    store_parts(sent, 0, state)
    totals = total[...]
    for tile in range(TILES):
        sent[tile, PART : PART + HEADS, :] = totals


def query_kernel(tokens, weight, query):
    query_rows = dot(tokens[...], weight[...], 1, 0).astype(BF16)
    for index in range(HEADS):
        query[index] = query_rows[:, index * HD : (index + 1) * HD]


def inverse_denominator(positive, total):
    return 1.0 / (jnp.sum(positive * total, axis=1, keepdims=True) + EPSILON)


def numerator_kernel(loss_scale, got, query_rows, upstream, sent, numer, total, state, query, arrived):
    copy = pltpu.make_async_copy(query_rows, query, arrived)
    copy.start()
    sums = got[0]
    for tile in range(1, TILES):
        sums = sums + got[tile]
    state_part = sums[:PART]
    totals = sums[PART : PART + HEADS]
    total[...] = totals
    copy.wait()
    for index in range(HEADS):
        part = slice(index * HD, (index + 1) * HD)
        positive = relu(query[index])
        inverse = inverse_denominator(positive.astype(F32), totals[index : index + 1])
        cotangent = upstream[:, part].astype(F32) * loss_scale
        numer_low = (cotangent * inverse).astype(BF16)
        numer[index] = numer_low
        state[index * HD : (index + 1) * HD, :] = dot(positive, numer_low, 0, 0)
    for tile in range(TILES):
        sent[tile, :PART, :] = state_part
    store_parts(sent, PART, state)


def total_grad_kernel(loss_scale, got, query, upstream, total, sent, grad_denom, state, totals):
    load_parts(state, got)
    for index in range(HEADS):
        part = slice(index * HD, (index + 1) * HD)
        positive = relu(query[index])
        wide = positive.astype(F32)
        inverse = inverse_denominator(wide, total[index : index + 1, :])
        cotangent = upstream[:, part].astype(F32) * loss_scale
        product = split_dot(positive, head(state, index), 1, 0)
        grad = -(jnp.sum(cotangent * product, axis=1, keepdims=True) * inverse) * inverse
        grad_denom[:, index : index + 1] = grad
        totals[index : index + 1, :] = jnp.sum(wide * grad, axis=0, keepdims=True)
    part_sum = got[0, PART:, :]
    for tile in range(1, TILES):
        part_sum = part_sum + got[tile, PART:, :]
    values = totals[...]
    for tile in range(TILES):
        sent[tile, :PART, :] = part_sum
        sent[tile, PART : PART + HEADS, :] = values


def place_columns(place, blocks, outs, at, first=0, last=COLS):
    for slot, out in enumerate(outs):
        block = blocks[lax.rem(place[0] + slot, REPLICAS)]
        out[:, at : at + last - first] = block[:, first:last]


def split_columns(flat, blocks):
    for block in range(REPLICAS):
        blocks[block] = flat[:, block * COLS : (block + 1) * COLS]


def query_grad_kernel(
    place, got, query, numer, total, grad_denom, grad, own, first, second, third, late, state, flat, blocks
):
    load_parts(state, got)
    for index in range(HEADS):
        part = slice(index * HD, (index + 1) * HD)
        values = split_dot(numer[index], head(state, index), 1, 1)
        values = values + grad_denom[:, index : index + 1] * total[index : index + 1, :]
        values = jnp.where(query[index].astype(F32) > 0, values, 0.0).astype(BF16)
        grad[:, part] = values
        flat[:, part] = values.astype(F32)
    split_columns(flat, blocks)
    place_columns(place, blocks, (own, first, second, third), 0, 0, EARLY)
    for block in range(REPLICAS):
        late[block] = blocks[block][:, EARLY:]


def key_value_grad_kernel(got, key, value, late, grad_key, grad_value, sent, state, flat_key, flat_value):
    load_parts(state, got)
    totals = got[0, PART : PART + HEADS, :]
    for tile in range(1, TILES):
        totals = totals + got[tile, PART : PART + HEADS, :]
    for index in range(HEADS):
        part = slice(index * HD, (index + 1) * HD)
        key_head = key[index]
        positive = relu(key_head)
        state_head = head(state, index)
        values = split_dot(positive, state_head, 1, 0).astype(BF16)
        grad_value[:, part] = values
        flat_value[:, part] = values.astype(F32)
        values = split_dot(value[index], state_head, 1, 1) + totals[index : index + 1]
        values = jnp.where(key_head.astype(F32) > 0, values, 0.0).astype(BF16)
        grad_key[:, part] = values
        flat_key[:, part] = values.astype(F32)
    for block in range(REPLICAS):
        part = slice(block * COLS, (block + 1) * COLS)
        sent[block, :, :COLS] = flat_key[:, part]
        sent[block, :, COLS : 2 * COLS] = flat_value[:, part]
        sent[block, :, 2 * COLS : WIDE] = late[block]
        sent[block, :, WIDE:] = jnp.zeros((TOKENS, LANES - WIDE), F32)


def turn_kernel(core, tokens, mine, other, turned):
    for start in range(0, D, 128):
        size = min(128, D - start)
        turned[start : start + size, :] = tokens[:, start : start + size].astype(F32).T
    for half in range(CORES):
        rows = slice(half * HALF, (half + 1) * HALF)
        for out, which in ((mine, core[0]), (other, 1 - core[0])):
            start = pl.multiple_of((half * CORES + which) * HALF, 16)
            out[rows, :] = turned[pl.ds(start, HALF), :]


def join_kernel(*refs):
    for slot, part in enumerate(refs[:-1]):
        refs[-1][:, slot * TOKENS : (slot + 1) * TOKENS] = part[...].astype(BF16)


def pack_kernel(*refs):
    out = refs[-1]
    for slot, part in enumerate(refs[:-1]):
        out[slot * TOKENS : (slot + 1) * TOKENS, :] = part[...].astype(out.dtype)


def query_product_kernel(normalizer, across, rows, own, other, *refs):
    outs, columns, product = refs[:-2], refs[-2], refs[-1]

    @pl.when(pl.program_id(0) == 0)
    def _():
        columns[: REPLICAS * TOKENS, :] = own[...].astype(BF16)
        columns[REPLICAS * TOKENS :, :] = other[...].astype(BF16)

    values = dot(rows[...], columns[...], 1, 0) * normalizer
    for index in range(PLANE_SIZE // CORES):
        product[index, :ROWS, :] = values[index * ROWS : (index + 1) * ROWS]
    for slot, out in enumerate(outs):
        at = lax.rem(across[0] + slot, RING)
        for block in range(2):
            out[block] = product[at * 2 + block]


def key_value_product_kernel(normalizer, place, rows, own, other, out, columns):
    @pl.when(pl.program_id(0) == 0)
    def _():
        for core, blocks in enumerate((own, other)):
            for slot in range(REPLICAS):
                at = (core * REPLICAS + slot) * TOKENS
                source = lax.rem(place[0] + REPLICAS - slot, REPLICAS)
                columns[at : at + TOKENS, :] = blocks[source].astype(BF16)

    values = dot(rows[...], columns[...], 1, 0) * normalizer
    for index in range(PLANE_SIZE // CORES):
        out[index, :ROWS, :] = values[index * ROWS : (index + 1) * ROWS]


def second_stage_kernel(along, own, first, second, third, *outs):
    for slot, out in enumerate(outs):
        at = lax.rem(along[0] + slot, RING)
        out[...] = (own[at] + first[at]) + (second[at] + third[at])


def last_kernel(key_value, own, first, second, third, query_out, key_out, value_out):
    total = key_value[0]
    for index in range(1, PLANE_SIZE):
        total = total + key_value[index]
    key_out[...] = total[:ROWS, :COLS]
    value_out[...] = total[:ROWS, COLS : 2 * COLS]
    query_out[:, EARLY:] = total[:ROWS, 2 * COLS : WIDE]
    total = (own[...] + first[...]) + (second[...] + third[...])
    query_out[:, :EARLY] = total[:ROWS]


def exchange(blocks, axes):
    return lax.all_to_all(blocks, axes, 0, 0, tiled=True)


def shift(values, by, axis):
    return lax.ppermute(values, axis, [(i, (i + by) % RING) for i in range(RING)])


def shifted(slots, axis):
    return [slots[0]] + [shift(slots[s], s, axis) for s in range(1, RING)]


def swap_cores(values):
    return lax.ppermute(values, "core", [(0, 1), (1, 0)])


def both_cores(blocks):
    return blocks + [swap_cores(block) for block in blocks]


def back_project(gradient, weight):
    return dot(gradient, weight, 1, 1)


def body(latent, query_weight, key_weight, value_weight, upstream_grad):
    image_tokens = TOKENS * TILES
    loss_scale = 4.0 * math.sqrt(image_tokens)
    normalizer = 1.0 / math.sqrt(image_tokens * REPLICAS)
    tokens = latent.reshape(TOKENS, D)
    upstream = upstream_grad.reshape(TOKENS, HW)
    place = lax.axis_index("dp").reshape(1)
    core = lax.axis_index("core").reshape(1)
    across = lax.axis_index("x").reshape(1)
    along = lax.axis_index(("zh", "zl")).reshape(1)
    heads = shaped((HEADS, TOKENS, HD), BF16)
    flat = shaped((TOKENS, HW), BF16)
    state = pltpu.VMEM((HW, HD), F32)
    totals = pltpu.VMEM((HEADS, HD), F32)
    weight = pltpu.VMEM((D, HW), BF16)
    wide = pltpu.VMEM((TOKENS, HW), F32)
    blocks = pltpu.VMEM((REPLICAS, TOKENS, COLS), F32)

    key, value, sent = call(
        key_value_kernel,
        "key_value",
        [heads, heads, shaped((TILES, PART + HEADS, HD))],
        [BLOCK, IN_HBM, IN_HBM],
        [weight, weight, state, totals, pltpu.SemaphoreType.DMA((2 * len(CHUNKS),))],
        vmem=20,
    )(tokens, key_weight, value_weight)
    sent, later_tokens = lax.optimization_barrier((sent, tokens))
    half = shaped((D // 2, TOKENS))
    top, bottom = call(
        turn_kernel, "turn", [half, half], [IN_SMEM, BLOCK], [pltpu.VMEM((D, TOKENS), F32)]
    )(core, later_tokens)
    bottom = swap_cores(bottom)
    left_top = shift(top, 1, "dp")
    right_bottom = shift(bottom, 3, "dp")
    got = exchange(sent, IMAGE)
    (query,) = call(
        query_kernel,
        "query",
        [pltpu.HBM((HEADS, TOKENS, HD), BF16)],
        [BLOCK, BLOCK],
    )(tokens, query_weight)
    sent, numer, total = call(
        lambda *refs: numerator_kernel(loss_scale, *refs),
        "numerator",
        [shaped((TILES, 2 * PART, HD)), heads, shaped((HEADS, HD))],
        [BLOCK, IN_HBM, BLOCK],
        [state, pltpu.VMEM((HEADS, TOKENS, HD), BF16), pltpu.SemaphoreType.DMA],
        arrived=(0, 2),
    )(got, query, upstream)
    sent, left_top, right_bottom, later_top, later_bottom = lax.optimization_barrier(
        (sent, left_top, right_bottom, top, bottom)
    )
    far_top = shift(left_top, 1, "dp")
    far_bottom = shift(right_bottom, 3, "dp")
    left_bottom = shift(later_bottom, 1, "dp")
    right_top = shift(later_top, 3, "dp")
    got_state = exchange(sent, IMAGE)
    sent, grad_denom = call(
        lambda *refs: total_grad_kernel(loss_scale, *refs[:4], *refs[6:]),
        "total_grad",
        [shaped((TILES, PART + HEADS, HD)), shaped((TOKENS, HEADS))],
        [BLOCK] * 4 + [ANYWHERE] * 2,
        [state, totals],
        arrived=(0, 1, 2, 3, 4, 5),
    )(got_state, query, upstream, total, swap_cores(left_bottom), swap_cores(right_top))
    sent, far_top, far_bottom, left_bottom, right_top = lax.optimization_barrier(
        (sent, far_top, far_bottom, left_bottom, right_top)
    )
    got = exchange(sent, IMAGE)

    block = shaped((TOKENS, EARLY))
    grad_query, *query_columns, late = call(
        query_grad_kernel,
        "query_grad",
        [flat, block, block, block, block, shaped((REPLICAS, TOKENS, LATE))],
        [IN_SMEM] + [BLOCK] * 5,
        [state, wide, blocks],
        arrived=(1,),
    )(place, got_state, query, numer, total, grad_denom)
    query_columns = shifted(query_columns, "dp")
    (rows,) = call(
        join_kernel,
        "join",
        [shaped((CORES * HALF, 2 * REPLICAS * TOKENS), BF16)],
        [BLOCK] * 8,
        arrived=tuple(range(1, 8)),
    )(top, left_top, far_top, right_top, bottom, left_bottom, far_bottom, right_bottom)
    (query_columns,) = call(
        pack_kernel,
        "pack_query",
        [shaped((REPLICAS * TOKENS, EARLY))],
        [BLOCK] * RING,
        arrived=(1, 2, 3),
    )(*query_columns)
    got, rows, query_columns = lax.optimization_barrier((got, rows, query_columns))

    grad_key, grad_value, sent = call(
        key_value_grad_kernel,
        "key_value_grad",
        [flat, flat, shaped((REPLICAS, TOKENS, LANES))],
        [BLOCK] * 4,
        [state, wide, wide],
        arrived=(0, 1, 2, 3),
    )(got, key, value, late)
    own_columns = exchange(sent, "dp")
    slots = call(
        lambda *refs: query_product_kernel(normalizer, *refs[:4], *refs[5:]),
        "query_product",
        [shaped((RING, PADDED_ROWS, EARLY))] * RING,
        [
            IN_SMEM,
            pl.BlockSpec((HALF, 2 * REPLICAS * TOKENS), lambda half: (half, 0)),
            BLOCK,
            BLOCK,
            ANYWHERE,
        ],
        [
            pltpu.VMEM((2 * REPLICAS * TOKENS, EARLY), BF16),
            pltpu.VMEM((PLANE_SIZE // CORES, PADDED_ROWS, EARLY), F32),
        ],
        vmem=24,
        arrived=(3,),
        steps=CORES,
        out_specs=[pl.BlockSpec((2, PADDED_ROWS, EARLY), lambda half: (half, 0, 0))] * RING,
    )(across, rows, query_columns, swap_cores(query_columns), sent)
    far_slot = shift(slots[2], 2, "x")
    slots = [slots[0], far_slot, shift(slots[1], 1, "x"), shift(slots[3], 3, "x")]
    own_columns, slots = lax.optimization_barrier((own_columns, slots))
    slots = call(
        second_stage_kernel,
        "second_stage",
        [shaped((PADDED_ROWS, EARLY))] * RING,
        [IN_SMEM] + [BLOCK] * RING,
        arrived=(2, 3, 4),
    )(along, *slots)
    (product,) = call(
        lambda *refs: key_value_product_kernel(normalizer, *refs[:4], *refs[5:]),
        "key_value_product",
        [shaped((PLANE_SIZE, PADDED_ROWS, LANES))],
        [
            IN_SMEM,
            pl.BlockSpec((HALF, 2 * REPLICAS * TOKENS), lambda half: (half, 0)),
            BLOCK,
            BLOCK,
            ANYWHERE,
        ],
        [pltpu.VMEM((2 * REPLICAS * TOKENS, LANES), BF16)],
        vmem=24,
        arrived=(2, 3),
        steps=CORES,
        out_specs=[
            pl.BlockSpec((PLANE_SIZE // CORES, PADDED_ROWS, LANES), lambda half: (half, 0, 0))
        ],
    )(place, rows, own_columns, swap_cores(own_columns), slots[0])
    key_value_out = exchange(product, PLANE)
    slots = shifted(slots, ("zh", "zl"))
    block = shaped((ROWS, COLS))
    query_out, key_out, value_out = call(
        last_kernel, "last", [block] * 3, [BLOCK] * 5, arrived=(0, 2, 3, 4)
    )(key_value_out, *slots)

    summed = back_project(grad_query, query_weight) + back_project(grad_key, key_weight)
    summed = summed + back_project(grad_value, value_weight)
    latent_grad = summed.astype(BF16).reshape(latent.shape)
    return latent_grad, query_out, key_out, value_out


def solution(mesh):
    devices = mesh.devices
    fine = Mesh(
        devices.reshape(REPLICAS, 2, CORES, 4, 2), ("dp", "zh", "core", "x", "zl")
    )
    grid = P("dp", ("zh", "core"), ("x", "zl"), None)
    weight_out = P(("zh", "core", "x", "zl"), "dp")
    return jax.shard_map(
        body,
        mesh=fine,
        in_specs=(grid, P(), P(), P(), grid),
        out_specs=(grid, weight_out, weight_out, weight_out),
        check_vma=False,
    )
```

```python
import math

import jax
import jax.numpy as jnp
from jax import lax
from jax.experimental import pallas as pl
from jax.experimental.pallas import tpu as pltpu
from jax.sharding import Mesh, PartitionSpec as P

D = 2240
HD = 112
HEADS = 10
HW = HEADS * HD
TILES = 32
PART = HW // TILES
PLANE_SIZE = 16
CORES = 2
ROWS = D // TILES
PADDED_ROWS = 72
HALF = D // 4
REPLICAS = 4
RING = 4
COLS = HW // REPLICAS
EARLY = 256
LATE = COLS - EARLY
WIDE = 2 * COLS + LATE
LANES = 640
TOKENS = 128

EPSILON = 1e-15
IMAGE = ("zh", "core", "x", "zl")
PLANE = ("zh", "x", "zl")
CHUNKS = [(0, 1152), (1152, D - 1152)]
WHOLE = [(0, D)]

F32 = jnp.float32
BF16 = jnp.bfloat16
BLOCK = pl.BlockSpec()
IN_SMEM = pl.BlockSpec(memory_space=pltpu.SMEM)
ANYWHERE = pl.BlockSpec(memory_space=pl.ANY)
IN_HBM = pl.BlockSpec(memory_space=pltpu.HBM)


def shaped(shape, dtype=F32):
    return pltpu.HBM(shape, dtype)


def call(kernel, name, outs, in_specs, scratch=(), vmem=12, arrived=(), steps=1, out_specs=None):
    run = pl.pallas_call(
        kernel,
        name=name,
        grid=(steps,),
        out_shape=outs,
        in_specs=in_specs,
        out_specs=out_specs or [BLOCK] * len(outs),
        scratch_shapes=list(scratch),
        compiler_params=pltpu.CompilerParams(vmem_limit_bytes=vmem * 1024 * 1024),
    )

    def with_placed(*operands):
        placed = [
            operand
            if spec is IN_SMEM or index in arrived
            else pltpu.with_memory_space_constraint(operand, pltpu.HBM)
            for index, (operand, spec) in enumerate(zip(operands, in_specs))
        ]
        return run(*placed)

    return with_placed


def dot(left, right, left_dim, right_dim):
    return lax.dot_general(
        left, right, (((left_dim,), (right_dim,)), ((), ())), preferred_element_type=F32
    )


def split_dot(left, right, left_dim, right_dim):
    high = right.astype(BF16)
    low = (right - high.astype(F32)).astype(BF16)
    return dot(left, high, left_dim, right_dim) + dot(left, low, left_dim, right_dim)


def relu(values):
    return jnp.maximum(values, jnp.zeros_like(values))


def weight_copies(weight, buffer, semaphores, first, chunks):
    copies = []
    for index, (start, size) in enumerate(chunks):
        copies.append(
            pltpu.make_async_copy(
                weight.at[pl.ds(start, size)],
                buffer.at[pl.ds(start, size)],
                semaphores.at[first + index],
            )
        )
    return copies


def project(tokens, buffer, copies, chunks):
    total = None
    for (start, size), copy in zip(chunks, copies):
        copy.wait()
        term = dot(tokens[:, start : start + size], buffer[start : start + size, :], 1, 0)
        total = term if total is None else total + term
    return total.astype(BF16)


def store_parts(sent, at, state):
    for tile in range(TILES):
        sent[tile, at : at + PART, :] = state[tile * PART : (tile + 1) * PART, :]


def load_parts(state, got):
    for tile in range(TILES):
        state[tile * PART : (tile + 1) * PART, :] = got[tile, :PART, :]


def head(ref, index):
    return ref[index * HD : (index + 1) * HD, :]


def key_value_kernel(
    tokens, key_weight, value_weight, key, value, sent, key_buffer, value_buffer, state, total, semaphores
):
    value_copies = weight_copies(value_weight, value_buffer, semaphores, 0, CHUNKS)
    key_copies = weight_copies(key_weight, key_buffer, semaphores, len(CHUNKS), WHOLE)
    for copy in value_copies + key_copies:
        copy.start()
    rows = tokens[...]
    value_rows = project(rows, value_buffer, value_copies, CHUNKS)
    key_rows = project(rows, key_buffer, key_copies, WHOLE)
    for index in range(HEADS):
        part = slice(index * HD, (index + 1) * HD)
        key_head = key_rows[:, part]
        value_head = value_rows[:, part]
        key[index] = key_head
        value[index] = value_head
        positive = relu(key_head)
        state[index * HD : (index + 1) * HD, :] = dot(positive, value_head, 0, 0)
        total[index : index + 1, :] = jnp.sum(positive.astype(F32), axis=0, keepdims=True)
    store_parts(sent, 0, state)
    totals = total[...]
    for tile in range(TILES):
        sent[tile, PART : PART + HEADS, :] = totals


def query_kernel(tokens, weight, query):
    query_rows = dot(tokens[...], weight[...], 1, 0).astype(BF16)
    for index in range(HEADS):
        query[index] = query_rows[:, index * HD : (index + 1) * HD]


def inverse_denominator(positive, total):
    return 1.0 / (jnp.sum(positive * total, axis=1, keepdims=True) + EPSILON)


def numerator_kernel(loss_scale, got, query_rows, upstream, sent, numer, total, state, query, arrived):
    copy = pltpu.make_async_copy(query_rows, query, arrived)
    copy.start()
    sums = got[0]
    for tile in range(1, TILES):
        sums = sums + got[tile]
    state_part = sums[:PART]
    totals = sums[PART : PART + HEADS]
    total[...] = totals
    copy.wait()
    for index in range(HEADS):
        part = slice(index * HD, (index + 1) * HD)
        positive = relu(query[index])
        inverse = inverse_denominator(positive.astype(F32), totals[index : index + 1])
        cotangent = upstream[:, part].astype(F32) * loss_scale
        numer_low = (cotangent * inverse).astype(BF16)
        numer[index] = numer_low
        state[index * HD : (index + 1) * HD, :] = dot(positive, numer_low, 0, 0)
    for tile in range(TILES):
        sent[tile, :PART, :] = state_part
    store_parts(sent, PART, state)


def total_grad_kernel(loss_scale, got, query, upstream, total, sent, grad_denom, state, totals):
    load_parts(state, got)
    for index in range(HEADS):
        part = slice(index * HD, (index + 1) * HD)
        positive = relu(query[index])
        wide = positive.astype(F32)
        inverse = inverse_denominator(wide, total[index : index + 1, :])
        cotangent = upstream[:, part].astype(F32) * loss_scale
        product = split_dot(positive, head(state, index), 1, 0)
        grad = -(jnp.sum(cotangent * product, axis=1, keepdims=True) * inverse) * inverse
        grad_denom[:, index : index + 1] = grad
        totals[index : index + 1, :] = jnp.sum(wide * grad, axis=0, keepdims=True)
    part_sum = got[0, PART:, :]
    for tile in range(1, TILES):
        part_sum = part_sum + got[tile, PART:, :]
    values = totals[...]
    for tile in range(TILES):
        sent[tile, :PART, :] = part_sum
        sent[tile, PART : PART + HEADS, :] = values


def place_columns(place, blocks, outs, at, first=0, last=COLS):
    for slot, out in enumerate(outs):
        block = blocks[lax.rem(place[0] + slot, REPLICAS)]
        out[:, at : at + last - first] = block[:, first:last]


def split_columns(flat, blocks):
    for block in range(REPLICAS):
        blocks[block] = flat[:, block * COLS : (block + 1) * COLS]


def query_grad_kernel(
    place, got, query, numer, total, grad_denom, grad, own, first, second, third, late, state, flat, blocks
):
    load_parts(state, got)
    for index in range(HEADS):
        part = slice(index * HD, (index + 1) * HD)
        values = split_dot(numer[index], head(state, index), 1, 1)
        values = values + grad_denom[:, index : index + 1] * total[index : index + 1, :]
        values = jnp.where(query[index].astype(F32) > 0, values, 0.0).astype(BF16)
        grad[:, part] = values
        flat[:, part] = values.astype(F32)
    split_columns(flat, blocks)
    place_columns(place, blocks, (own, first, second, third), 0, 0, EARLY)
    for block in range(REPLICAS):
        late[block] = blocks[block][:, EARLY:]


def key_value_grad_kernel(got, key, value, late, grad_key, grad_value, sent, state, flat_key, flat_value):
    load_parts(state, got)
    totals = got[0, PART : PART + HEADS, :]
    for tile in range(1, TILES):
        totals = totals + got[tile, PART : PART + HEADS, :]
    for index in range(HEADS):
        part = slice(index * HD, (index + 1) * HD)
        key_head = key[index]
        positive = relu(key_head)
        state_head = head(state, index)
        values = split_dot(positive, state_head, 1, 0).astype(BF16)
        grad_value[:, part] = values
        flat_value[:, part] = values.astype(F32)
        values = split_dot(value[index], state_head, 1, 1) + totals[index : index + 1]
        values = jnp.where(key_head.astype(F32) > 0, values, 0.0).astype(BF16)
        grad_key[:, part] = values
        flat_key[:, part] = values.astype(F32)
    for block in range(REPLICAS):
        part = slice(block * COLS, (block + 1) * COLS)
        sent[block, :, :COLS] = flat_key[:, part]
        sent[block, :, COLS : 2 * COLS] = flat_value[:, part]
        sent[block, :, 2 * COLS : WIDE] = late[block]
        sent[block, :, WIDE:] = jnp.zeros((TOKENS, LANES - WIDE), F32)


def turn_kernel(core, tokens, mine, other, turned):
    for start in range(0, D, 128):
        size = min(128, D - start)
        turned[start : start + size, :] = tokens[:, start : start + size].astype(F32).T
    for half in range(CORES):
        rows = slice(half * HALF, (half + 1) * HALF)
        for out, which in ((mine, core[0]), (other, 1 - core[0])):
            start = pl.multiple_of((half * CORES + which) * HALF, 16)
            out[rows, :] = turned[pl.ds(start, HALF), :]


def join_kernel(*refs):
    for slot, part in enumerate(refs[:-1]):
        refs[-1][:, slot * TOKENS : (slot + 1) * TOKENS] = part[...].astype(BF16)


def pack_kernel(*refs):
    out = refs[-1]
    for slot, part in enumerate(refs[:-1]):
        out[slot * TOKENS : (slot + 1) * TOKENS, :] = part[...].astype(out.dtype)


def query_product_kernel(normalizer, across, rows, own, other, *refs):
    outs, columns, product = refs[:-2], refs[-2], refs[-1]

    @pl.when(pl.program_id(0) == 0)
    def _():
        columns[: REPLICAS * TOKENS, :] = own[...].astype(BF16)
        columns[REPLICAS * TOKENS :, :] = other[...].astype(BF16)

    values = dot(rows[...], columns[...], 1, 0) * normalizer
    for index in range(PLANE_SIZE // CORES):
        product[index, :ROWS, :] = values[index * ROWS : (index + 1) * ROWS]
    for slot, out in enumerate(outs):
        at = lax.rem(across[0] + slot, RING)
        for block in range(2):
            out[block] = product[at * 2 + block]


def key_value_product_kernel(normalizer, place, rows, own, other, out, columns):
    @pl.when(pl.program_id(0) == 0)
    def _():
        for core, blocks in enumerate((own, other)):
            for slot in range(REPLICAS):
                at = (core * REPLICAS + slot) * TOKENS
                source = lax.rem(place[0] + REPLICAS - slot, REPLICAS)
                columns[at : at + TOKENS, :] = blocks[source].astype(BF16)

    values = dot(rows[...], columns[...], 1, 0) * normalizer
    for index in range(PLANE_SIZE // CORES):
        out[index, :ROWS, :] = values[index * ROWS : (index + 1) * ROWS]


def second_stage_kernel(along, own, first, second, third, *outs):
    for slot, out in enumerate(outs):
        at = lax.rem(along[0] + slot, RING)
        out[...] = (own[at] + first[at]) + (second[at] + third[at])


def last_kernel(key_value, own, first, second, third, query_out, key_out, value_out):
    total = key_value[0]
    for index in range(1, PLANE_SIZE):
        total = total + key_value[index]
    key_out[...] = total[:ROWS, :COLS]
    value_out[...] = total[:ROWS, COLS : 2 * COLS]
    query_out[:, EARLY:] = total[:ROWS, 2 * COLS : WIDE]
    total = (own[...] + first[...]) + (second[...] + third[...])
    query_out[:, :EARLY] = total[:ROWS]


def exchange(blocks, axes):
    return lax.all_to_all(blocks, axes, 0, 0, tiled=True)


def shift(values, by, axis):
    return lax.ppermute(values, axis, [(i, (i + by) % RING) for i in range(RING)])


def shifted(slots, axis):
    return [slots[0]] + [shift(slots[s], s, axis) for s in range(1, RING)]


def swap_cores(values):
    return lax.ppermute(values, "core", [(0, 1), (1, 0)])


def both_cores(blocks):
    return blocks + [swap_cores(block) for block in blocks]


def back_project(gradient, weight):
    return dot(gradient, weight, 1, 1)


def body(latent, query_weight, key_weight, value_weight, upstream_grad):
    image_tokens = TOKENS * TILES
    loss_scale = 4.0 * math.sqrt(image_tokens)
    normalizer = 1.0 / math.sqrt(image_tokens * REPLICAS)
    tokens = latent.reshape(TOKENS, D)
    upstream = upstream_grad.reshape(TOKENS, HW)
    place = lax.axis_index("dp").reshape(1)
    core = lax.axis_index("core").reshape(1)
    across = lax.axis_index("x").reshape(1)
    along = lax.axis_index(("zh", "zl")).reshape(1)
    heads = shaped((HEADS, TOKENS, HD), BF16)
    flat = shaped((TOKENS, HW), BF16)
    state = pltpu.VMEM((HW, HD), F32)
    totals = pltpu.VMEM((HEADS, HD), F32)
    weight = pltpu.VMEM((D, HW), BF16)
    wide = pltpu.VMEM((TOKENS, HW), F32)
    blocks = pltpu.VMEM((REPLICAS, TOKENS, COLS), F32)

    key, value, sent = call(
        key_value_kernel,
        "key_value",
        [heads, heads, shaped((TILES, PART + HEADS, HD))],
        [BLOCK, IN_HBM, IN_HBM],
        [weight, weight, state, totals, pltpu.SemaphoreType.DMA((len(CHUNKS) + 1,))],
        vmem=20,
    )(tokens, key_weight, value_weight)
    sent, later_tokens = lax.optimization_barrier((sent, tokens))
    half = shaped((D // 2, TOKENS))
    top, bottom = call(
        turn_kernel, "turn", [half, half], [IN_SMEM, BLOCK], [pltpu.VMEM((D, TOKENS), F32)]
    )(core, later_tokens)
    bottom = swap_cores(bottom)
    left_top = shift(top, 1, "dp")
    right_bottom = shift(bottom, 3, "dp")
    got = exchange(sent, IMAGE)
    (query,) = call(
        query_kernel,
        "query",
        [pltpu.HBM((HEADS, TOKENS, HD), BF16)],
        [BLOCK, BLOCK],
    )(tokens, query_weight)
    sent, numer, total = call(
        lambda *refs: numerator_kernel(loss_scale, *refs),
        "numerator",
        [shaped((TILES, 2 * PART, HD)), heads, shaped((HEADS, HD))],
        [BLOCK, IN_HBM, BLOCK],
        [state, pltpu.VMEM((HEADS, TOKENS, HD), BF16), pltpu.SemaphoreType.DMA],
        arrived=(0, 2),
    )(got, query, upstream)
    sent, left_top, right_bottom, later_top, later_bottom = lax.optimization_barrier(
        (sent, left_top, right_bottom, top, bottom)
    )
    far_top = shift(left_top, 1, "dp")
    far_bottom = shift(right_bottom, 3, "dp")
    left_bottom = shift(later_bottom, 1, "dp")
    right_top = shift(later_top, 3, "dp")
    got_state = exchange(sent, IMAGE)
    sent, grad_denom = call(
        lambda *refs: total_grad_kernel(loss_scale, *refs[:4], *refs[6:]),
        "total_grad",
        [shaped((TILES, PART + HEADS, HD)), shaped((TOKENS, HEADS))],
        [BLOCK] * 4 + [ANYWHERE] * 2,
        [state, totals],
        arrived=(0, 1, 2, 3, 4, 5),
    )(got_state, query, upstream, total, swap_cores(left_bottom), swap_cores(right_top))
    sent, far_top, far_bottom, left_bottom, right_top = lax.optimization_barrier(
        (sent, far_top, far_bottom, left_bottom, right_top)
    )
    got = exchange(sent, IMAGE)

    block = shaped((TOKENS, EARLY))
    grad_query, *query_columns, late = call(
        query_grad_kernel,
        "query_grad",
        [flat, block, block, block, block, shaped((REPLICAS, TOKENS, LATE))],
        [IN_SMEM] + [BLOCK] * 5,
        [state, wide, blocks],
        arrived=(1,),
    )(place, got_state, query, numer, total, grad_denom)
    query_columns = shifted(query_columns, "dp")
    (rows,) = call(
        join_kernel,
        "join",
        [shaped((CORES * HALF, 2 * REPLICAS * TOKENS), BF16)],
        [BLOCK] * 8,
        arrived=tuple(range(1, 8)),
    )(top, left_top, far_top, right_top, bottom, left_bottom, far_bottom, right_bottom)
    (query_columns,) = call(
        pack_kernel,
        "pack_query",
        [shaped((REPLICAS * TOKENS, EARLY))],
        [BLOCK] * RING,
        arrived=(1, 2, 3),
    )(*query_columns)
    got, rows, query_columns = lax.optimization_barrier((got, rows, query_columns))

    grad_key, grad_value, sent = call(
        key_value_grad_kernel,
        "key_value_grad",
        [flat, flat, shaped((REPLICAS, TOKENS, LANES))],
        [BLOCK] * 4,
        [state, wide, wide],
        arrived=(0, 1, 2, 3),
    )(got, key, value, late)
    own_columns = exchange(sent, "dp")
    slots = call(
        lambda *refs: query_product_kernel(normalizer, *refs[:4], *refs[5:]),
        "query_product",
        [shaped((RING, PADDED_ROWS, EARLY))] * RING,
        [
            IN_SMEM,
            pl.BlockSpec((HALF, 2 * REPLICAS * TOKENS), lambda half: (half, 0)),
            BLOCK,
            BLOCK,
            ANYWHERE,
        ],
        [
            pltpu.VMEM((2 * REPLICAS * TOKENS, EARLY), BF16),
            pltpu.VMEM((PLANE_SIZE // CORES, PADDED_ROWS, EARLY), F32),
        ],
        vmem=24,
        arrived=(3,),
        steps=CORES,
        out_specs=[pl.BlockSpec((2, PADDED_ROWS, EARLY), lambda half: (half, 0, 0))] * RING,
    )(across, rows, query_columns, swap_cores(query_columns), sent)
    far_slot = shift(slots[2], 2, "x")
    slots = [slots[0], far_slot, shift(slots[1], 1, "x"), shift(slots[3], 3, "x")]
    own_columns, slots = lax.optimization_barrier((own_columns, slots))
    slots = call(
        second_stage_kernel,
        "second_stage",
        [shaped((PADDED_ROWS, EARLY))] * RING,
        [IN_SMEM] + [BLOCK] * RING,
        arrived=(2, 3, 4),
    )(along, *slots)
    (product,) = call(
        lambda *refs: key_value_product_kernel(normalizer, *refs[:4], *refs[5:]),
        "key_value_product",
        [shaped((PLANE_SIZE, PADDED_ROWS, LANES))],
        [
            IN_SMEM,
            pl.BlockSpec((HALF, 2 * REPLICAS * TOKENS), lambda half: (half, 0)),
            BLOCK,
            BLOCK,
            ANYWHERE,
        ],
        [pltpu.VMEM((2 * REPLICAS * TOKENS, LANES), BF16)],
        vmem=24,
        arrived=(2, 3),
        steps=CORES,
        out_specs=[
            pl.BlockSpec((PLANE_SIZE // CORES, PADDED_ROWS, LANES), lambda half: (half, 0, 0))
        ],
    )(place, rows, own_columns, swap_cores(own_columns), slots[0])
    key_value_out = exchange(product, PLANE)
    slots = shifted(slots, ("zh", "zl"))
    block = shaped((ROWS, COLS))
    query_out, key_out, value_out = call(
        last_kernel, "last", [block] * 3, [BLOCK] * 5, arrived=(0, 2, 3, 4)
    )(key_value_out, *slots)

    summed = back_project(grad_query, query_weight) + back_project(grad_key, key_weight)
    summed = summed + back_project(grad_value, value_weight)
    latent_grad = summed.astype(BF16).reshape(latent.shape)
    return latent_grad, query_out, key_out, value_out


def solution(mesh):
    devices = mesh.devices
    fine = Mesh(
        devices.reshape(REPLICAS, 2, CORES, 4, 2), ("dp", "zh", "core", "x", "zl")
    )
    grid = P("dp", ("zh", "core"), ("x", "zl"), None)
    weight_out = P(("zh", "core", "x", "zl"), "dp")
    return jax.shard_map(
        body,
        mesh=fine,
        in_specs=(grid, P(), P(), P(), grid),
        out_specs=(grid, weight_out, weight_out, weight_out),
        check_vma=False,
    )
```
